128 devices in a mesh: ep: 4 (over x), tm: 32 (over y, z, core).
Axes of the slice: x: 4, y: 4, z: 4, core: 2. Of those that a mesh axis runs over, the one named last changes fastest.
Arguments:
- predictions: float32 [128, 1048576], P('ep', 'tm'), may hold values from -6 to 6
- leaf_index: int32 [128, 1048576], P('ep', 'tm'), may hold values from 0 to 63
- events: int32 [128, 1048576], P('ep', 'tm'), may hold values 0 or 1
- tie_start: int32 [1048576], P('tm'), may hold values from 0 to 1, as said below
Outputs:
- new_pred: float32 [128, 1048576], P('ep', 'tm')
- leaf_weights: float32 [128, 64], P('ep')
- grad_hess: bfloat16 [2, 128, 32, 32768], P(None, None, 'tm', 'ep')
The draws below stay inside these ranges and needn't reach their ends.
Inputs may be any that keep to these rules, and one draw needn't show every extreme that they name: `tie_start`: every row whose index is a multiple of 128 begins a tie group.
All inputs are finite; a program needn't handle non-finite values. No bound on the sum of `events` on one device may be relied on, other than what follows from the above.
Results may differ from the reference program's by a relative error of at most 0.0023.
Values may be sent and summed in bfloat16 or wider, within the bound.
A program may use at most 128 MiB of HBM per device.

```python
import jax
import jax.numpy as jnp
from jax import lax

ENDPOINTS = 128
LEAVES = 64
ROWS_DEV = 32768
ROWS = 1048576
N_TM = 32


def draw_tie_start(key, part):
    positions = jnp.arange(ROWS_DEV * N_TM, dtype=jnp.int32)
    coins = (jax.random.randint(key, (ROWS_DEV * N_TM,), 0, 16) == 0).astype(jnp.int32)
    return jnp.where(positions % 128 == 0, 1, coins).astype(jnp.int32)


def draw_predictions(key, part):
    rows_all = ROWS_DEV * N_TM
    noise_key = jax.random.fold_in(key, 11)
    spike_key = jax.random.fold_in(key, 23)
    place = jnp.arange(rows_all, dtype=jnp.float32) / jnp.float32(rows_all)
    noise = jax.random.normal(noise_key, (ENDPOINTS, rows_all), jnp.float32)
    level = -3.0 * place * place
    spikes = (jax.random.randint(spike_key, (ENDPOINTS, rows_all), 0, 512) == 0).astype(jnp.float32)
    return jnp.clip(level[None, :] + noise + 5.0 * spikes, -6.0, 6.0).astype(jnp.float32)


def with_ends(result, own_key, least, largest):
    spot = [jax.random.randint(jax.random.fold_in(own_key, axis), (), 0, length) for axis, length in enumerate(result.shape)]
    longest = result.shape.index(max(result.shape))
    next_to = spot[:longest] + [(spot[longest] + 1) % result.shape[longest]] + spot[longest + 1:]
    return result.at[tuple(spot)].set(least).at[tuple(next_to)].set(largest)


def setup_inputs(seed: int = 0) -> dict:
    streams_of = jax.random.split(jax.random.key(seed), 5)
    predictions = draw_predictions(jax.random.fold_in(streams_of[4], 71), 0)
    leaf_index = with_ends(jax.random.randint(streams_of[1], (ENDPOINTS, ROWS), 0, LEAVES), jax.random.fold_in(streams_of[1], 1), 0, LEAVES - 1).astype(jnp.int32)
    events = with_ends((jax.random.randint(streams_of[2], (ENDPOINTS, ROWS), 0, 3) < 1).astype(jnp.int32), jax.random.fold_in(streams_of[2], 1), 0, 1)
    tie_start = draw_tie_start(jax.random.fold_in(streams_of[4], 71), 0)
    return {"predictions": predictions, "leaf_index": leaf_index, "events": events, "tie_start": tie_start}


def reference(predictions, leaf_index, events, tie_start):
    rows_all = tie_start.shape[0]
    positions = jnp.arange(rows_all, dtype=jnp.int32)
    first_row = lax.cummax(jnp.where(tie_start == 1, positions, 0).astype(jnp.int32), axis=0)
    next_start = jnp.concatenate([tie_start[1:], jnp.ones((1,), jnp.int32)])
    last_row = lax.cummin(jnp.where(next_start == 1, positions, rows_all - 1).astype(jnp.int32), axis=0, reverse=True)

    def endpoint(packed):
        pred_row, leaf_row, event_row = packed
        weight = jnp.exp(pred_row)
        suffix = jnp.cumsum(weight[::-1])[::-1]
        risk = suffix[first_row]
        observed = event_row.astype(jnp.float32)
        inv_one = observed / risk
        inv_two = inv_one / risk
        accum_one = jnp.cumsum(inv_one)[last_row]
        accum_two = jnp.cumsum(inv_two)[last_row]
        gradient = weight * accum_one - observed
        hessian = weight * accum_one - weight * weight * accum_two
        gsum = jax.ops.segment_sum(gradient, leaf_row, num_segments=LEAVES)
        hsum = jax.ops.segment_sum(hessian, leaf_row, num_segments=LEAVES)
        leaf_w = -gsum / (hsum + 1.0)
        updated = pred_row + leaf_w[leaf_row]
        return updated, leaf_w, gradient.astype(jnp.bfloat16), hessian.astype(jnp.bfloat16)

    new_pred, leaf_weights, gradients, hessians = lax.map(endpoint, (predictions, leaf_index, events))
    grad_hess = jnp.stack([gradients, hessians]).reshape(2, ENDPOINTS, N_TM, ROWS_DEV)
    return new_pred, leaf_weights, grad_hess
```

```python
import math

import jax
import jax.numpy as jnp
from jax import lax
from jax.experimental import pallas as pl
from jax.experimental.pallas import tpu as pltpu
from jax.sharding import PartitionSpec as P

LEAVES = 64
MESH = pl.DeviceIdType.MESH


def tm_combine(part, mode, cid):
    n = lax.axis_size("tm")
    rows = part.shape[0]

    def kernel(x_ref, out_ref, held, send_sem, recv_sem):
        me = lax.axis_index("tm")
        ep = lax.axis_index("ep")
        barrier = pltpu.get_barrier_semaphore()

        def greet(k, carry):
            p = lax.rem(me + k, n)
            pl.semaphore_signal(barrier, inc=1, device_id=(ep, p), device_id_type=MESH)
            return carry

        lax.fori_loop(1, n, greet, 0)
        pl.semaphore_wait(barrier, n - 1)

        def copy_to(p):
            return pltpu.make_async_remote_copy(
                src_ref=x_ref,
                dst_ref=held.at[me],
                send_sem=send_sem.at[p],
                recv_sem=recv_sem.at[me],
                device_id=(ep, p),
                device_id_type=MESH,
            )

        def copy_from(p):
            return pltpu.make_async_remote_copy(
                src_ref=x_ref,
                dst_ref=held.at[p],
                send_sem=send_sem.at[p],
                recv_sem=recv_sem.at[p],
                device_id=(ep, p),
                device_id_type=MESH,
            )

        def send(k, carry):
            copy_to(lax.rem(me + k, n)).start()
            return carry

        lax.fori_loop(1, n, send, 0)

        def wait(k, carry):
            p = lax.rem(me + k, n)
            copy_to(p).wait_send()
            copy_from(p).wait_recv()
            return carry

        lax.fori_loop(1, n, wait, 0)

        if mode == "all":
            total = x_ref[...]
        else:
            total = jnp.zeros((rows, 128), jnp.float32)

        def add(k, total):
            p = lax.rem(me + k, n)
            if mode == "all":
                keep = True
            elif mode == "later":
                keep = p > me
            else:
                keep = p < me
            return total + jnp.where(keep, held[p], 0.0)

        out_ref[...] = lax.fori_loop(1, n, add, total)

    return pl.pallas_call(
        kernel,
        out_shape=jax.ShapeDtypeStruct((rows, 128), jnp.float32),
        in_specs=[pl.BlockSpec(memory_space=pltpu.VMEM)],
        out_specs=pl.BlockSpec(memory_space=pltpu.VMEM),
        scratch_shapes=[
            pltpu.VMEM((n, rows, 128), jnp.float32),
            pltpu.SemaphoreType.DMA((n,)),
            pltpu.SemaphoreType.DMA((n,)),
        ],
        compiler_params=pltpu.CompilerParams(collective_id=cid, has_side_effects=True),
    )(part)


def ep_exchange(stacked, cid):
    m = lax.axis_size("ep")
    two, groups, length = stacked.shape
    width = length // m

    def kernel(src_ref, out_ref, send_sem, recv_sem, local_sem):
        me = lax.axis_index("ep")
        tm = lax.axis_index("tm")
        barrier = pltpu.get_barrier_semaphore()
        for k in range(1, m):
            p = lax.rem(me + k, m)
            pl.semaphore_signal(barrier, inc=1, device_id=(p, tm), device_id_type=MESH)
        pl.semaphore_wait(barrier, m - 1)

        def copy_to(p):
            return pltpu.make_async_remote_copy(
                src_ref=src_ref.at[:, :, pl.ds(p * width, width)],
                dst_ref=out_ref.at[:, pl.ds(me * groups, groups), :],
                send_sem=send_sem.at[p],
                recv_sem=recv_sem.at[me],
                device_id=(p, tm),
                device_id_type=MESH,
            )

        def copy_from(p):
            return pltpu.make_async_remote_copy(
                src_ref=src_ref.at[:, :, pl.ds(me * width, width)],
                dst_ref=out_ref.at[:, pl.ds(p * groups, groups), :],
                send_sem=send_sem.at[p],
                recv_sem=recv_sem.at[p],
                device_id=(p, tm),
                device_id_type=MESH,
            )

        for k in range(1, m):
            copy_to(lax.rem(me + k, m)).start()
        local = pltpu.make_async_copy(
            src_ref.at[:, :, pl.ds(me * width, width)],
            out_ref.at[:, pl.ds(me * groups, groups), :],
            local_sem.at[0],
        )
        local.start()
        local.wait()
        for k in range(1, m):
            p = lax.rem(me + k, m)
            copy_to(p).wait_send()
            copy_from(p).wait_recv()

    return pl.pallas_call(
        kernel,
        out_shape=jax.ShapeDtypeStruct((two, groups * m, width), stacked.dtype),
        in_specs=[pl.BlockSpec(memory_space=pl.ANY)],
        out_specs=pl.BlockSpec(memory_space=pl.ANY),
        scratch_shapes=[
            pltpu.SemaphoreType.DMA((m,)),
            pltpu.SemaphoreType.DMA((m,)),
            pltpu.SemaphoreType.DMA((1,)),
        ],
        compiler_params=pltpu.CompilerParams(collective_id=cid, has_side_effects=True),
    )(stacked)


def lane_pad(vectors):
    width = vectors.shape[1]
    return jnp.pad(vectors, ((0, 0), (0, 128 - width)))


def tile_matrices(tie_start):
    length = tie_start.shape[0]
    blocks = length // 128
    starts = tie_start.reshape(blocks, 128)
    labels = jnp.arange(128, dtype=jnp.int32)
    first_local = lax.cummax(jnp.where(starts == 1, labels[None, :], 0), axis=1)
    next_start = jnp.concatenate([starts[:, 1:], jnp.ones((blocks, 1), jnp.int32)], axis=1)
    last_local = lax.cummin(jnp.where(next_start == 1, labels[None, :], 127), axis=1, reverse=True)
    backward = (labels[None, :, None] >= first_local[:, None, :]).astype(jnp.float32)
    forward = (labels[None, :, None] <= last_local[:, None, :]).astype(jnp.float32)
    return (backward, forward)


def block_cumsum(values, matrices, from_end):
    groups = values.shape[0]
    length = values.shape[1]
    blocks = length // 128
    shaped = values.reshape(groups, blocks, 128)
    within = jnp.einsum("ebj,bji->ebi", shaped, matrices, precision=lax.Precision.HIGHEST)
    totals = jnp.sum(shaped, axis=2)
    if from_end:
        offsets = jnp.cumsum(totals[:, ::-1], axis=1)[:, ::-1] - totals
    else:
        offsets = jnp.cumsum(totals, axis=1) - totals
    return (within + offsets[:, :, None]).reshape(groups, length)


def leaf_partials(leaf_index, gradient, hessian, leaves):
    length = leaf_index.shape[1]
    width = math.gcd(length, 2048)
    labels = jnp.arange(leaves, dtype=jnp.int32)

    def one_block(step, totals):
        start = step * width
        part_leaf = lax.dynamic_slice_in_dim(leaf_index, start, width, 1)
        part_grad = lax.dynamic_slice_in_dim(gradient, start, width, 1)
        part_hess = lax.dynamic_slice_in_dim(hessian, start, width, 1)
        hits = part_leaf[:, None, :] == labels[None, :, None]
        gsum = jnp.sum(jnp.where(hits, part_grad[:, None, :], 0.0), axis=2)
        hsum = jnp.sum(jnp.where(hits, part_hess[:, None, :], 0.0), axis=2)
        return totals + jnp.stack([gsum, hsum], axis=1)

    empty = jnp.zeros((leaf_index.shape[0], 2, leaves), jnp.float32)
    return lax.fori_loop(0, length // width, one_block, empty)


def leaf_lookup(leaf_index, table):
    length = leaf_index.shape[1]
    width = math.gcd(length, 2048)
    labels = jnp.arange(table.shape[1], dtype=jnp.int32)

    def one_block(step, result):
        start = step * width
        part_leaf = lax.dynamic_slice_in_dim(leaf_index, start, width, 1)
        hits = part_leaf[:, None, :] == labels[None, :, None]
        picked = jnp.sum(jnp.where(hits, table[:, :, None], 0.0), axis=1)
        return lax.dynamic_update_slice_in_dim(result, picked, start, 1)

    empty = jnp.zeros(leaf_index.shape, jnp.float32)
    return lax.fori_loop(0, length // width, one_block, empty)


def on_device(predictions, leaf_index, events, tie_start):
    groups = predictions.shape[0]
    length = predictions.shape[1]
    backward, forward = tile_matrices(tie_start)
    weight = jnp.exp(predictions)
    local_risk = block_cumsum(weight, backward, True)
    block_total = local_risk[:, 0]
    later_total = tm_combine(lane_pad(block_total[None, :]), "later", 0)[0, :groups]
    risk = local_risk + later_total[:, None]
    observed = events.astype(jnp.float32)
    inv_one = observed / risk
    inv_two = inv_one / risk
    local_one = block_cumsum(inv_one, forward, False)
    local_two = block_cumsum(inv_two, forward, False)
    pair = lane_pad(jnp.stack([local_one[:, -1], local_two[:, -1]]))
    earlier = tm_combine(pair, "earlier", 1)
    accum_one = local_one + earlier[0, :groups][:, None]
    accum_two = local_two + earlier[1, :groups][:, None]
    gradient = weight * accum_one - observed
    hessian = weight * accum_one - weight * weight * accum_two
    stacked = jnp.stack([gradient, hessian]).astype(jnp.bfloat16)
    grad_hess = ep_exchange(stacked, 2)
    grad_hess = grad_hess.reshape(2, grad_hess.shape[1], 1, grad_hess.shape[2])
    partial_value = leaf_partials(leaf_index, gradient, hessian, LEAVES)
    totals = tm_combine(partial_value.reshape(groups, 2 * LEAVES), "all", 3)
    totals = totals.reshape(groups, 2, LEAVES)
    leaf_weights = -totals[:, 0] / (totals[:, 1] + 1.0)
    new_pred = predictions + leaf_lookup(leaf_index, leaf_weights)
    return (new_pred, leaf_weights, grad_hess)


def solution(mesh):
    placed = (P("ep", "tm"), P("ep", "tm"), P("ep", "tm"), P("tm"))
    return jax.shard_map(
        on_device,
        mesh=mesh,
        in_specs=placed,
        out_specs=(P("ep", "tm"), P("ep", None), P(None, None, "tm", "ep")),
        check_vma=False,
    )
```

```python
import jax
import jax.numpy as jnp
from jax import lax
from jax.experimental import pallas as pl
from jax.experimental.pallas import tpu as pltpu
from jax.sharding import PartitionSpec as P

LEAVES = 64
MESH = pl.DeviceIdType.MESH


def tm_combine(part, mode, cid):
    n = lax.axis_size("tm")
    rows = part.shape[0]

    def kernel(x_ref, out_ref, held, send_sem, recv_sem):
        me = lax.axis_index("tm")
        ep = lax.axis_index("ep")
        barrier = pltpu.get_barrier_semaphore()

        def greet(k, carry):
            p = lax.rem(me + k, n)
            pl.semaphore_signal(barrier, inc=1, device_id=(ep, p), device_id_type=MESH)
            return carry

        lax.fori_loop(1, n, greet, 0)
        pl.semaphore_wait(barrier, n - 1)

        def copy_to(p):
            return pltpu.make_async_remote_copy(
                src_ref=x_ref,
                dst_ref=held.at[me],
                send_sem=send_sem.at[p],
                recv_sem=recv_sem.at[me],
                device_id=(ep, p),
                device_id_type=MESH,
            )

        def copy_from(p):
            return pltpu.make_async_remote_copy(
                src_ref=x_ref,
                dst_ref=held.at[p],
                send_sem=send_sem.at[p],
                recv_sem=recv_sem.at[p],
                device_id=(ep, p),
                device_id_type=MESH,
            )

        def send(k, carry):
            copy_to(lax.rem(me + k, n)).start()
            return carry

        lax.fori_loop(1, n, send, 0)

        def wait(k, carry):
            p = lax.rem(me + k, n)
            copy_to(p).wait_send()
            copy_from(p).wait_recv()
            return carry

        lax.fori_loop(1, n, wait, 0)

        if mode == "all":
            total = x_ref[...]
        else:
            total = jnp.zeros((rows, 128), jnp.float32)

        def add(k, total):
            p = lax.rem(me + k, n)
            if mode == "all":
                keep = True
            elif mode == "later":
                keep = p > me
            else:
                keep = p < me
            return total + jnp.where(keep, held[p], 0.0)

        out_ref[...] = lax.fori_loop(1, n, add, total)

    return pl.pallas_call(
        kernel,
        out_shape=jax.ShapeDtypeStruct((rows, 128), jnp.float32),
        in_specs=[pl.BlockSpec(memory_space=pltpu.VMEM)],
        out_specs=pl.BlockSpec(memory_space=pltpu.VMEM),
        scratch_shapes=[
            pltpu.VMEM((n, rows, 128), jnp.float32),
            pltpu.SemaphoreType.DMA((n,)),
            pltpu.SemaphoreType.DMA((n,)),
        ],
        compiler_params=pltpu.CompilerParams(collective_id=cid, has_side_effects=True),
    )(part)


def ep_exchange(stacked, cid):
    m = lax.axis_size("ep")
    two, groups, length = stacked.shape
    width = length // m

    def kernel(src_ref, out_ref, send_sem, recv_sem, local_sem):
        me = lax.axis_index("ep")
        tm = lax.axis_index("tm")
        barrier = pltpu.get_barrier_semaphore()
        for k in range(1, m):
            p = lax.rem(me + k, m)
            pl.semaphore_signal(barrier, inc=1, device_id=(p, tm), device_id_type=MESH)
        pl.semaphore_wait(barrier, m - 1)

        def copy_to(p):
            return pltpu.make_async_remote_copy(
                src_ref=src_ref.at[:, :, pl.ds(p * width, width)],
                dst_ref=out_ref.at[:, pl.ds(me * groups, groups), :],
                send_sem=send_sem.at[p],
                recv_sem=recv_sem.at[me],
                device_id=(p, tm),
                device_id_type=MESH,
            )

        def copy_from(p):
            return pltpu.make_async_remote_copy(
                src_ref=src_ref.at[:, :, pl.ds(me * width, width)],
                dst_ref=out_ref.at[:, pl.ds(p * groups, groups), :],
                send_sem=send_sem.at[p],
                recv_sem=recv_sem.at[p],
                device_id=(p, tm),
                device_id_type=MESH,
            )

        for k in range(1, m):
            copy_to(lax.rem(me + k, m)).start()
        local = pltpu.make_async_copy(
            src_ref.at[:, :, pl.ds(me * width, width)],
            out_ref.at[:, pl.ds(me * groups, groups), :],
            local_sem.at[0],
        )
        local.start()
        local.wait()
        for k in range(1, m):
            p = lax.rem(me + k, m)
            copy_to(p).wait_send()
            copy_from(p).wait_recv()

    return pl.pallas_call(
        kernel,
        out_shape=jax.ShapeDtypeStruct((two, groups * m, width), stacked.dtype),
        in_specs=[pl.BlockSpec(memory_space=pl.ANY)],
        out_specs=pl.BlockSpec(memory_space=pl.ANY),
        scratch_shapes=[
            pltpu.SemaphoreType.DMA((m,)),
            pltpu.SemaphoreType.DMA((m,)),
            pltpu.SemaphoreType.DMA((1,)),
        ],
        compiler_params=pltpu.CompilerParams(collective_id=cid, has_side_effects=True),
    )(stacked)


def lane_pad(vectors):
    width = vectors.shape[1]
    return jnp.pad(vectors, ((0, 0), (0, 128 - width)))


def tile_matrices(tie_start):
    length = tie_start.shape[0]
    blocks = length // 128
    starts = tie_start.reshape(blocks, 128)
    labels = jnp.arange(128, dtype=jnp.int32)
    first_local = lax.cummax(jnp.where(starts == 1, labels[None, :], 0), axis=1)
    next_start = jnp.concatenate([starts[:, 1:], jnp.ones((blocks, 1), jnp.int32)], axis=1)
    last_local = lax.cummin(jnp.where(next_start == 1, labels[None, :], 127), axis=1, reverse=True)
    backward = (labels[None, :, None] >= first_local[:, None, :]).astype(jnp.float32)
    forward = (labels[None, :, None] <= last_local[:, None, :]).astype(jnp.float32)
    return (backward, forward)


def block_cumsum(values, matrices, from_end):
    groups = values.shape[0]
    length = values.shape[1]
    blocks = length // 128
    shaped = values.reshape(groups, blocks, 128)
    within = jnp.einsum("ebj,bji->ebi", shaped, matrices, precision=lax.Precision.HIGHEST)
    totals = jnp.sum(shaped, axis=2)
    if from_end:
        offsets = jnp.cumsum(totals[:, ::-1], axis=1)[:, ::-1] - totals
    else:
        offsets = jnp.cumsum(totals, axis=1) - totals
    return (within + offsets[:, :, None]).reshape(groups, length)


def leaf_partials(leaf_index, gradient, hessian, leaves):
    groups, length = leaf_index.shape
    tiles = groups // 8
    chunk = 512
    side = leaves // 8

    def kernel(leaf_ref, grad_ref, hess_ref, out_ref):
        def one_chunk(step, total):
            cols = pl.ds(pl.multiple_of(step * chunk, chunk), chunk)
            leaf = leaf_ref[:, cols]
            grad = grad_ref[:, cols]
            hess = hess_ref[:, cols]
            high = lax.shift_right_logical(leaf, 3)
            low = jnp.bitwise_and(leaf, 7)
            grad_hi = grad.astype(jnp.bfloat16).astype(jnp.float32)
            hess_hi = hess.astype(jnp.bfloat16).astype(jnp.float32)
            values = (grad_hi, grad - grad_hi, hess_hi, hess - hess_hi)
            ones = jnp.concatenate(
                [jnp.where(high == a, 1.0, 0.0) for a in range(side)], axis=0
            ).astype(jnp.bfloat16)
            pieces = []
            for b in range(side):
                hit = low == b
                for value in values:
                    pieces.append(jnp.where(hit, value, 0.0))
            parts = jnp.concatenate(pieces, axis=0).astype(jnp.bfloat16)
            return total + lax.dot_general(
                ones, parts, (((1,), (1,)), ((), ())), preferred_element_type=jnp.float32
            )

        total = jnp.zeros((side * 8, side * 4 * 8), jnp.float32)
        out_ref[0] = lax.fori_loop(0, length // chunk, one_chunk, total)

    spec = pl.BlockSpec((8, length), lambda t: (t, 0))
    raw = pl.pallas_call(
        kernel,
        grid=(tiles,),
        out_shape=jax.ShapeDtypeStruct((tiles, side * 8, side * 4 * 8), jnp.float32),
        in_specs=[spec, spec, spec],
        out_specs=pl.BlockSpec((1, side * 8, side * 4 * 8), lambda t: (t, 0, 0)),
    )(leaf_index, gradient, hessian)
    raw = raw.reshape(tiles, side, 8, side, 4, 8)
    eye = jnp.eye(8, dtype=jnp.float32)
    picked = jnp.einsum("taebcf,ef->teabc", raw, eye, precision=lax.Precision.HIGHEST)
    picked = picked.reshape(groups, leaves, 4)
    gsum = picked[:, :, 0] + picked[:, :, 1]
    hsum = picked[:, :, 2] + picked[:, :, 3]
    return jnp.stack([gsum, hsum], axis=1)


def leaf_update(predictions, leaf_index, table):
    groups, length = leaf_index.shape
    tiles = groups // 8
    table = lane_pad(table)

    def kernel(table_ref, pred_ref, leaf_ref, out_ref):
        row = table_ref[...]

        def one(step, carry):
            cols = pl.ds(pl.multiple_of(step * 128, 128), 128)
            picked = jnp.take_along_axis(row, leaf_ref[:, cols], axis=1, mode="promise_in_bounds")
            out_ref[:, cols] = pred_ref[:, cols] + picked
            return carry

        lax.fori_loop(0, length // 128, one, 0, unroll=8)

    spec = pl.BlockSpec((8, length), lambda t: (t, 0))
    return pl.pallas_call(
        kernel,
        grid=(tiles,),
        out_shape=jax.ShapeDtypeStruct((groups, length), jnp.float32),
        in_specs=[pl.BlockSpec((8, 128), lambda t: (t, 0)), spec, spec],
        out_specs=spec,
    )(table, predictions, leaf_index)


def on_device(predictions, leaf_index, events, tie_start):
    groups = predictions.shape[0]
    length = predictions.shape[1]
    backward, forward = tile_matrices(tie_start)
    weight = jnp.exp(predictions)
    local_risk = block_cumsum(weight, backward, True)
    block_total = local_risk[:, 0]
    later_total = tm_combine(lane_pad(block_total[None, :]), "later", 0)[0, :groups]
    risk = local_risk + later_total[:, None]
    observed = events.astype(jnp.float32)
    inv_one = observed / risk
    inv_two = inv_one / risk
    local_one = block_cumsum(inv_one, forward, False)
    local_two = block_cumsum(inv_two, forward, False)
    pair = lane_pad(jnp.stack([local_one[:, -1], local_two[:, -1]]))
    earlier = tm_combine(pair, "earlier", 1)
    accum_one = local_one + earlier[0, :groups][:, None]
    accum_two = local_two + earlier[1, :groups][:, None]
    gradient = weight * accum_one - observed
    hessian = weight * accum_one - weight * weight * accum_two
    stacked = jnp.stack([gradient, hessian]).astype(jnp.bfloat16)
    grad_hess = ep_exchange(stacked, 2)
    grad_hess = grad_hess.reshape(2, grad_hess.shape[1], 1, grad_hess.shape[2])
    partial_value = leaf_partials(leaf_index, gradient, hessian, LEAVES)
    totals = tm_combine(partial_value.reshape(groups, 2 * LEAVES), "all", 3)
    totals = totals.reshape(groups, 2, LEAVES)
    leaf_weights = -totals[:, 0] / (totals[:, 1] + 1.0)
    new_pred = leaf_update(predictions, leaf_index, leaf_weights)
    return (new_pred, leaf_weights, grad_hess)


def solution(mesh):
    placed = (P("ep", "tm"), P("ep", "tm"), P("ep", "tm"), P("tm"))
    return jax.shard_map(
        on_device,
        mesh=mesh,
        in_specs=placed,
        out_specs=(P("ep", "tm"), P("ep", None), P(None, None, "tm", "ep")),
        check_vma=False,
    )
```

```python
import math

import jax
import jax.numpy as jnp
from jax import lax
from jax.experimental import pallas as pl
from jax.experimental.pallas import tpu as pltpu
from jax.sharding import PartitionSpec as P

LEAVES = 64
MESH = pl.DeviceIdType.MESH


def tm_combine(part, mode, cid):
    n = lax.axis_size("tm")
    rows = part.shape[0]

    def kernel(x_ref, out_ref, held, send_sem, recv_sem):
        me = lax.axis_index("tm")
        ep = lax.axis_index("ep")
        barrier = pltpu.get_barrier_semaphore()

        def greet(k, carry):
            p = lax.rem(me + k, n)
            pl.semaphore_signal(barrier, inc=1, device_id=(ep, p), device_id_type=MESH)
            return carry

        lax.fori_loop(1, n, greet, 0)
        pl.semaphore_wait(barrier, n - 1)

        def copy_to(p):
            return pltpu.make_async_remote_copy(
                src_ref=x_ref,
                dst_ref=held.at[me],
                send_sem=send_sem.at[p],
                recv_sem=recv_sem.at[me],
                device_id=(ep, p),
                device_id_type=MESH,
            )

        def copy_from(p):
            return pltpu.make_async_remote_copy(
                src_ref=x_ref,
                dst_ref=held.at[p],
                send_sem=send_sem.at[p],
                recv_sem=recv_sem.at[p],
                device_id=(ep, p),
                device_id_type=MESH,
            )

        def send(k, carry):
            copy_to(lax.rem(me + k, n)).start()
            return carry

        lax.fori_loop(1, n, send, 0)

        def wait(k, carry):
            p = lax.rem(me + k, n)
            copy_to(p).wait_send()
            copy_from(p).wait_recv()
            return carry

        lax.fori_loop(1, n, wait, 0)

        if mode == "all":
            total = x_ref[...]
        else:
            total = jnp.zeros((rows, 128), jnp.float32)

        def add(k, total):
            p = lax.rem(me + k, n)
            if mode == "all":
                keep = True
            elif mode == "later":
                keep = p > me
            else:
                keep = p < me
            return total + jnp.where(keep, held[p], 0.0)

        out_ref[...] = lax.fori_loop(1, n, add, total)

    return pl.pallas_call(
        kernel,
        out_shape=jax.ShapeDtypeStruct((rows, 128), jnp.float32),
        in_specs=[pl.BlockSpec(memory_space=pltpu.VMEM)],
        out_specs=pl.BlockSpec(memory_space=pltpu.VMEM),
        scratch_shapes=[
            pltpu.VMEM((n, rows, 128), jnp.float32),
            pltpu.SemaphoreType.DMA((n,)),
            pltpu.SemaphoreType.DMA((n,)),
        ],
        compiler_params=pltpu.CompilerParams(collective_id=cid, has_side_effects=True),
    )(part)


def exchange_and_sum(stacked, leaf_index, gradient, hessian, leaves, cid):
    m = lax.axis_size("ep")
    two, groups, length = stacked.shape
    width = length // m
    tiles = groups // 8
    side = leaves // 8
    chunk = math.gcd(length, 4096)
    cols_all = side * 4 * 8

    def histogram(leaf_ref, grad_ref, hess_ref, sums_ref):
        row_id = lax.broadcasted_iota(jnp.int32, (side * 8, cols_all), 0)
        col_id = lax.broadcasted_iota(jnp.int32, (side * 8, cols_all), 1)
        diagonal = lax.rem(row_id, 8) == lax.rem(col_id, 8)
        fold = (
            lax.broadcasted_iota(jnp.int32, (cols_all, side * 4), 0) // 8
            == lax.broadcasted_iota(jnp.int32, (cols_all, side * 4), 1)
        ).astype(jnp.float32)

        def one_tile(t, carry):
            rows = pl.ds(pl.multiple_of(t * 8, 8), 8)

            def one_chunk(step, total):
                cols = pl.ds(pl.multiple_of(step * chunk, chunk), chunk)
                leaf = leaf_ref[rows, cols]
                grad = grad_ref[rows, cols]
                hess = hess_ref[rows, cols]
                high = lax.shift_right_logical(leaf, 3)
                low = jnp.bitwise_and(leaf, 7)
                grad_hi = grad.astype(jnp.bfloat16).astype(jnp.float32)
                hess_hi = hess.astype(jnp.bfloat16).astype(jnp.float32)
                values = (grad_hi, grad - grad_hi, hess_hi, hess - hess_hi)
                ones = jnp.concatenate(
                    [jnp.where(high == a, 1.0, 0.0) for a in range(side)], axis=0
                ).astype(jnp.bfloat16)
                pieces = []
                for b in range(side):
                    hit = low == b
                    for value in values:
                        pieces.append(jnp.where(hit, value, 0.0))
                parts = jnp.concatenate(pieces, axis=0).astype(jnp.bfloat16)
                return total + lax.dot_general(
                    ones, parts, (((1,), (1,)), ((), ())), preferred_element_type=jnp.float32
                )

            total = jnp.zeros((side * 8, cols_all), jnp.float32)
            total = lax.fori_loop(0, length // chunk, one_chunk, total)
            total = jnp.where(diagonal, total, 0.0)
            sums_ref[t] = jnp.dot(
                total, fold, precision=lax.Precision.HIGHEST, preferred_element_type=jnp.float32
            )
            return carry

        lax.fori_loop(0, tiles, one_tile, 0)

    def kernel(src_ref, leaf_ref, grad_ref, hess_ref, out_ref, sums_ref, send_sem, recv_sem, local_sem):
        me = lax.axis_index("ep")
        tm = lax.axis_index("tm")
        barrier = pltpu.get_barrier_semaphore()
        for k in range(1, m):
            p = lax.rem(me + k, m)
            pl.semaphore_signal(barrier, inc=1, device_id=(p, tm), device_id_type=MESH)
        pl.semaphore_wait(barrier, m - 1)

        def copy_to(p):
            return pltpu.make_async_remote_copy(
                src_ref=src_ref.at[:, :, pl.ds(p * width, width)],
                dst_ref=out_ref.at[:, pl.ds(me * groups, groups), :],
                send_sem=send_sem.at[p],
                recv_sem=recv_sem.at[me],
                device_id=(p, tm),
                device_id_type=MESH,
            )

        def copy_from(p):
            return pltpu.make_async_remote_copy(
                src_ref=src_ref.at[:, :, pl.ds(me * width, width)],
                dst_ref=out_ref.at[:, pl.ds(p * groups, groups), :],
                send_sem=send_sem.at[p],
                recv_sem=recv_sem.at[p],
                device_id=(p, tm),
                device_id_type=MESH,
            )

        for k in range(1, m):
            copy_to(lax.rem(me + k, m)).start()
        local = pltpu.make_async_copy(
            src_ref.at[:, :, pl.ds(me * width, width)],
            out_ref.at[:, pl.ds(me * groups, groups), :],
            local_sem.at[0],
        )
        local.start()
        histogram(leaf_ref, grad_ref, hess_ref, sums_ref)
        local.wait()
        for k in range(1, m):
            p = lax.rem(me + k, m)
            copy_to(p).wait_send()
            copy_from(p).wait_recv()

    vmem = pl.BlockSpec(memory_space=pltpu.VMEM)
    grad_hess, sums = pl.pallas_call(
        kernel,
        out_shape=(
            jax.ShapeDtypeStruct((two, groups * m, width), stacked.dtype),
            jax.ShapeDtypeStruct((tiles, side * 8, side * 4), jnp.float32),
        ),
        in_specs=[pl.BlockSpec(memory_space=pl.ANY), vmem, vmem, vmem],
        out_specs=(pl.BlockSpec(memory_space=pl.ANY), vmem),
        scratch_shapes=[
            pltpu.SemaphoreType.DMA((m,)),
            pltpu.SemaphoreType.DMA((m,)),
            pltpu.SemaphoreType.DMA((1,)),
        ],
        compiler_params=pltpu.CompilerParams(collective_id=cid, has_side_effects=True),
    )(stacked, leaf_index, gradient, hessian)
    sums = sums.reshape(tiles, side, 8, side, 4).transpose(0, 2, 1, 3, 4)
    sums = sums.reshape(groups, leaves, 4)
    gsum = sums[:, :, 0] + sums[:, :, 1]
    hsum = sums[:, :, 2] + sums[:, :, 3]
    return grad_hess, jnp.stack([gsum, hsum], axis=1)


def lane_pad(vectors):
    width = vectors.shape[1]
    return jnp.pad(vectors, ((0, 0), (0, 128 - width)))


def tile_matrices(tie_start):
    length = tie_start.shape[0]
    blocks = length // 128
    starts = tie_start.reshape(blocks, 128)
    labels = jnp.arange(128, dtype=jnp.int32)
    first_local = lax.cummax(jnp.where(starts == 1, labels[None, :], 0), axis=1)
    next_start = jnp.concatenate([starts[:, 1:], jnp.ones((blocks, 1), jnp.int32)], axis=1)
    last_local = lax.cummin(jnp.where(next_start == 1, labels[None, :], 127), axis=1, reverse=True)
    backward = (labels[None, :, None] >= first_local[:, None, :]).astype(jnp.float32)
    forward = (labels[None, :, None] <= last_local[:, None, :]).astype(jnp.float32)
    return (backward, forward)


def block_cumsum(values, matrices, from_end):
    groups = values.shape[0]
    length = values.shape[1]
    blocks = length // 128
    shaped = values.reshape(groups, blocks, 128)
    within = jnp.einsum("ebj,bji->ebi", shaped, matrices, precision=lax.Precision.HIGHEST)
    totals = jnp.sum(shaped, axis=2)
    if from_end:
        offsets = jnp.cumsum(totals[:, ::-1], axis=1)[:, ::-1] - totals
    else:
        offsets = jnp.cumsum(totals, axis=1) - totals
    return (within + offsets[:, :, None]).reshape(groups, length)


def leaf_update(predictions, leaf_index, table):
    groups, length = leaf_index.shape
    tiles = groups // 8
    table = lane_pad(table)

    def kernel(table_ref, pred_ref, leaf_ref, out_ref):
        row = table_ref[...]

        def one(step, carry):
            cols = pl.ds(pl.multiple_of(step * 128, 128), 128)
            picked = jnp.take_along_axis(row, leaf_ref[:, cols], axis=1, mode="promise_in_bounds")
            out_ref[:, cols] = pred_ref[:, cols] + picked
            return carry

        lax.fori_loop(0, length // 128, one, 0, unroll=8)

    spec = pl.BlockSpec((8, length), lambda t: (t, 0))
    return pl.pallas_call(
        kernel,
        grid=(tiles,),
        out_shape=jax.ShapeDtypeStruct((groups, length), jnp.float32),
        in_specs=[pl.BlockSpec((8, 128), lambda t: (t, 0)), spec, spec],
        out_specs=spec,
    )(table, predictions, leaf_index)


def on_device(predictions, leaf_index, events, tie_start):
    groups = predictions.shape[0]
    length = predictions.shape[1]
    backward, forward = tile_matrices(tie_start)
    weight = jnp.exp(predictions)
    local_risk = block_cumsum(weight, backward, True)
    block_total = local_risk[:, 0]
    later_total = tm_combine(lane_pad(block_total[None, :]), "later", 0)[0, :groups]
    risk = local_risk + later_total[:, None]
    observed = events.astype(jnp.float32)
    inv_one = observed / risk
    inv_two = inv_one / risk
    local_one = block_cumsum(inv_one, forward, False)
    local_two = block_cumsum(inv_two, forward, False)
    pair = lane_pad(jnp.stack([local_one[:, -1], local_two[:, -1]]))
    earlier = tm_combine(pair, "earlier", 1)
    accum_one = local_one + earlier[0, :groups][:, None]
    accum_two = local_two + earlier[1, :groups][:, None]
    gradient = weight * accum_one - observed
    hessian = weight * accum_one - weight * weight * accum_two
    stacked = jnp.stack([gradient, hessian]).astype(jnp.bfloat16)
    grad_hess, partial_value = exchange_and_sum(stacked, leaf_index, gradient, hessian, LEAVES, 2)
    grad_hess = grad_hess.reshape(2, grad_hess.shape[1], 1, grad_hess.shape[2])
    totals = tm_combine(partial_value.reshape(groups, 2 * LEAVES), "all", 3)
    totals = totals.reshape(groups, 2, LEAVES)
    leaf_weights = -totals[:, 0] / (totals[:, 1] + 1.0)
    new_pred = leaf_update(predictions, leaf_index, leaf_weights)
    return (new_pred, leaf_weights, grad_hess)


def solution(mesh):
    placed = (P("ep", "tm"), P("ep", "tm"), P("ep", "tm"), P("tm"))
    return jax.shard_map(
        on_device,
        mesh=mesh,
        in_specs=placed,
        out_specs=(P("ep", "tm"), P("ep", None), P(None, None, "tm", "ep")),
        check_vma=False,
    )
```

```python
import math

import jax
import jax.numpy as jnp
from jax import lax
from jax.experimental import pallas as pl
from jax.experimental.pallas import tpu as pltpu
from jax.sharding import PartitionSpec as P

LEAVES = 64
MESH = pl.DeviceIdType.MESH


def tm_combine(part, mode, cid):
    n = lax.axis_size("tm")
    rows = part.shape[0]

    def kernel(x_ref, out_ref, held, send_sem, recv_sem):
        me = lax.axis_index("tm")
        ep = lax.axis_index("ep")
        barrier = pltpu.get_barrier_semaphore()

        def greet(k, carry):
            p = lax.rem(me + k, n)
            pl.semaphore_signal(barrier, inc=1, device_id=(ep, p), device_id_type=MESH)
            return carry

        lax.fori_loop(1, n, greet, 0)
        pl.semaphore_wait(barrier, n - 1)

        def copy_to(p):
            return pltpu.make_async_remote_copy(
                src_ref=x_ref,
                dst_ref=held.at[me],
                send_sem=send_sem.at[p],
                recv_sem=recv_sem.at[me],
                device_id=(ep, p),
                device_id_type=MESH,
            )

        def copy_from(p):
            return pltpu.make_async_remote_copy(
                src_ref=x_ref,
                dst_ref=held.at[p],
                send_sem=send_sem.at[p],
                recv_sem=recv_sem.at[p],
                device_id=(ep, p),
                device_id_type=MESH,
            )

        def send(k, carry):
            copy_to(lax.rem(me + k, n)).start()
            return carry

        lax.fori_loop(1, n, send, 0)

        def wait(k, carry):
            p = lax.rem(me + k, n)
            copy_to(p).wait_send()
            copy_from(p).wait_recv()
            return carry

        lax.fori_loop(1, n, wait, 0)

        if mode == "all":
            total = x_ref[...]
        else:
            total = jnp.zeros((rows, 128), jnp.float32)

        def add(k, total):
            p = lax.rem(me + k, n)
            if mode == "all":
                keep = True
            elif mode == "later":
                keep = p > me
            else:
                keep = p < me
            return total + jnp.where(keep, held[p], 0.0)

        out_ref[...] = lax.fori_loop(1, n, add, total)

    return pl.pallas_call(
        kernel,
        out_shape=jax.ShapeDtypeStruct((rows, 128), jnp.float32),
        in_specs=[pl.BlockSpec(memory_space=pltpu.VMEM)],
        out_specs=pl.BlockSpec(memory_space=pltpu.VMEM),
        scratch_shapes=[
            pltpu.VMEM((n, rows, 128), jnp.float32),
            pltpu.SemaphoreType.DMA((n,)),
            pltpu.SemaphoreType.DMA((n,)),
        ],
        compiler_params=pltpu.CompilerParams(collective_id=cid, has_side_effects=True),
    )(part)


def exchange_and_sum(stacked, leaf_index, gradient, hessian, leaves, cid):
    m = lax.axis_size("ep")
    two, groups, length = stacked.shape
    width = length // m
    tiles = groups // 8
    side = leaves // 8
    chunk = math.gcd(length, 4096)
    cols_all = side * 4 * 8

    def histogram(leaf_ref, grad_ref, hess_ref, sums_ref):
        row_id = lax.broadcasted_iota(jnp.int32, (side * 8, cols_all), 0)
        col_id = lax.broadcasted_iota(jnp.int32, (side * 8, cols_all), 1)
        diagonal = lax.rem(row_id, 8) == lax.rem(col_id, 8)
        fold = (
            lax.broadcasted_iota(jnp.int32, (cols_all, side * 4), 0) // 8
            == lax.broadcasted_iota(jnp.int32, (cols_all, side * 4), 1)
        ).astype(jnp.float32)

        def one_tile(t, carry):
            rows = pl.ds(pl.multiple_of(t * 8, 8), 8)

            def one_chunk(step, total):
                cols = pl.ds(pl.multiple_of(step * chunk, chunk), chunk)
                leaf = leaf_ref[rows, cols]
                grad = grad_ref[rows, cols]
                hess = hess_ref[rows, cols]
                high = lax.shift_right_logical(leaf, 3)
                low = jnp.bitwise_and(leaf, 7)
                grad_hi = grad.astype(jnp.bfloat16).astype(jnp.float32)
                hess_hi = hess.astype(jnp.bfloat16).astype(jnp.float32)
                values = (grad_hi, grad - grad_hi, hess_hi, hess - hess_hi)
                ones = jnp.concatenate(
                    [jnp.where(high == a, 1.0, 0.0) for a in range(side)], axis=0
                ).astype(jnp.bfloat16)
                pieces = []
                for b in range(side):
                    hit = low == b
                    for value in values:
                        pieces.append(jnp.where(hit, value, 0.0))
                parts = jnp.concatenate(pieces, axis=0).astype(jnp.bfloat16)
                return total + lax.dot_general(
                    ones, parts, (((1,), (1,)), ((), ())), preferred_element_type=jnp.float32
                )

            total = jnp.zeros((side * 8, cols_all), jnp.float32)
            total = lax.fori_loop(0, length // chunk, one_chunk, total)
            total = jnp.where(diagonal, total, 0.0)
            sums_ref[t] = jnp.dot(
                total, fold, precision=lax.Precision.HIGHEST, preferred_element_type=jnp.float32
            )
            return carry

        lax.fori_loop(0, tiles, one_tile, 0)

    def kernel(src_ref, leaf_ref, grad_ref, hess_ref, out_ref, sums_ref, send_sem, recv_sem, local_sem):
        me = lax.axis_index("ep")
        tm = lax.axis_index("tm")
        barrier = pltpu.get_barrier_semaphore()
        for k in range(1, m):
            p = lax.rem(me + k, m)
            pl.semaphore_signal(barrier, inc=1, device_id=(p, tm), device_id_type=MESH)
        pl.semaphore_wait(barrier, m - 1)

        def copy_to(p):
            return pltpu.make_async_remote_copy(
                src_ref=src_ref.at[:, :, pl.ds(p * width, width)],
                dst_ref=out_ref.at[:, pl.ds(me * groups, groups), :],
                send_sem=send_sem.at[p],
                recv_sem=recv_sem.at[me],
                device_id=(p, tm),
                device_id_type=MESH,
            )

        def copy_from(p):
            return pltpu.make_async_remote_copy(
                src_ref=src_ref.at[:, :, pl.ds(me * width, width)],
                dst_ref=out_ref.at[:, pl.ds(p * groups, groups), :],
                send_sem=send_sem.at[p],
                recv_sem=recv_sem.at[p],
                device_id=(p, tm),
                device_id_type=MESH,
            )

        for k in range(1, m):
            copy_to(lax.rem(me + k, m)).start()
        local = pltpu.make_async_copy(
            src_ref.at[:, :, pl.ds(me * width, width)],
            out_ref.at[:, pl.ds(me * groups, groups), :],
            local_sem.at[0],
        )
        local.start()
        histogram(leaf_ref, grad_ref, hess_ref, sums_ref)
        local.wait()
        for k in range(1, m):
            p = lax.rem(me + k, m)
            copy_to(p).wait_send()
            copy_from(p).wait_recv()

    vmem = pl.BlockSpec(memory_space=pltpu.VMEM)
    grad_hess, sums = pl.pallas_call(
        kernel,
        out_shape=(
            jax.ShapeDtypeStruct((two, groups * m, width), stacked.dtype),
            jax.ShapeDtypeStruct((tiles, side * 8, side * 4), jnp.float32),
        ),
        in_specs=[pl.BlockSpec(memory_space=pl.ANY), vmem, vmem, vmem],
        out_specs=(pl.BlockSpec(memory_space=pl.ANY), vmem),
        scratch_shapes=[
            pltpu.SemaphoreType.DMA((m,)),
            pltpu.SemaphoreType.DMA((m,)),
            pltpu.SemaphoreType.DMA((1,)),
        ],
        compiler_params=pltpu.CompilerParams(collective_id=cid, has_side_effects=True),
    )(stacked, leaf_index, gradient, hessian)
    sums = sums.reshape(tiles, side, 8, side, 4).transpose(0, 2, 1, 3, 4)
    sums = sums.reshape(groups, leaves, 4)
    gsum = sums[:, :, 0] + sums[:, :, 1]
    hsum = sums[:, :, 2] + sums[:, :, 3]
    return grad_hess, jnp.stack([gsum, hsum], axis=1)


def finish(stacked, leaf_index, gradient, hessian, predictions, leaves, cid):
    m = lax.axis_size("ep")
    n = lax.axis_size("tm")
    two, groups, length = stacked.shape
    width = length // m
    tiles = groups // 8
    side = leaves // 8
    chunk = math.gcd(length, 4096)
    cols_all = side * 4 * 8

    def histogram(leaf_ref, grad_ref, hess_ref, mine):
        row_id = lax.broadcasted_iota(jnp.int32, (side * 8, cols_all), 0)
        col_id = lax.broadcasted_iota(jnp.int32, (side * 8, cols_all), 1)
        diagonal = lax.rem(row_id, 8) == lax.rem(col_id, 8)
        src = lax.broadcasted_iota(jnp.int32, (cols_all, 2 * leaves), 0)
        dst = lax.broadcasted_iota(jnp.int32, (cols_all, 2 * leaves), 1)
        src_b = src // 32
        src_c = lax.rem(src // 8, 4)

        def one_tile(t, carry):
            rows = pl.ds(pl.multiple_of(t * 8, 8), 8)

            def one_chunk(step, total):
                cols = pl.ds(pl.multiple_of(step * chunk, chunk), chunk)
                leaf = leaf_ref[rows, cols]
                grad = grad_ref[rows, cols]
                hess = hess_ref[rows, cols]
                high = lax.shift_right_logical(leaf, 3)
                low = jnp.bitwise_and(leaf, 7)
                grad_hi = grad.astype(jnp.bfloat16).astype(jnp.float32)
                hess_hi = hess.astype(jnp.bfloat16).astype(jnp.float32)
                values = (grad_hi, grad - grad_hi, hess_hi, hess - hess_hi)
                ones = jnp.concatenate(
                    [jnp.where(high == a, 1.0, 0.0) for a in range(side)], axis=0
                ).astype(jnp.bfloat16)
                pieces = []
                for b in range(side):
                    hit = low == b
                    for value in values:
                        pieces.append(jnp.where(hit, value, 0.0))
                parts = jnp.concatenate(pieces, axis=0).astype(jnp.bfloat16)
                return total + lax.dot_general(
                    ones, parts, (((1,), (1,)), ((), ())), preferred_element_type=jnp.float32
                )

            total = jnp.zeros((side * 8, cols_all), jnp.float32)
            total = lax.fori_loop(0, length // chunk, one_chunk, total)
            total = jnp.where(diagonal, total, 0.0)
            out = jnp.zeros((8, 2 * leaves), jnp.float32)
            for a in range(side):
                fold = (dst == (src_c // 2) * leaves + a * side + src_b).astype(jnp.float32)
                out = out + jnp.dot(
                    total[a * 8:(a + 1) * 8, :], fold,
                    precision=lax.Precision.HIGHEST, preferred_element_type=jnp.float32,
                )
            mine[rows, :] = out
            return carry

        lax.fori_loop(0, tiles, one_tile, 0)

    def kernel(src_ref, leaf_ref, grad_ref, hess_ref, pred_ref,
               out_ref, weights_ref, new_ref,
               mine, held, ep_send, ep_recv, tm_send, tm_recv, local_sem):
        me = lax.axis_index("ep")
        tm = lax.axis_index("tm")
        barrier = pltpu.get_barrier_semaphore()
        for k in range(1, m):
            p = lax.rem(me + k, m)
            pl.semaphore_signal(barrier, inc=1, device_id=(p, tm), device_id_type=MESH)

        def greet(k, carry):
            p = lax.rem(tm + k, n)
            pl.semaphore_signal(barrier, inc=1, device_id=(me, p), device_id_type=MESH)
            return carry

        lax.fori_loop(1, n, greet, 0)
        pl.semaphore_wait(barrier, (m - 1) + (n - 1))

        def ep_to(p):
            return pltpu.make_async_remote_copy(
                src_ref=src_ref.at[:, :, pl.ds(p * width, width)],
                dst_ref=out_ref.at[:, pl.ds(me * groups, groups), :],
                send_sem=ep_send.at[p],
                recv_sem=ep_recv.at[me],
                device_id=(p, tm),
                device_id_type=MESH,
            )

        def ep_from(p):
            return pltpu.make_async_remote_copy(
                src_ref=src_ref.at[:, :, pl.ds(me * width, width)],
                dst_ref=out_ref.at[:, pl.ds(p * groups, groups), :],
                send_sem=ep_send.at[p],
                recv_sem=ep_recv.at[p],
                device_id=(p, tm),
                device_id_type=MESH,
            )

        for k in range(1, m):
            ep_to(lax.rem(me + k, m)).start()
        local = pltpu.make_async_copy(
            src_ref.at[:, :, pl.ds(me * width, width)],
            out_ref.at[:, pl.ds(me * groups, groups), :],
            local_sem.at[0],
        )
        local.start()

        histogram(leaf_ref, grad_ref, hess_ref, mine)
        staged = pltpu.make_async_copy(mine, held.at[tm], local_sem.at[1])
        staged.start()
        staged.wait()

        def tm_to(p):
            return pltpu.make_async_remote_copy(
                src_ref=held.at[tm],
                dst_ref=held.at[tm],
                send_sem=tm_send.at[p],
                recv_sem=tm_recv.at[tm],
                device_id=(me, p),
                device_id_type=MESH,
            )

        def tm_from(p):
            return pltpu.make_async_remote_copy(
                src_ref=held.at[tm],
                dst_ref=held.at[p],
                send_sem=tm_send.at[p],
                recv_sem=tm_recv.at[p],
                device_id=(me, p),
                device_id_type=MESH,
            )

        def send(k, carry):
            tm_to(lax.rem(tm + k, n)).start()
            return carry

        lax.fori_loop(1, n, send, 0)

        def wait(k, carry):
            p = lax.rem(tm + k, n)
            tm_to(p).wait_send()
            tm_from(p).wait_recv()
            return carry

        lax.fori_loop(1, n, wait, 0)

        def add(k, total):
            return total + held[lax.rem(tm + k, n)]

        totals = lax.fori_loop(1, n, add, held[tm])
        lane = lax.broadcasted_iota(jnp.int32, (groups, 2 * leaves), 1)
        hsum = pltpu.roll(totals, leaves, 1)
        table = jnp.where(lane < leaves, -totals / (hsum + 1.0), 0.0)
        weights_ref[...] = table[:, :leaves]

        mine[...] = table

        def one_tile(t, carry):
            rows = pl.ds(pl.multiple_of(t * 8, 8), 8)
            row = mine[rows, :]

            def one(step, carry):
                cols = pl.ds(pl.multiple_of(step * 128, 128), 128)
                picked = jnp.take_along_axis(
                    row, leaf_ref[rows, cols], axis=1, mode="promise_in_bounds"
                )
                new_ref[rows, cols] = pred_ref[rows, cols] + picked
                return carry

            lax.fori_loop(0, length // 128, one, 0, unroll=8)
            return carry

        lax.fori_loop(0, tiles, one_tile, 0)

        local.wait()
        for k in range(1, m):
            p = lax.rem(me + k, m)
            ep_to(p).wait_send()
            ep_from(p).wait_recv()

    vmem = pl.BlockSpec(memory_space=pltpu.VMEM)
    grad_hess, leaf_weights, new_pred = pl.pallas_call(
        kernel,
        out_shape=(
            jax.ShapeDtypeStruct((two, groups * m, width), stacked.dtype),
            jax.ShapeDtypeStruct((groups, leaves), jnp.float32),
            jax.ShapeDtypeStruct((groups, length), jnp.float32),
        ),
        in_specs=[pl.BlockSpec(memory_space=pl.ANY), vmem, vmem, vmem, vmem],
        out_specs=(pl.BlockSpec(memory_space=pl.ANY), vmem, vmem),
        scratch_shapes=[
            pltpu.VMEM((groups, 2 * leaves), jnp.float32),
            pltpu.VMEM((n, groups, 2 * leaves), jnp.float32),
            pltpu.SemaphoreType.DMA((m,)),
            pltpu.SemaphoreType.DMA((m,)),
            pltpu.SemaphoreType.DMA((n,)),
            pltpu.SemaphoreType.DMA((n,)),
            pltpu.SemaphoreType.DMA((2,)),
        ],
        compiler_params=pltpu.CompilerParams(
            collective_id=cid, has_side_effects=True, vmem_limit_bytes=60 * 1024 * 1024
        ),
    )(stacked, leaf_index, gradient, hessian, predictions)
    return grad_hess, leaf_weights, new_pred


def lane_pad(vectors):
    width = vectors.shape[1]
    return jnp.pad(vectors, ((0, 0), (0, 128 - width)))


def tile_matrices(tie_start):
    length = tie_start.shape[0]
    blocks = length // 128
    starts = tie_start.reshape(blocks, 128)
    labels = jnp.arange(128, dtype=jnp.int32)
    first_local = lax.cummax(jnp.where(starts == 1, labels[None, :], 0), axis=1)
    next_start = jnp.concatenate([starts[:, 1:], jnp.ones((blocks, 1), jnp.int32)], axis=1)
    last_local = lax.cummin(jnp.where(next_start == 1, labels[None, :], 127), axis=1, reverse=True)
    backward = (labels[None, :, None] >= first_local[:, None, :]).astype(jnp.float32)
    forward = (labels[None, :, None] <= last_local[:, None, :]).astype(jnp.float32)
    return (backward, forward)


def block_cumsum(values, matrices, from_end):
    groups = values.shape[0]
    length = values.shape[1]
    blocks = length // 128
    shaped = values.reshape(groups, blocks, 128)
    within = jnp.einsum("ebj,bji->ebi", shaped, matrices, precision=lax.Precision.HIGHEST)
    totals = jnp.sum(shaped, axis=2)
    if from_end:
        offsets = jnp.cumsum(totals[:, ::-1], axis=1)[:, ::-1] - totals
    else:
        offsets = jnp.cumsum(totals, axis=1) - totals
    return (within + offsets[:, :, None]).reshape(groups, length)


def leaf_update(predictions, leaf_index, table):
    groups, length = leaf_index.shape
    tiles = groups // 8
    table = lane_pad(table)

    def kernel(table_ref, pred_ref, leaf_ref, out_ref):
        row = table_ref[...]

        def one(step, carry):
            cols = pl.ds(pl.multiple_of(step * 128, 128), 128)
            picked = jnp.take_along_axis(row, leaf_ref[:, cols], axis=1, mode="promise_in_bounds")
            out_ref[:, cols] = pred_ref[:, cols] + picked
            return carry

        lax.fori_loop(0, length // 128, one, 0, unroll=8)

    spec = pl.BlockSpec((8, length), lambda t: (t, 0))
    return pl.pallas_call(
        kernel,
        grid=(tiles,),
        out_shape=jax.ShapeDtypeStruct((groups, length), jnp.float32),
        in_specs=[pl.BlockSpec((8, 128), lambda t: (t, 0)), spec, spec],
        out_specs=spec,
    )(table, predictions, leaf_index)


def on_device(predictions, leaf_index, events, tie_start):
    groups = predictions.shape[0]
    length = predictions.shape[1]
    backward, forward = tile_matrices(tie_start)
    weight = jnp.exp(predictions)
    local_risk = block_cumsum(weight, backward, True)
    block_total = local_risk[:, 0]
    later_total = tm_combine(lane_pad(block_total[None, :]), "later", 0)[0, :groups]
    risk = local_risk + later_total[:, None]
    observed = events.astype(jnp.float32)
    inv_one = observed / risk
    inv_two = inv_one / risk
    local_one = block_cumsum(inv_one, forward, False)
    local_two = block_cumsum(inv_two, forward, False)
    pair = lane_pad(jnp.stack([local_one[:, -1], local_two[:, -1]]))
    earlier = tm_combine(pair, "earlier", 1)
    accum_one = local_one + earlier[0, :groups][:, None]
    accum_two = local_two + earlier[1, :groups][:, None]
    gradient = weight * accum_one - observed
    hessian = weight * accum_one - weight * weight * accum_two
    stacked = jnp.stack([gradient, hessian]).astype(jnp.bfloat16)
    grad_hess, leaf_weights, new_pred = finish(
        stacked, leaf_index, gradient, hessian, predictions, LEAVES, 2
    )
    grad_hess = grad_hess.reshape(2, grad_hess.shape[1], 1, grad_hess.shape[2])
    return (new_pred, leaf_weights, grad_hess)


def solution(mesh):
    placed = (P("ep", "tm"), P("ep", "tm"), P("ep", "tm"), P("tm"))
    return jax.shard_map(
        on_device,
        mesh=mesh,
        in_specs=placed,
        out_specs=(P("ep", "tm"), P("ep", None), P(None, None, "tm", "ep")),
        check_vma=False,
    )
```

```python
import math

import jax
import jax.numpy as jnp
from jax import lax
from jax.experimental import pallas as pl
from jax.experimental.pallas import tpu as pltpu
from jax.sharding import PartitionSpec as P

LEAVES = 64
MESH = pl.DeviceIdType.MESH


def tm_combine(part, mode, cid):
    n = lax.axis_size("tm")
    rows = part.shape[0]

    def kernel(x_ref, out_ref, held, send_sem, recv_sem):
        me = lax.axis_index("tm")
        ep = lax.axis_index("ep")
        barrier = pltpu.get_barrier_semaphore()

        def greet(k, carry):
            p = lax.rem(me + k, n)
            pl.semaphore_signal(barrier, inc=1, device_id=(ep, p), device_id_type=MESH)
            return carry

        lax.fori_loop(1, n, greet, 0)
        pl.semaphore_wait(barrier, n - 1)

        def copy_to(p):
            return pltpu.make_async_remote_copy(
                src_ref=x_ref,
                dst_ref=held.at[me],
                send_sem=send_sem.at[p],
                recv_sem=recv_sem.at[me],
                device_id=(ep, p),
                device_id_type=MESH,
            )

        def copy_from(p):
            return pltpu.make_async_remote_copy(
                src_ref=x_ref,
                dst_ref=held.at[p],
                send_sem=send_sem.at[p],
                recv_sem=recv_sem.at[p],
                device_id=(ep, p),
                device_id_type=MESH,
            )

        def send(k, carry):
            copy_to(lax.rem(me + k, n)).start()
            return carry

        lax.fori_loop(1, n, send, 0)

        def wait(k, carry):
            p = lax.rem(me + k, n)
            copy_to(p).wait_send()
            copy_from(p).wait_recv()
            return carry

        lax.fori_loop(1, n, wait, 0)

        if mode == "all":
            total = x_ref[...]
        else:
            total = jnp.zeros((rows, 128), jnp.float32)

        def add(k, total):
            p = lax.rem(me + k, n)
            if mode == "all":
                keep = True
            elif mode == "later":
                keep = p > me
            else:
                keep = p < me
            return total + jnp.where(keep, held[p], 0.0)

        out_ref[...] = lax.fori_loop(1, n, add, total)

    return pl.pallas_call(
        kernel,
        out_shape=jax.ShapeDtypeStruct((rows, 128), jnp.float32),
        in_specs=[pl.BlockSpec(memory_space=pltpu.VMEM)],
        out_specs=pl.BlockSpec(memory_space=pltpu.VMEM),
        scratch_shapes=[
            pltpu.VMEM((n, rows, 128), jnp.float32),
            pltpu.SemaphoreType.DMA((n,)),
            pltpu.SemaphoreType.DMA((n,)),
        ],
        compiler_params=pltpu.CompilerParams(collective_id=cid, has_side_effects=True),
    )(part)


def exchange_and_sum(stacked, leaf_index, gradient, hessian, leaves, cid):
    m = lax.axis_size("ep")
    two, groups, length = stacked.shape
    width = length // m
    tiles = groups // 8
    side = leaves // 8
    chunk = math.gcd(length, 4096)
    cols_all = side * 4 * 8

    def histogram(leaf_ref, grad_ref, hess_ref, sums_ref):
        row_id = lax.broadcasted_iota(jnp.int32, (side * 8, cols_all), 0)
        col_id = lax.broadcasted_iota(jnp.int32, (side * 8, cols_all), 1)
        diagonal = lax.rem(row_id, 8) == lax.rem(col_id, 8)
        fold = (
            lax.broadcasted_iota(jnp.int32, (cols_all, side * 4), 0) // 8
            == lax.broadcasted_iota(jnp.int32, (cols_all, side * 4), 1)
        ).astype(jnp.float32)

        def one_tile(t, carry):
            rows = pl.ds(pl.multiple_of(t * 8, 8), 8)

            def one_chunk(step, total):
                cols = pl.ds(pl.multiple_of(step * chunk, chunk), chunk)
                leaf = leaf_ref[rows, cols]
                grad = grad_ref[rows, cols]
                hess = hess_ref[rows, cols]
                high = lax.shift_right_logical(leaf, 3)
                low = jnp.bitwise_and(leaf, 7)
                grad_hi = grad.astype(jnp.bfloat16).astype(jnp.float32)
                hess_hi = hess.astype(jnp.bfloat16).astype(jnp.float32)
                values = (grad_hi, grad - grad_hi, hess_hi, hess - hess_hi)
                ones = jnp.concatenate(
                    [jnp.where(high == a, 1.0, 0.0) for a in range(side)], axis=0
                ).astype(jnp.bfloat16)
                pieces = []
                for b in range(side):
                    hit = low == b
                    for value in values:
                        pieces.append(jnp.where(hit, value, 0.0))
                parts = jnp.concatenate(pieces, axis=0).astype(jnp.bfloat16)
                return total + lax.dot_general(
                    ones, parts, (((1,), (1,)), ((), ())), preferred_element_type=jnp.float32
                )

            total = jnp.zeros((side * 8, cols_all), jnp.float32)
            total = lax.fori_loop(0, length // chunk, one_chunk, total)
            total = jnp.where(diagonal, total, 0.0)
            sums_ref[t] = jnp.dot(
                total, fold, precision=lax.Precision.HIGHEST, preferred_element_type=jnp.float32
            )
            return carry

        lax.fori_loop(0, tiles, one_tile, 0)

    def kernel(src_ref, leaf_ref, grad_ref, hess_ref, out_ref, sums_ref, send_sem, recv_sem, local_sem):
        me = lax.axis_index("ep")
        tm = lax.axis_index("tm")
        barrier = pltpu.get_barrier_semaphore()
        for k in range(1, m):
            p = lax.rem(me + k, m)
            pl.semaphore_signal(barrier, inc=1, device_id=(p, tm), device_id_type=MESH)
        pl.semaphore_wait(barrier, m - 1)

        def copy_to(p):
            return pltpu.make_async_remote_copy(
                src_ref=src_ref.at[:, :, pl.ds(p * width, width)],
                dst_ref=out_ref.at[:, pl.ds(me * groups, groups), :],
                send_sem=send_sem.at[p],
                recv_sem=recv_sem.at[me],
                device_id=(p, tm),
                device_id_type=MESH,
            )

        def copy_from(p):
            return pltpu.make_async_remote_copy(
                src_ref=src_ref.at[:, :, pl.ds(me * width, width)],
                dst_ref=out_ref.at[:, pl.ds(p * groups, groups), :],
                send_sem=send_sem.at[p],
                recv_sem=recv_sem.at[p],
                device_id=(p, tm),
                device_id_type=MESH,
            )

        for k in range(1, m):
            copy_to(lax.rem(me + k, m)).start()
        local = pltpu.make_async_copy(
            src_ref.at[:, :, pl.ds(me * width, width)],
            out_ref.at[:, pl.ds(me * groups, groups), :],
            local_sem.at[0],
        )
        local.start()
        histogram(leaf_ref, grad_ref, hess_ref, sums_ref)
        local.wait()
        for k in range(1, m):
            p = lax.rem(me + k, m)
            copy_to(p).wait_send()
            copy_from(p).wait_recv()

    vmem = pl.BlockSpec(memory_space=pltpu.VMEM)
    grad_hess, sums = pl.pallas_call(
        kernel,
        out_shape=(
            jax.ShapeDtypeStruct((two, groups * m, width), stacked.dtype),
            jax.ShapeDtypeStruct((tiles, side * 8, side * 4), jnp.float32),
        ),
        in_specs=[pl.BlockSpec(memory_space=pl.ANY), vmem, vmem, vmem],
        out_specs=(pl.BlockSpec(memory_space=pl.ANY), vmem),
        scratch_shapes=[
            pltpu.SemaphoreType.DMA((m,)),
            pltpu.SemaphoreType.DMA((m,)),
            pltpu.SemaphoreType.DMA((1,)),
        ],
        compiler_params=pltpu.CompilerParams(collective_id=cid, has_side_effects=True),
    )(stacked, leaf_index, gradient, hessian)
    sums = sums.reshape(tiles, side, 8, side, 4).transpose(0, 2, 1, 3, 4)
    sums = sums.reshape(groups, leaves, 4)
    gsum = sums[:, :, 0] + sums[:, :, 1]
    hsum = sums[:, :, 2] + sums[:, :, 3]
    return grad_hess, jnp.stack([gsum, hsum], axis=1)


def finish(stacked, leaf_index, gradient, hessian, predictions, leaves, cid):
    m = lax.axis_size("ep")
    n = lax.axis_size("tm")
    two, groups, length = stacked.shape
    width = length // m
    tiles = groups // 8
    side = leaves // 8
    chunk = math.gcd(length, 4096)
    cols_all = side * 4 * 8

    def histogram(leaf_ref, grad_ref, hess_ref, mine):
        row_id = lax.broadcasted_iota(jnp.int32, (side * 8, cols_all), 0)
        col_id = lax.broadcasted_iota(jnp.int32, (side * 8, cols_all), 1)
        diagonal = lax.rem(row_id, 8) == lax.rem(col_id, 8)
        src = lax.broadcasted_iota(jnp.int32, (cols_all, 2 * leaves), 0)
        dst = lax.broadcasted_iota(jnp.int32, (cols_all, 2 * leaves), 1)
        src_b = src // 32
        src_c = lax.rem(src // 8, 4)

        def one_tile(t, carry):
            rows = pl.ds(pl.multiple_of(t * 8, 8), 8)

            def one_chunk(step, total):
                cols = pl.ds(pl.multiple_of(step * chunk, chunk), chunk)
                leaf = leaf_ref[rows, cols]
                grad = grad_ref[rows, cols]
                hess = hess_ref[rows, cols]
                high = lax.shift_right_logical(leaf, 3)
                low = jnp.bitwise_and(leaf, 7)
                grad_hi = grad.astype(jnp.bfloat16).astype(jnp.float32)
                hess_hi = hess.astype(jnp.bfloat16).astype(jnp.float32)
                values = (grad_hi, grad - grad_hi, hess_hi, hess - hess_hi)
                ones = jnp.concatenate(
                    [jnp.where(high == a, 1.0, 0.0) for a in range(side)], axis=0
                ).astype(jnp.bfloat16)
                pieces = []
                for b in range(side):
                    hit = low == b
                    for value in values:
                        pieces.append(jnp.where(hit, value, 0.0))
                parts = jnp.concatenate(pieces, axis=0).astype(jnp.bfloat16)
                return total + lax.dot_general(
                    ones, parts, (((1,), (1,)), ((), ())), preferred_element_type=jnp.float32
                )

            total = jnp.zeros((side * 8, cols_all), jnp.float32)
            total = lax.fori_loop(0, length // chunk, one_chunk, total)
            total = jnp.where(diagonal, total, 0.0)
            out = jnp.zeros((8, 2 * leaves), jnp.float32)
            for a in range(side):
                fold = (dst == (src_c // 2) * leaves + a * side + src_b).astype(jnp.float32)
                out = out + jnp.dot(
                    total[a * 8:(a + 1) * 8, :], fold,
                    precision=lax.Precision.HIGHEST, preferred_element_type=jnp.float32,
                )
            mine[rows, :] = out
            return carry

        lax.fori_loop(0, tiles, one_tile, 0)

    def kernel(src_ref, leaf_ref, grad_ref, hess_ref, pred_ref,
               out_ref, weights_ref, new_ref,
               mine, held, ep_send, ep_recv, tm_send, tm_recv, local_sem):
        me = lax.axis_index("ep")
        tm = lax.axis_index("tm")
        barrier = pltpu.get_barrier_semaphore()
        for k in range(1, m):
            p = lax.rem(me + k, m)
            pl.semaphore_signal(barrier, inc=1, device_id=(p, tm), device_id_type=MESH)

        def greet(k, carry):
            p = lax.rem(tm + k, n)
            pl.semaphore_signal(barrier, inc=1, device_id=(me, p), device_id_type=MESH)
            return carry

        lax.fori_loop(1, n, greet, 0)
        pl.semaphore_wait(barrier, (m - 1) + (n - 1))

        def ep_to(p):
            return pltpu.make_async_remote_copy(
                src_ref=src_ref.at[:, :, pl.ds(p * width, width)],
                dst_ref=out_ref.at[:, pl.ds(me * groups, groups), :],
                send_sem=ep_send.at[p],
                recv_sem=ep_recv.at[me],
                device_id=(p, tm),
                device_id_type=MESH,
            )

        def ep_from(p):
            return pltpu.make_async_remote_copy(
                src_ref=src_ref.at[:, :, pl.ds(me * width, width)],
                dst_ref=out_ref.at[:, pl.ds(p * groups, groups), :],
                send_sem=ep_send.at[p],
                recv_sem=ep_recv.at[p],
                device_id=(p, tm),
                device_id_type=MESH,
            )

        for k in range(1, m):
            ep_to(lax.rem(me + k, m)).start()
        local = pltpu.make_async_copy(
            src_ref.at[:, :, pl.ds(me * width, width)],
            out_ref.at[:, pl.ds(me * groups, groups), :],
            local_sem.at[0],
        )
        local.start()

        histogram(leaf_ref, grad_ref, hess_ref, mine)
        staged = pltpu.make_async_copy(mine, held.at[tm], local_sem.at[1])
        staged.start()
        staged.wait()

        def tm_to(p):
            return pltpu.make_async_remote_copy(
                src_ref=held.at[tm],
                dst_ref=held.at[tm],
                send_sem=tm_send.at[p],
                recv_sem=tm_recv.at[tm],
                device_id=(me, p),
                device_id_type=MESH,
            )

        def tm_from(p):
            return pltpu.make_async_remote_copy(
                src_ref=held.at[tm],
                dst_ref=held.at[p],
                send_sem=tm_send.at[p],
                recv_sem=tm_recv.at[p],
                device_id=(me, p),
                device_id_type=MESH,
            )

        def send(k, carry):
            tm_to(lax.rem(tm + k, n)).start()
            return carry

        lax.fori_loop(1, n, send, 0)

        def wait(k, carry):
            p = lax.rem(tm + k, n)
            tm_to(p).wait_send()
            tm_from(p).wait_recv()
            return carry

        lax.fori_loop(1, n, wait, 0)

        def add(k, total):
            return total + held[lax.rem(tm + k, n)]

        totals = lax.fori_loop(1, n, add, held[tm])
        lane = lax.broadcasted_iota(jnp.int32, (groups, 2 * leaves), 1)
        hsum = pltpu.roll(totals, leaves, 1)
        table = jnp.where(lane < leaves, -totals / (hsum + 1.0), 0.0)
        weights_ref[...] = table[:, :leaves]

        mine[...] = table

        def one_tile(t, carry):
            rows = pl.ds(pl.multiple_of(t * 8, 8), 8)
            row = mine[rows, :]

            def one(step, carry):
                cols = pl.ds(pl.multiple_of(step * 128, 128), 128)
                picked = jnp.take_along_axis(
                    row, leaf_ref[rows, cols], axis=1, mode="promise_in_bounds"
                )
                new_ref[rows, cols] = pred_ref[rows, cols] + picked
                return carry

            lax.fori_loop(0, length // 128, one, 0, unroll=8)
            return carry

        lax.fori_loop(0, tiles, one_tile, 0)

        local.wait()
        for k in range(1, m):
            p = lax.rem(me + k, m)
            ep_to(p).wait_send()
            ep_from(p).wait_recv()

    vmem = pl.BlockSpec(memory_space=pltpu.VMEM)
    grad_hess, leaf_weights, new_pred = pl.pallas_call(
        kernel,
        out_shape=(
            jax.ShapeDtypeStruct((two, groups * m, width), stacked.dtype),
            jax.ShapeDtypeStruct((groups, leaves), jnp.float32),
            jax.ShapeDtypeStruct((groups, length), jnp.float32),
        ),
        in_specs=[pl.BlockSpec(memory_space=pl.ANY), vmem, vmem, vmem, vmem],
        out_specs=(pl.BlockSpec(memory_space=pl.ANY), vmem, vmem),
        scratch_shapes=[
            pltpu.VMEM((groups, 2 * leaves), jnp.float32),
            pltpu.VMEM((n, groups, 2 * leaves), jnp.float32),
            pltpu.SemaphoreType.DMA((m,)),
            pltpu.SemaphoreType.DMA((m,)),
            pltpu.SemaphoreType.DMA((n,)),
            pltpu.SemaphoreType.DMA((n,)),
            pltpu.SemaphoreType.DMA((2,)),
        ],
        compiler_params=pltpu.CompilerParams(
            collective_id=cid, has_side_effects=True, vmem_limit_bytes=60 * 1024 * 1024
        ),
    )(stacked, leaf_index, gradient, hessian, predictions)
    return grad_hess, leaf_weights, new_pred


def lane_pad(vectors):
    width = vectors.shape[1]
    return jnp.pad(vectors, ((0, 0), (0, 128 - width)))


def tile_matrices(tie_start):
    length = tie_start.shape[0]
    blocks = length // 128
    starts = tie_start.reshape(blocks, 128)
    labels = jnp.arange(128, dtype=jnp.int32)
    first_local = lax.cummax(jnp.where(starts == 1, labels[None, :], 0), axis=1)
    next_start = jnp.concatenate([starts[:, 1:], jnp.ones((blocks, 1), jnp.int32)], axis=1)
    last_local = lax.cummin(jnp.where(next_start == 1, labels[None, :], 127), axis=1, reverse=True)
    backward = (labels[None, :, None] >= first_local[:, None, :]).astype(jnp.float32)
    forward = (labels[None, :, None] <= last_local[:, None, :]).astype(jnp.float32)
    return (backward, forward)


def block_cumsum(values, matrices, from_end):
    groups = values.shape[0]
    length = values.shape[1]
    blocks = length // 128
    shaped = values.reshape(groups, blocks, 128)
    within = jnp.einsum("ebj,bji->ebi", shaped, matrices, precision=lax.Precision.HIGH)
    totals = jnp.sum(shaped, axis=2)
    if from_end:
        offsets = jnp.cumsum(totals[:, ::-1], axis=1)[:, ::-1] - totals
    else:
        offsets = jnp.cumsum(totals, axis=1) - totals
    return (within + offsets[:, :, None]).reshape(groups, length)


def leaf_update(predictions, leaf_index, table):
    groups, length = leaf_index.shape
    tiles = groups // 8
    table = lane_pad(table)

    def kernel(table_ref, pred_ref, leaf_ref, out_ref):
        row = table_ref[...]

        def one(step, carry):
            cols = pl.ds(pl.multiple_of(step * 128, 128), 128)
            picked = jnp.take_along_axis(row, leaf_ref[:, cols], axis=1, mode="promise_in_bounds")
            out_ref[:, cols] = pred_ref[:, cols] + picked
            return carry

        lax.fori_loop(0, length // 128, one, 0, unroll=8)

    spec = pl.BlockSpec((8, length), lambda t: (t, 0))
    return pl.pallas_call(
        kernel,
        grid=(tiles,),
        out_shape=jax.ShapeDtypeStruct((groups, length), jnp.float32),
        in_specs=[pl.BlockSpec((8, 128), lambda t: (t, 0)), spec, spec],
        out_specs=spec,
    )(table, predictions, leaf_index)


def on_device(predictions, leaf_index, events, tie_start):
    groups = predictions.shape[0]
    length = predictions.shape[1]
    backward, forward = tile_matrices(tie_start)
    weight = jnp.exp(predictions)
    local_risk = block_cumsum(weight, backward, True)
    block_total = local_risk[:, 0]
    later_total = tm_combine(lane_pad(block_total[None, :]), "later", 0)[0, :groups]
    risk = local_risk + later_total[:, None]
    observed = events.astype(jnp.float32)
    inv_one = observed / risk
    inv_two = inv_one / risk
    local_both = block_cumsum(jnp.concatenate([inv_one, inv_two]), forward, False)
    local_one = local_both[:groups]
    local_two = local_both[groups:]
    pair = lane_pad(jnp.stack([local_one[:, -1], local_two[:, -1]]))
    earlier = tm_combine(pair, "earlier", 1)
    accum_one = local_one + earlier[0, :groups][:, None]
    accum_two = local_two + earlier[1, :groups][:, None]
    gradient = weight * accum_one - observed
    hessian = weight * accum_one - weight * weight * accum_two
    stacked = jnp.stack([gradient, hessian]).astype(jnp.bfloat16)
    grad_hess, leaf_weights, new_pred = finish(
        stacked, leaf_index, gradient, hessian, predictions, LEAVES, 2
    )
    grad_hess = grad_hess.reshape(2, grad_hess.shape[1], 1, grad_hess.shape[2])
    return (new_pred, leaf_weights, grad_hess)


def solution(mesh):
    placed = (P("ep", "tm"), P("ep", "tm"), P("ep", "tm"), P("tm"))
    return jax.shard_map(
        on_device,
        mesh=mesh,
        in_specs=placed,
        out_specs=(P("ep", "tm"), P("ep", None), P(None, None, "tm", "ep")),
        check_vma=False,
    )
```

```python
import math

import jax
import jax.numpy as jnp
from jax import lax
from jax.experimental import pallas as pl
from jax.experimental.pallas import tpu as pltpu
from jax.sharding import PartitionSpec as P

LEAVES = 64
MESH = pl.DeviceIdType.MESH


def tm_combine(part, mode, cid):
    n = lax.axis_size("tm")
    rows = part.shape[0]

    def kernel(x_ref, out_ref, held, send_sem, recv_sem):
        me = lax.axis_index("tm")
        ep = lax.axis_index("ep")
        barrier = pltpu.get_barrier_semaphore()

        def greet(k, carry):
            p = lax.rem(me + k, n)
            pl.semaphore_signal(barrier, inc=1, device_id=(ep, p), device_id_type=MESH)
            return carry

        lax.fori_loop(1, n, greet, 0)
        pl.semaphore_wait(barrier, n - 1)

        def copy_to(p):
            return pltpu.make_async_remote_copy(
                src_ref=x_ref,
                dst_ref=held.at[me],
                send_sem=send_sem.at[p],
                recv_sem=recv_sem.at[me],
                device_id=(ep, p),
                device_id_type=MESH,
            )

        def copy_from(p):
            return pltpu.make_async_remote_copy(
                src_ref=x_ref,
                dst_ref=held.at[p],
                send_sem=send_sem.at[p],
                recv_sem=recv_sem.at[p],
                device_id=(ep, p),
                device_id_type=MESH,
            )

        def send(k, carry):
            copy_to(lax.rem(me + k, n)).start()
            return carry

        lax.fori_loop(1, n, send, 0)

        def wait(k, carry):
            p = lax.rem(me + k, n)
            copy_to(p).wait_send()
            copy_from(p).wait_recv()
            return carry

        lax.fori_loop(1, n, wait, 0)

        if mode == "all":
            total = x_ref[...]
        else:
            total = jnp.zeros((rows, 128), jnp.float32)

        def add(k, total):
            p = lax.rem(me + k, n)
            if mode == "all":
                keep = True
            elif mode == "later":
                keep = p > me
            else:
                keep = p < me
            return total + jnp.where(keep, held[p], 0.0)

        out_ref[...] = lax.fori_loop(1, n, add, total)

    return pl.pallas_call(
        kernel,
        out_shape=jax.ShapeDtypeStruct((rows, 128), jnp.float32),
        in_specs=[pl.BlockSpec(memory_space=pltpu.VMEM)],
        out_specs=pl.BlockSpec(memory_space=pltpu.VMEM),
        scratch_shapes=[
            pltpu.VMEM((n, rows, 128), jnp.float32),
            pltpu.SemaphoreType.DMA((n,)),
            pltpu.SemaphoreType.DMA((n,)),
        ],
        compiler_params=pltpu.CompilerParams(collective_id=cid, has_side_effects=True),
    )(part)


def exchange_and_sum(stacked, leaf_index, gradient, hessian, leaves, cid):
    m = lax.axis_size("ep")
    two, groups, length = stacked.shape
    width = length // m
    tiles = groups // 8
    side = leaves // 8
    chunk = math.gcd(length, 4096)
    cols_all = side * 4 * 8

    def histogram(leaf_ref, grad_ref, hess_ref, sums_ref):
        row_id = lax.broadcasted_iota(jnp.int32, (side * 8, cols_all), 0)
        col_id = lax.broadcasted_iota(jnp.int32, (side * 8, cols_all), 1)
        diagonal = lax.rem(row_id, 8) == lax.rem(col_id, 8)
        fold = (
            lax.broadcasted_iota(jnp.int32, (cols_all, side * 4), 0) // 8
            == lax.broadcasted_iota(jnp.int32, (cols_all, side * 4), 1)
        ).astype(jnp.float32)

        def one_tile(t, carry):
            rows = pl.ds(pl.multiple_of(t * 8, 8), 8)

            def one_chunk(step, total):
                cols = pl.ds(pl.multiple_of(step * chunk, chunk), chunk)
                leaf = leaf_ref[rows, cols]
                grad = grad_ref[rows, cols]
                hess = hess_ref[rows, cols]
                high = lax.shift_right_logical(leaf, 3)
                low = jnp.bitwise_and(leaf, 7)
                grad_hi = grad.astype(jnp.bfloat16).astype(jnp.float32)
                hess_hi = hess.astype(jnp.bfloat16).astype(jnp.float32)
                values = (grad_hi, grad - grad_hi, hess_hi, hess - hess_hi)
                ones = jnp.concatenate(
                    [jnp.where(high == a, 1.0, 0.0) for a in range(side)], axis=0
                ).astype(jnp.bfloat16)
                pieces = []
                for b in range(side):
                    hit = low == b
                    for value in values:
                        pieces.append(jnp.where(hit, value, 0.0))
                parts = jnp.concatenate(pieces, axis=0).astype(jnp.bfloat16)
                return total + lax.dot_general(
                    ones, parts, (((1,), (1,)), ((), ())), preferred_element_type=jnp.float32
                )

            total = jnp.zeros((side * 8, cols_all), jnp.float32)
            total = lax.fori_loop(0, length // chunk, one_chunk, total)
            total = jnp.where(diagonal, total, 0.0)
            sums_ref[t] = jnp.dot(
                total, fold, precision=lax.Precision.HIGHEST, preferred_element_type=jnp.float32
            )
            return carry

        lax.fori_loop(0, tiles, one_tile, 0)

    def kernel(src_ref, leaf_ref, grad_ref, hess_ref, out_ref, sums_ref, send_sem, recv_sem, local_sem):
        me = lax.axis_index("ep")
        tm = lax.axis_index("tm")
        barrier = pltpu.get_barrier_semaphore()
        for k in range(1, m):
            p = lax.rem(me + k, m)
            pl.semaphore_signal(barrier, inc=1, device_id=(p, tm), device_id_type=MESH)
        pl.semaphore_wait(barrier, m - 1)

        def copy_to(p):
            return pltpu.make_async_remote_copy(
                src_ref=src_ref.at[:, :, pl.ds(p * width, width)],
                dst_ref=out_ref.at[:, pl.ds(me * groups, groups), :],
                send_sem=send_sem.at[p],
                recv_sem=recv_sem.at[me],
                device_id=(p, tm),
                device_id_type=MESH,
            )

        def copy_from(p):
            return pltpu.make_async_remote_copy(
                src_ref=src_ref.at[:, :, pl.ds(me * width, width)],
                dst_ref=out_ref.at[:, pl.ds(p * groups, groups), :],
                send_sem=send_sem.at[p],
                recv_sem=recv_sem.at[p],
                device_id=(p, tm),
                device_id_type=MESH,
            )

        for k in range(1, m):
            copy_to(lax.rem(me + k, m)).start()
        local = pltpu.make_async_copy(
            src_ref.at[:, :, pl.ds(me * width, width)],
            out_ref.at[:, pl.ds(me * groups, groups), :],
            local_sem.at[0],
        )
        local.start()
        histogram(leaf_ref, grad_ref, hess_ref, sums_ref)
        local.wait()
        for k in range(1, m):
            p = lax.rem(me + k, m)
            copy_to(p).wait_send()
            copy_from(p).wait_recv()

    vmem = pl.BlockSpec(memory_space=pltpu.VMEM)
    grad_hess, sums = pl.pallas_call(
        kernel,
        out_shape=(
            jax.ShapeDtypeStruct((two, groups * m, width), stacked.dtype),
            jax.ShapeDtypeStruct((tiles, side * 8, side * 4), jnp.float32),
        ),
        in_specs=[pl.BlockSpec(memory_space=pl.ANY), vmem, vmem, vmem],
        out_specs=(pl.BlockSpec(memory_space=pl.ANY), vmem),
        scratch_shapes=[
            pltpu.SemaphoreType.DMA((m,)),
            pltpu.SemaphoreType.DMA((m,)),
            pltpu.SemaphoreType.DMA((1,)),
        ],
        compiler_params=pltpu.CompilerParams(collective_id=cid, has_side_effects=True),
    )(stacked, leaf_index, gradient, hessian)
    sums = sums.reshape(tiles, side, 8, side, 4).transpose(0, 2, 1, 3, 4)
    sums = sums.reshape(groups, leaves, 4)
    gsum = sums[:, :, 0] + sums[:, :, 1]
    hsum = sums[:, :, 2] + sums[:, :, 3]
    return grad_hess, jnp.stack([gsum, hsum], axis=1)


def finish(stacked, leaf_index, gradient, hessian, predictions, leaves, cid):
    m = lax.axis_size("ep")
    n = lax.axis_size("tm")
    two, groups, length = stacked.shape
    width = length // m
    tiles = groups // 8
    side = leaves // 8
    chunk = math.gcd(length, 4096)
    cols_all = side * 4 * 8

    def histogram(leaf_ref, grad_ref, hess_ref, mine):
        row_id = lax.broadcasted_iota(jnp.int32, (side * 8, cols_all), 0)
        col_id = lax.broadcasted_iota(jnp.int32, (side * 8, cols_all), 1)
        diagonal = lax.rem(row_id, 8) == lax.rem(col_id, 8)
        src = lax.broadcasted_iota(jnp.int32, (cols_all, 2 * leaves), 0)
        dst = lax.broadcasted_iota(jnp.int32, (cols_all, 2 * leaves), 1)
        src_b = src // 32
        src_c = lax.rem(src // 8, 4)

        def one_tile(t, carry):
            rows = pl.ds(pl.multiple_of(t * 8, 8), 8)

            def one_chunk(step, total):
                cols = pl.ds(pl.multiple_of(step * chunk, chunk), chunk)
                leaf = leaf_ref[rows, cols]
                grad = grad_ref[rows, cols]
                hess = hess_ref[rows, cols]
                high = lax.shift_right_logical(leaf, 3)
                low = jnp.bitwise_and(leaf, 7)
                grad_hi = grad.astype(jnp.bfloat16).astype(jnp.float32)
                hess_hi = hess.astype(jnp.bfloat16).astype(jnp.float32)
                values = (grad_hi, grad - grad_hi, hess_hi, hess - hess_hi)
                ones = jnp.concatenate(
                    [jnp.where(high == a, 1.0, 0.0) for a in range(side)], axis=0
                ).astype(jnp.bfloat16)
                pieces = []
                for b in range(side):
                    hit = low == b
                    for value in values:
                        pieces.append(jnp.where(hit, value, 0.0))
                parts = jnp.concatenate(pieces, axis=0).astype(jnp.bfloat16)
                return total + lax.dot_general(
                    ones, parts, (((1,), (1,)), ((), ())), preferred_element_type=jnp.float32
                )

            total = jnp.zeros((side * 8, cols_all), jnp.float32)
            total = lax.fori_loop(0, length // chunk, one_chunk, total)
            total = jnp.where(diagonal, total, 0.0)
            out = jnp.zeros((8, 2 * leaves), jnp.float32)
            for a in range(side):
                fold = (dst == (src_c // 2) * leaves + a * side + src_b).astype(jnp.float32)
                out = out + jnp.dot(
                    total[a * 8:(a + 1) * 8, :], fold,
                    precision=lax.Precision.HIGHEST, preferred_element_type=jnp.float32,
                )
            mine[rows, :] = out
            return carry

        lax.fori_loop(0, tiles, one_tile, 0)

    def kernel(src_ref, leaf_ref, grad_ref, hess_ref, pred_ref,
               out_ref, weights_ref, new_ref,
               mine, held, ep_send, ep_recv, tm_send, tm_recv, local_sem):
        me = lax.axis_index("ep")
        tm = lax.axis_index("tm")
        barrier = pltpu.get_barrier_semaphore()
        for k in range(1, m):
            p = lax.rem(me + k, m)
            pl.semaphore_signal(barrier, inc=1, device_id=(p, tm), device_id_type=MESH)

        def greet(k, carry):
            p = lax.rem(tm + k, n)
            pl.semaphore_signal(barrier, inc=1, device_id=(me, p), device_id_type=MESH)
            return carry

        lax.fori_loop(1, n, greet, 0)
        pl.semaphore_wait(barrier, (m - 1) + (n - 1))

        def ep_to(p):
            return pltpu.make_async_remote_copy(
                src_ref=src_ref.at[:, :, pl.ds(p * width, width)],
                dst_ref=out_ref.at[:, pl.ds(me * groups, groups), :],
                send_sem=ep_send.at[p],
                recv_sem=ep_recv.at[me],
                device_id=(p, tm),
                device_id_type=MESH,
            )

        def ep_from(p):
            return pltpu.make_async_remote_copy(
                src_ref=src_ref.at[:, :, pl.ds(me * width, width)],
                dst_ref=out_ref.at[:, pl.ds(p * groups, groups), :],
                send_sem=ep_send.at[p],
                recv_sem=ep_recv.at[p],
                device_id=(p, tm),
                device_id_type=MESH,
            )

        for k in range(1, m):
            ep_to(lax.rem(me + k, m)).start()
        local = pltpu.make_async_copy(
            src_ref.at[:, :, pl.ds(me * width, width)],
            out_ref.at[:, pl.ds(me * groups, groups), :],
            local_sem.at[0],
        )
        local.start()

        histogram(leaf_ref, grad_ref, hess_ref, mine)
        staged = pltpu.make_async_copy(mine, held.at[tm], local_sem.at[1])
        staged.start()
        staged.wait()

        def tm_to(p):
            return pltpu.make_async_remote_copy(
                src_ref=held.at[tm],
                dst_ref=held.at[tm],
                send_sem=tm_send.at[p],
                recv_sem=tm_recv.at[tm],
                device_id=(me, p),
                device_id_type=MESH,
            )

        def tm_from(p):
            return pltpu.make_async_remote_copy(
                src_ref=held.at[tm],
                dst_ref=held.at[p],
                send_sem=tm_send.at[p],
                recv_sem=tm_recv.at[p],
                device_id=(me, p),
                device_id_type=MESH,
            )

        def send(k, carry):
            tm_to(lax.rem(tm + k, n)).start()
            return carry

        lax.fori_loop(1, n, send, 0)

        def wait(k, carry):
            p = lax.rem(tm + k, n)
            tm_to(p).wait_send()
            tm_from(p).wait_recv()
            return carry

        lax.fori_loop(1, n, wait, 0)

        def add(k, total):
            return total + held[lax.rem(tm + k, n)]

        totals = lax.fori_loop(1, n, add, held[tm])
        lane = lax.broadcasted_iota(jnp.int32, (groups, 2 * leaves), 1)
        hsum = pltpu.roll(totals, leaves, 1)
        table = jnp.where(lane < leaves, -totals / (hsum + 1.0), 0.0)
        weights_ref[...] = table[:, :leaves]

        mine[...] = table

        def one_tile(t, carry):
            rows = pl.ds(pl.multiple_of(t * 8, 8), 8)
            row = mine[rows, :]

            def one(step, carry):
                cols = pl.ds(pl.multiple_of(step * 128, 128), 128)
                picked = jnp.take_along_axis(
                    row, leaf_ref[rows, cols], axis=1, mode="promise_in_bounds"
                )
                new_ref[rows, cols] = pred_ref[rows, cols] + picked
                return carry

            lax.fori_loop(0, length // 128, one, 0, unroll=8)
            return carry

        lax.fori_loop(0, tiles, one_tile, 0)

        local.wait()
        for k in range(1, m):
            p = lax.rem(me + k, m)
            ep_to(p).wait_send()
            ep_from(p).wait_recv()

    vmem = pl.BlockSpec(memory_space=pltpu.VMEM)
    grad_hess, leaf_weights, new_pred = pl.pallas_call(
        kernel,
        out_shape=(
            jax.ShapeDtypeStruct((two, groups * m, width), stacked.dtype),
            jax.ShapeDtypeStruct((groups, leaves), jnp.float32),
            jax.ShapeDtypeStruct((groups, length), jnp.float32),
        ),
        in_specs=[pl.BlockSpec(memory_space=pl.ANY), vmem, vmem, vmem, vmem],
        out_specs=(pl.BlockSpec(memory_space=pl.ANY), vmem, vmem),
        scratch_shapes=[
            pltpu.VMEM((groups, 2 * leaves), jnp.float32),
            pltpu.VMEM((n, groups, 2 * leaves), jnp.float32),
            pltpu.SemaphoreType.DMA((m,)),
            pltpu.SemaphoreType.DMA((m,)),
            pltpu.SemaphoreType.DMA((n,)),
            pltpu.SemaphoreType.DMA((n,)),
            pltpu.SemaphoreType.DMA((2,)),
        ],
        compiler_params=pltpu.CompilerParams(
            collective_id=cid, has_side_effects=True, vmem_limit_bytes=60 * 1024 * 1024
        ),
    )(stacked, leaf_index, gradient, hessian, predictions)
    return grad_hess, leaf_weights, new_pred


def tm_exchange(payload, held, send_sem, recv_sem, stage_sem, ep, me, n):
    staged = pltpu.make_async_copy(payload, held.at[me], stage_sem)
    staged.start()
    staged.wait()

    def copy_to(p):
        return pltpu.make_async_remote_copy(
            src_ref=held.at[me],
            dst_ref=held.at[me],
            send_sem=send_sem.at[p],
            recv_sem=recv_sem.at[me],
            device_id=(ep, p),
            device_id_type=MESH,
        )

    def copy_from(p):
        return pltpu.make_async_remote_copy(
            src_ref=held.at[me],
            dst_ref=held.at[p],
            send_sem=send_sem.at[p],
            recv_sem=recv_sem.at[p],
            device_id=(ep, p),
            device_id_type=MESH,
        )

    def send(k, carry):
        copy_to(lax.rem(me + k, n)).start()
        return carry

    lax.fori_loop(1, n, send, 0)

    def wait(k, carry):
        p = lax.rem(me + k, n)
        copy_to(p).wait_send()
        copy_from(p).wait_recv()
        return carry

    lax.fori_loop(1, n, wait, 0)


def scan_lanes(x, from_end):
    lane = lax.broadcasted_iota(jnp.int32, x.shape, 1)
    k = 1
    while k < 128:
        if from_end:
            moved = pltpu.roll(x, 128 - k, 1)
            x = x + jnp.where(lane < 128 - k, moved, 0.0)
        else:
            moved = pltpu.roll(x, k, 1)
            x = x + jnp.where(lane >= k, moved, 0.0)
        k *= 2
    return x


def front(predictions, events, first_rows, last_rows):
    n = lax.axis_size("tm")
    groups, length = predictions.shape
    tiles = groups // 8
    blocks = length // 128

    def kernel(pred_ref, ev_ref, first_ref, last_ref,
               grad_ref, hess_ref, both_ref,
               weight, one, two, pay_a, held_a, pay_b, held_b,
               send_a, recv_a, send_b, recv_b, stage):
        me = lax.axis_index("tm")
        ep = lax.axis_index("ep")
        barrier = pltpu.get_barrier_semaphore()

        def greet(k, carry):
            p = lax.rem(me + k, n)
            pl.semaphore_signal(barrier, inc=1, device_id=(ep, p), device_id_type=MESH)
            return carry

        lax.fori_loop(1, n, greet, 0)
        pl.semaphore_wait(barrier, n - 1)

        def suffix_tile(t, carry):
            rows = pl.ds(pl.multiple_of(t * 8, 8), 8)

            def one_block(j, later):
                b = blocks - 1 - j
                cols = pl.ds(pl.multiple_of(b * 128, 128), 128)
                w = jnp.exp(pred_ref[rows, cols])
                weight[rows, cols] = w
                s = scan_lanes(w, True)
                idx = first_ref[pl.ds(pl.multiple_of(b * 8, 8), 8), :]
                one[rows, cols] = jnp.take_along_axis(s, idx, axis=1, mode="promise_in_bounds") + later
                return later + jnp.broadcast_to(s[:, 0:1], (8, 128))

            total = lax.fori_loop(0, blocks, one_block, jnp.zeros((8, 128), jnp.float32), unroll=4)
            pay_a[rows, :] = total
            return carry

        lax.fori_loop(0, tiles, suffix_tile, 0)
        tm_exchange(pay_a, held_a, send_a, recv_a, stage.at[0], ep, me, n)

        def add_later(k, total):
            p = lax.rem(me + k, n)
            return total + jnp.where(p > me, held_a[p], 0.0)

        pay_a[...] = lax.fori_loop(1, n, add_later, jnp.zeros((groups, 128), jnp.float32))

        def prefix_tile(t, carry):
            rows = pl.ds(pl.multiple_of(t * 8, 8), 8)
            later = pay_a[rows, :]

            def one_block(b, carries):
                c1, c2 = carries
                cols = pl.ds(pl.multiple_of(b * 128, 128), 128)
                risk = one[rows, cols] + later
                observed = ev_ref[rows, cols].astype(jnp.float32)
                inv_one = observed / risk
                inv_two = inv_one / risk
                s1 = scan_lanes(inv_one, False)
                s2 = scan_lanes(inv_two, False)
                idx = last_ref[pl.ds(pl.multiple_of(b * 8, 8), 8), :]
                one[rows, cols] = jnp.take_along_axis(s1, idx, axis=1, mode="promise_in_bounds") + c1
                two[rows, cols] = jnp.take_along_axis(s2, idx, axis=1, mode="promise_in_bounds") + c2
                return (
                    c1 + jnp.broadcast_to(s1[:, 127:128], (8, 128)),
                    c2 + jnp.broadcast_to(s2[:, 127:128], (8, 128)),
                )

            zero = jnp.zeros((8, 128), jnp.float32)
            c1, c2 = lax.fori_loop(0, blocks, one_block, (zero, zero), unroll=4)
            pay_b[rows, :] = c1
            pay_b[pl.ds(pl.multiple_of(groups + t * 8, 8), 8), :] = c2
            return carry

        lax.fori_loop(0, tiles, prefix_tile, 0)
        tm_exchange(pay_b, held_b, send_b, recv_b, stage.at[1], ep, me, n)

        def add_earlier(k, total):
            p = lax.rem(me + k, n)
            return total + jnp.where(p < me, held_b[p], 0.0)

        pay_b[...] = lax.fori_loop(1, n, add_earlier, jnp.zeros((2 * groups, 128), jnp.float32))

        def out_tile(t, carry):
            rows = pl.ds(pl.multiple_of(t * 8, 8), 8)
            e1 = pay_b[rows, :]
            e2 = pay_b[pl.ds(pl.multiple_of(groups + t * 8, 8), 8), :]

            def one_block(b, carry):
                cols = pl.ds(pl.multiple_of(b * 128, 128), 128)
                w = weight[rows, cols]
                a1 = one[rows, cols] + e1
                a2 = two[rows, cols] + e2
                observed = ev_ref[rows, cols].astype(jnp.float32)
                g = w * a1 - observed
                h = w * a1 - w * w * a2
                grad_ref[rows, cols] = g
                hess_ref[rows, cols] = h
                both_ref[0, rows, cols] = g.astype(jnp.bfloat16)
                both_ref[1, rows, cols] = h.astype(jnp.bfloat16)
                return carry

            lax.fori_loop(0, blocks, one_block, 0, unroll=4)
            return carry

        lax.fori_loop(0, tiles, out_tile, 0)

    vmem = pl.BlockSpec(memory_space=pltpu.VMEM)
    return pl.pallas_call(
        kernel,
        out_shape=(
            jax.ShapeDtypeStruct((groups, length), jnp.float32),
            jax.ShapeDtypeStruct((groups, length), jnp.float32),
            jax.ShapeDtypeStruct((2, groups, length), jnp.bfloat16),
        ),
        in_specs=[vmem, vmem, vmem, vmem],
        out_specs=(vmem, vmem, vmem),
        scratch_shapes=[
            pltpu.VMEM((groups, length), jnp.float32),
            pltpu.VMEM((groups, length), jnp.float32),
            pltpu.VMEM((groups, length), jnp.float32),
            pltpu.VMEM((groups, 128), jnp.float32),
            pltpu.VMEM((n, groups, 128), jnp.float32),
            pltpu.VMEM((2 * groups, 128), jnp.float32),
            pltpu.VMEM((n, 2 * groups, 128), jnp.float32),
            pltpu.SemaphoreType.DMA((n,)),
            pltpu.SemaphoreType.DMA((n,)),
            pltpu.SemaphoreType.DMA((n,)),
            pltpu.SemaphoreType.DMA((n,)),
            pltpu.SemaphoreType.DMA((2,)),
        ],
        compiler_params=pltpu.CompilerParams(
            collective_id=0, has_side_effects=True, vmem_limit_bytes=60 * 1024 * 1024
        ),
    )(predictions, events, first_rows, last_rows)


def tie_rows(tie_start):
    length = tie_start.shape[0]
    blocks = length // 128
    starts = tie_start.reshape(blocks, 128)
    labels = jnp.arange(128, dtype=jnp.int32)
    first_local = lax.cummax(jnp.where(starts == 1, labels[None, :], 0), axis=1)
    next_start = jnp.concatenate([starts[:, 1:], jnp.ones((blocks, 1), jnp.int32)], axis=1)
    last_local = lax.cummin(jnp.where(next_start == 1, labels[None, :], 127), axis=1, reverse=True)

    def spread(rows):
        return jnp.broadcast_to(rows[:, None, :], (blocks, 8, 128)).reshape(blocks * 8, 128)

    return spread(first_local), spread(last_local)


def lane_pad(vectors):
    width = vectors.shape[1]
    return jnp.pad(vectors, ((0, 0), (0, 128 - width)))


def tile_matrices(tie_start):
    length = tie_start.shape[0]
    blocks = length // 128
    starts = tie_start.reshape(blocks, 128)
    labels = jnp.arange(128, dtype=jnp.int32)
    first_local = lax.cummax(jnp.where(starts == 1, labels[None, :], 0), axis=1)
    next_start = jnp.concatenate([starts[:, 1:], jnp.ones((blocks, 1), jnp.int32)], axis=1)
    last_local = lax.cummin(jnp.where(next_start == 1, labels[None, :], 127), axis=1, reverse=True)
    backward = (labels[None, :, None] >= first_local[:, None, :]).astype(jnp.float32)
    forward = (labels[None, :, None] <= last_local[:, None, :]).astype(jnp.float32)
    return (backward, forward)


def block_cumsum(values, matrices, from_end):
    groups = values.shape[0]
    length = values.shape[1]
    blocks = length // 128
    shaped = values.reshape(groups, blocks, 128)
    within = jnp.einsum("ebj,bji->ebi", shaped, matrices, precision=lax.Precision.HIGH)
    totals = jnp.sum(shaped, axis=2)
    if from_end:
        offsets = jnp.cumsum(totals[:, ::-1], axis=1)[:, ::-1] - totals
    else:
        offsets = jnp.cumsum(totals, axis=1) - totals
    return (within + offsets[:, :, None]).reshape(groups, length)


def leaf_update(predictions, leaf_index, table):
    groups, length = leaf_index.shape
    tiles = groups // 8
    table = lane_pad(table)

    def kernel(table_ref, pred_ref, leaf_ref, out_ref):
        row = table_ref[...]

        def one(step, carry):
            cols = pl.ds(pl.multiple_of(step * 128, 128), 128)
            picked = jnp.take_along_axis(row, leaf_ref[:, cols], axis=1, mode="promise_in_bounds")
            out_ref[:, cols] = pred_ref[:, cols] + picked
            return carry

        lax.fori_loop(0, length // 128, one, 0, unroll=8)

    spec = pl.BlockSpec((8, length), lambda t: (t, 0))
    return pl.pallas_call(
        kernel,
        grid=(tiles,),
        out_shape=jax.ShapeDtypeStruct((groups, length), jnp.float32),
        in_specs=[pl.BlockSpec((8, 128), lambda t: (t, 0)), spec, spec],
        out_specs=spec,
    )(table, predictions, leaf_index)


def on_device(predictions, leaf_index, events, tie_start):
    first_rows, last_rows = tie_rows(tie_start)
    gradient, hessian, stacked = front(predictions, events, first_rows, last_rows)
    grad_hess, leaf_weights, new_pred = finish(
        stacked, leaf_index, gradient, hessian, predictions, LEAVES, 2
    )
    grad_hess = grad_hess.reshape(2, grad_hess.shape[1], 1, grad_hess.shape[2])
    return (new_pred, leaf_weights, grad_hess)


def solution(mesh):
    placed = (P("ep", "tm"), P("ep", "tm"), P("ep", "tm"), P("tm"))
    return jax.shard_map(
        on_device,
        mesh=mesh,
        in_specs=placed,
        out_specs=(P("ep", "tm"), P("ep", None), P(None, None, "tm", "ep")),
        check_vma=False,
    )
```

```python
import math

import jax
import jax.numpy as jnp
from jax import lax
from jax.experimental import pallas as pl
from jax.experimental.pallas import tpu as pltpu
from jax.sharding import PartitionSpec as P

LEAVES = 64
MESH = pl.DeviceIdType.MESH


def tm_combine(part, mode, cid):
    n = lax.axis_size("tm")
    rows = part.shape[0]

    def kernel(x_ref, out_ref, held, send_sem, recv_sem):
        me = lax.axis_index("tm")
        ep = lax.axis_index("ep")
        barrier = pltpu.get_barrier_semaphore()

        def greet(k, carry):
            p = lax.rem(me + k, n)
            pl.semaphore_signal(barrier, inc=1, device_id=(ep, p), device_id_type=MESH)
            return carry

        lax.fori_loop(1, n, greet, 0)
        pl.semaphore_wait(barrier, n - 1)

        def copy_to(p):
            return pltpu.make_async_remote_copy(
                src_ref=x_ref,
                dst_ref=held.at[me],
                send_sem=send_sem.at[p],
                recv_sem=recv_sem.at[me],
                device_id=(ep, p),
                device_id_type=MESH,
            )

        def copy_from(p):
            return pltpu.make_async_remote_copy(
                src_ref=x_ref,
                dst_ref=held.at[p],
                send_sem=send_sem.at[p],
                recv_sem=recv_sem.at[p],
                device_id=(ep, p),
                device_id_type=MESH,
            )

        def send(k, carry):
            copy_to(lax.rem(me + k, n)).start()
            return carry

        lax.fori_loop(1, n, send, 0)

        def wait(k, carry):
            p = lax.rem(me + k, n)
            copy_to(p).wait_send()
            copy_from(p).wait_recv()
            return carry

        lax.fori_loop(1, n, wait, 0)

        if mode == "all":
            total = x_ref[...]
        else:
            total = jnp.zeros((rows, 128), jnp.float32)

        def add(k, total):
            p = lax.rem(me + k, n)
            if mode == "all":
                keep = True
            elif mode == "later":
                keep = p > me
            else:
                keep = p < me
            return total + jnp.where(keep, held[p], 0.0)

        out_ref[...] = lax.fori_loop(1, n, add, total)

    return pl.pallas_call(
        kernel,
        out_shape=jax.ShapeDtypeStruct((rows, 128), jnp.float32),
        in_specs=[pl.BlockSpec(memory_space=pltpu.VMEM)],
        out_specs=pl.BlockSpec(memory_space=pltpu.VMEM),
        scratch_shapes=[
            pltpu.VMEM((n, rows, 128), jnp.float32),
            pltpu.SemaphoreType.DMA((n,)),
            pltpu.SemaphoreType.DMA((n,)),
        ],
        compiler_params=pltpu.CompilerParams(collective_id=cid, has_side_effects=True),
    )(part)


def exchange_and_sum(stacked, leaf_index, gradient, hessian, leaves, cid):
    m = lax.axis_size("ep")
    two, groups, length = stacked.shape
    width = length // m
    tiles = groups // 8
    side = leaves // 8
    chunk = math.gcd(length, 4096)
    cols_all = side * 4 * 8

    def histogram(leaf_ref, grad_ref, hess_ref, sums_ref):
        row_id = lax.broadcasted_iota(jnp.int32, (side * 8, cols_all), 0)
        col_id = lax.broadcasted_iota(jnp.int32, (side * 8, cols_all), 1)
        diagonal = lax.rem(row_id, 8) == lax.rem(col_id, 8)
        fold = (
            lax.broadcasted_iota(jnp.int32, (cols_all, side * 4), 0) // 8
            == lax.broadcasted_iota(jnp.int32, (cols_all, side * 4), 1)
        ).astype(jnp.float32)

        def one_tile(t, carry):
            rows = pl.ds(pl.multiple_of(t * 8, 8), 8)

            def one_chunk(step, total):
                cols = pl.ds(pl.multiple_of(step * chunk, chunk), chunk)
                leaf = leaf_ref[rows, cols]
                grad = grad_ref[rows, cols]
                hess = hess_ref[rows, cols]
                high = lax.shift_right_logical(leaf, 3)
                low = jnp.bitwise_and(leaf, 7)
                grad_hi = grad.astype(jnp.bfloat16).astype(jnp.float32)
                hess_hi = hess.astype(jnp.bfloat16).astype(jnp.float32)
                values = (grad_hi, grad - grad_hi, hess_hi, hess - hess_hi)
                ones = jnp.concatenate(
                    [jnp.where(high == a, 1.0, 0.0) for a in range(side)], axis=0
                ).astype(jnp.bfloat16)
                pieces = []
                for b in range(side):
                    hit = low == b
                    for value in values:
                        pieces.append(jnp.where(hit, value, 0.0))
                parts = jnp.concatenate(pieces, axis=0).astype(jnp.bfloat16)
                return total + lax.dot_general(
                    ones, parts, (((1,), (1,)), ((), ())), preferred_element_type=jnp.float32
                )

            total = jnp.zeros((side * 8, cols_all), jnp.float32)
            total = lax.fori_loop(0, length // chunk, one_chunk, total)
            total = jnp.where(diagonal, total, 0.0)
            sums_ref[t] = jnp.dot(
                total, fold, precision=lax.Precision.HIGHEST, preferred_element_type=jnp.float32
            )
            return carry

        lax.fori_loop(0, tiles, one_tile, 0)

    def kernel(src_ref, leaf_ref, grad_ref, hess_ref, out_ref, sums_ref, send_sem, recv_sem, local_sem):
        me = lax.axis_index("ep")
        tm = lax.axis_index("tm")
        barrier = pltpu.get_barrier_semaphore()
        for k in range(1, m):
            p = lax.rem(me + k, m)
            pl.semaphore_signal(barrier, inc=1, device_id=(p, tm), device_id_type=MESH)
        pl.semaphore_wait(barrier, m - 1)

        def copy_to(p):
            return pltpu.make_async_remote_copy(
                src_ref=src_ref.at[:, :, pl.ds(p * width, width)],
                dst_ref=out_ref.at[:, pl.ds(me * groups, groups), :],
                send_sem=send_sem.at[p],
                recv_sem=recv_sem.at[me],
                device_id=(p, tm),
                device_id_type=MESH,
            )

        def copy_from(p):
            return pltpu.make_async_remote_copy(
                src_ref=src_ref.at[:, :, pl.ds(me * width, width)],
                dst_ref=out_ref.at[:, pl.ds(p * groups, groups), :],
                send_sem=send_sem.at[p],
                recv_sem=recv_sem.at[p],
                device_id=(p, tm),
                device_id_type=MESH,
            )

        for k in range(1, m):
            copy_to(lax.rem(me + k, m)).start()
        local = pltpu.make_async_copy(
            src_ref.at[:, :, pl.ds(me * width, width)],
            out_ref.at[:, pl.ds(me * groups, groups), :],
            local_sem.at[0],
        )
        local.start()
        histogram(leaf_ref, grad_ref, hess_ref, sums_ref)
        local.wait()
        for k in range(1, m):
            p = lax.rem(me + k, m)
            copy_to(p).wait_send()
            copy_from(p).wait_recv()

    vmem = pl.BlockSpec(memory_space=pltpu.VMEM)
    grad_hess, sums = pl.pallas_call(
        kernel,
        out_shape=(
            jax.ShapeDtypeStruct((two, groups * m, width), stacked.dtype),
            jax.ShapeDtypeStruct((tiles, side * 8, side * 4), jnp.float32),
        ),
        in_specs=[pl.BlockSpec(memory_space=pl.ANY), vmem, vmem, vmem],
        out_specs=(pl.BlockSpec(memory_space=pl.ANY), vmem),
        scratch_shapes=[
            pltpu.SemaphoreType.DMA((m,)),
            pltpu.SemaphoreType.DMA((m,)),
            pltpu.SemaphoreType.DMA((1,)),
        ],
        compiler_params=pltpu.CompilerParams(collective_id=cid, has_side_effects=True),
    )(stacked, leaf_index, gradient, hessian)
    sums = sums.reshape(tiles, side, 8, side, 4).transpose(0, 2, 1, 3, 4)
    sums = sums.reshape(groups, leaves, 4)
    gsum = sums[:, :, 0] + sums[:, :, 1]
    hsum = sums[:, :, 2] + sums[:, :, 3]
    return grad_hess, jnp.stack([gsum, hsum], axis=1)


def finish(stacked, leaf_index, gradient, hessian, predictions, leaves, cid):
    m = lax.axis_size("ep")
    n = lax.axis_size("tm")
    two, groups, length = stacked.shape
    width = length // m
    tiles = groups // 8
    side = leaves // 8
    chunk = math.gcd(length, 4096)
    cols_all = side * 4 * 8

    def histogram(leaf_ref, grad_ref, hess_ref, mine):
        row_id = lax.broadcasted_iota(jnp.int32, (side * 8, cols_all), 0)
        col_id = lax.broadcasted_iota(jnp.int32, (side * 8, cols_all), 1)
        diagonal = lax.rem(row_id, 8) == lax.rem(col_id, 8)
        src = lax.broadcasted_iota(jnp.int32, (cols_all, 2 * leaves), 0)
        dst = lax.broadcasted_iota(jnp.int32, (cols_all, 2 * leaves), 1)
        src_b = src // 32
        src_c = lax.rem(src // 8, 4)

        def one_tile(t, carry):
            rows = pl.ds(pl.multiple_of(t * 8, 8), 8)

            def one_chunk(step, total):
                cols = pl.ds(pl.multiple_of(step * chunk, chunk), chunk)
                leaf = leaf_ref[rows, cols]
                grad = grad_ref[rows, cols]
                hess = hess_ref[rows, cols]
                high = lax.shift_right_logical(leaf, 3)
                low = jnp.bitwise_and(leaf, 7)
                grad_hi = grad.astype(jnp.bfloat16).astype(jnp.float32)
                hess_hi = hess.astype(jnp.bfloat16).astype(jnp.float32)
                values = (grad_hi, grad - grad_hi, hess_hi, hess - hess_hi)
                ones = jnp.concatenate(
                    [jnp.where(high == a, 1.0, 0.0) for a in range(side)], axis=0
                ).astype(jnp.bfloat16)
                pieces = []
                for b in range(side):
                    hit = low == b
                    for value in values:
                        pieces.append(jnp.where(hit, value, 0.0))
                parts = jnp.concatenate(pieces, axis=0).astype(jnp.bfloat16)
                return total + lax.dot_general(
                    ones, parts, (((1,), (1,)), ((), ())), preferred_element_type=jnp.float32
                )

            total = jnp.zeros((side * 8, cols_all), jnp.float32)
            total = lax.fori_loop(0, length // chunk, one_chunk, total)
            total = jnp.where(diagonal, total, 0.0)
            out = jnp.zeros((8, 2 * leaves), jnp.float32)
            for a in range(side):
                fold = (dst == (src_c // 2) * leaves + a * side + src_b).astype(jnp.float32)
                out = out + jnp.dot(
                    total[a * 8:(a + 1) * 8, :], fold,
                    precision=lax.Precision.HIGHEST, preferred_element_type=jnp.float32,
                )
            mine[rows, :] = out
            return carry

        lax.fori_loop(0, tiles, one_tile, 0)

    def kernel(src_ref, leaf_ref, grad_ref, hess_ref, pred_ref,
               out_ref, weights_ref, new_ref,
               mine, held, ep_send, ep_recv, tm_send, tm_recv, local_sem):
        me = lax.axis_index("ep")
        tm = lax.axis_index("tm")
        barrier = pltpu.get_barrier_semaphore()
        for k in range(1, m):
            p = lax.rem(me + k, m)
            pl.semaphore_signal(barrier, inc=1, device_id=(p, tm), device_id_type=MESH)

        def greet(k, carry):
            p = lax.rem(tm + k, n)
            pl.semaphore_signal(barrier, inc=1, device_id=(me, p), device_id_type=MESH)
            return carry

        lax.fori_loop(1, n, greet, 0)
        pl.semaphore_wait(barrier, (m - 1) + (n - 1))

        def ep_to(p):
            return pltpu.make_async_remote_copy(
                src_ref=src_ref.at[:, :, pl.ds(p * width, width)],
                dst_ref=out_ref.at[:, pl.ds(me * groups, groups), :],
                send_sem=ep_send.at[p],
                recv_sem=ep_recv.at[me],
                device_id=(p, tm),
                device_id_type=MESH,
            )

        def ep_from(p):
            return pltpu.make_async_remote_copy(
                src_ref=src_ref.at[:, :, pl.ds(me * width, width)],
                dst_ref=out_ref.at[:, pl.ds(p * groups, groups), :],
                send_sem=ep_send.at[p],
                recv_sem=ep_recv.at[p],
                device_id=(p, tm),
                device_id_type=MESH,
            )

        for k in range(1, m):
            ep_to(lax.rem(me + k, m)).start()
        local = pltpu.make_async_copy(
            src_ref.at[:, :, pl.ds(me * width, width)],
            out_ref.at[:, pl.ds(me * groups, groups), :],
            local_sem.at[0],
        )
        local.start()

        histogram(leaf_ref, grad_ref, hess_ref, mine)
        staged = pltpu.make_async_copy(mine, held.at[tm], local_sem.at[1])
        staged.start()
        staged.wait()

        def tm_to(p):
            return pltpu.make_async_remote_copy(
                src_ref=held.at[tm],
                dst_ref=held.at[tm],
                send_sem=tm_send.at[p],
                recv_sem=tm_recv.at[tm],
                device_id=(me, p),
                device_id_type=MESH,
            )

        def tm_from(p):
            return pltpu.make_async_remote_copy(
                src_ref=held.at[tm],
                dst_ref=held.at[p],
                send_sem=tm_send.at[p],
                recv_sem=tm_recv.at[p],
                device_id=(me, p),
                device_id_type=MESH,
            )

        def send(k, carry):
            tm_to(lax.rem(tm + k, n)).start()
            return carry

        lax.fori_loop(1, n, send, 0)

        def wait(k, carry):
            p = lax.rem(tm + k, n)
            tm_to(p).wait_send()
            tm_from(p).wait_recv()
            return carry

        lax.fori_loop(1, n, wait, 0)

        def add(k, total):
            return total + held[lax.rem(tm + k, n)]

        totals = lax.fori_loop(1, n, add, held[tm])
        lane = lax.broadcasted_iota(jnp.int32, (groups, 2 * leaves), 1)
        hsum = pltpu.roll(totals, leaves, 1)
        table = jnp.where(lane < leaves, -totals / (hsum + 1.0), 0.0)
        weights_ref[...] = table[:, :leaves]

        mine[...] = table

        def one_tile(t, carry):
            rows = pl.ds(pl.multiple_of(t * 8, 8), 8)
            row = mine[rows, :]

            def one(step, carry):
                cols = pl.ds(pl.multiple_of(step * 128, 128), 128)
                picked = jnp.take_along_axis(
                    row, leaf_ref[rows, cols], axis=1, mode="promise_in_bounds"
                )
                new_ref[rows, cols] = pred_ref[rows, cols] + picked
                return carry

            lax.fori_loop(0, length // 128, one, 0, unroll=8)
            return carry

        lax.fori_loop(0, tiles, one_tile, 0)

        local.wait()
        for k in range(1, m):
            p = lax.rem(me + k, m)
            ep_to(p).wait_send()
            ep_from(p).wait_recv()

    vmem = pl.BlockSpec(memory_space=pltpu.VMEM)
    grad_hess, leaf_weights, new_pred = pl.pallas_call(
        kernel,
        out_shape=(
            jax.ShapeDtypeStruct((two, groups * m, width), stacked.dtype),
            jax.ShapeDtypeStruct((groups, leaves), jnp.float32),
            jax.ShapeDtypeStruct((groups, length), jnp.float32),
        ),
        in_specs=[pl.BlockSpec(memory_space=pl.ANY), vmem, vmem, vmem, vmem],
        out_specs=(pl.BlockSpec(memory_space=pl.ANY), vmem, vmem),
        scratch_shapes=[
            pltpu.VMEM((groups, 2 * leaves), jnp.float32),
            pltpu.VMEM((n, groups, 2 * leaves), jnp.float32),
            pltpu.SemaphoreType.DMA((m,)),
            pltpu.SemaphoreType.DMA((m,)),
            pltpu.SemaphoreType.DMA((n,)),
            pltpu.SemaphoreType.DMA((n,)),
            pltpu.SemaphoreType.DMA((2,)),
        ],
        compiler_params=pltpu.CompilerParams(
            collective_id=cid, has_side_effects=True, vmem_limit_bytes=60 * 1024 * 1024
        ),
    )(stacked, leaf_index, gradient, hessian, predictions)
    return grad_hess, leaf_weights, new_pred


def tm_exchange(payload, held, send_sem, recv_sem, stage_sem, ep, me, n):
    staged = pltpu.make_async_copy(payload, held.at[me], stage_sem)
    staged.start()
    staged.wait()

    def copy_to(p):
        return pltpu.make_async_remote_copy(
            src_ref=held.at[me],
            dst_ref=held.at[me],
            send_sem=send_sem.at[p],
            recv_sem=recv_sem.at[me],
            device_id=(ep, p),
            device_id_type=MESH,
        )

    def copy_from(p):
        return pltpu.make_async_remote_copy(
            src_ref=held.at[me],
            dst_ref=held.at[p],
            send_sem=send_sem.at[p],
            recv_sem=recv_sem.at[p],
            device_id=(ep, p),
            device_id_type=MESH,
        )

    def send(k, carry):
        copy_to(lax.rem(me + k, n)).start()
        return carry

    lax.fori_loop(1, n, send, 0)

    def wait(k, carry):
        p = lax.rem(me + k, n)
        copy_to(p).wait_send()
        copy_from(p).wait_recv()
        return carry

    lax.fori_loop(1, n, wait, 0)


def scan_lanes(x, from_end):
    lane = lax.broadcasted_iota(jnp.int32, x.shape, 1)
    k = 1
    while k < 128:
        if from_end:
            moved = pltpu.roll(x, 128 - k, 1)
            x = x + jnp.where(lane < 128 - k, moved, 0.0)
        else:
            moved = pltpu.roll(x, k, 1)
            x = x + jnp.where(lane >= k, moved, 0.0)
        k *= 2
    return x


def front(predictions, events, first_rows, last_rows):
    n = lax.axis_size("tm")
    groups, length = predictions.shape
    tiles = groups // 8
    blocks = length // 128
    span = math.gcd(blocks, 8)
    groups_n = blocks // span

    def kernel(pred_ref, ev_ref, first_ref, last_ref,
               grad_ref, hess_ref, both_ref,
               weight, one, two, pay_a, held_a, pay_b, held_b,
               send_a, recv_a, send_b, recv_b, stage):
        me = lax.axis_index("tm")
        ep = lax.axis_index("ep")
        barrier = pltpu.get_barrier_semaphore()

        def greet(k, carry):
            p = lax.rem(me + k, n)
            pl.semaphore_signal(barrier, inc=1, device_id=(ep, p), device_id_type=MESH)
            return carry

        lax.fori_loop(1, n, greet, 0)
        pl.semaphore_wait(barrier, n - 1)

        lane_j = lax.broadcasted_iota(jnp.int32, (128, 128), 0)
        lane_i = lax.broadcasted_iota(jnp.int32, (128, 128), 1)
        upper = (lane_j >= lane_i).astype(jnp.bfloat16)
        lower = (lane_j <= lane_i).astype(jnp.bfloat16)

        def run_sum(x, matrix):
            hi = x.astype(jnp.bfloat16)
            rest = x - hi.astype(jnp.float32)
            mid = rest.astype(jnp.bfloat16)
            lo = (rest - mid.astype(jnp.float32)).astype(jnp.bfloat16)
            out = jnp.dot(hi, matrix, preferred_element_type=jnp.float32)
            out = out + jnp.dot(mid, matrix, preferred_element_type=jnp.float32)
            return out + jnp.dot(lo, matrix, preferred_element_type=jnp.float32)

        def block_cols(b):
            return pl.ds(pl.multiple_of(b * 128, 128), 128)

        def suffix_tile(t, carry):
            rows = pl.ds(pl.multiple_of(t * 8, 8), 8)

            def one_group(j, later):
                b0 = (groups_n - 1 - j) * span
                pieces = []
                for k in range(span):
                    w = jnp.exp(pred_ref[rows, block_cols(b0 + k)])
                    weight[rows, block_cols(b0 + k)] = w
                    pieces.append(w)
                s = run_sum(jnp.concatenate(pieces, axis=0), upper)
                idx = first_ref[pl.ds(pl.multiple_of(b0 * 8, 8), 8 * span), :]
                r = jnp.take_along_axis(s, idx, axis=1, mode="promise_in_bounds")
                for k in reversed(range(span)):
                    one[rows, block_cols(b0 + k)] = r[8 * k:8 * k + 8] + later
                    later = later + jnp.broadcast_to(s[8 * k:8 * k + 8, 0:1], (8, 128))
                return later

            total = lax.fori_loop(0, groups_n, one_group, jnp.zeros((8, 128), jnp.float32))
            pay_a[rows, :] = total
            return carry

        lax.fori_loop(0, tiles, suffix_tile, 0)
        tm_exchange(pay_a, held_a, send_a, recv_a, stage.at[0], ep, me, n)

        def add_later(k, total):
            p = lax.rem(me + k, n)
            return total + jnp.where(p > me, held_a[p], 0.0)

        pay_a[...] = lax.fori_loop(1, n, add_later, jnp.zeros((groups, 128), jnp.float32))

        def prefix_tile(t, carry):
            rows = pl.ds(pl.multiple_of(t * 8, 8), 8)
            later = pay_a[rows, :]

            def one_group(j, carries):
                c1, c2 = carries
                b0 = j * span
                firsts, seconds = [], []
                for k in range(span):
                    risk = one[rows, block_cols(b0 + k)] + later
                    observed = ev_ref[rows, block_cols(b0 + k)].astype(jnp.float32)
                    inv_one = observed / risk
                    firsts.append(inv_one)
                    seconds.append(inv_one / risk)
                s = run_sum(jnp.concatenate(firsts + seconds, axis=0), lower)
                idx = last_ref[pl.ds(pl.multiple_of(b0 * 8, 8), 8 * span), :]
                idx = jnp.concatenate([idx, idx], axis=0)
                r = jnp.take_along_axis(s, idx, axis=1, mode="promise_in_bounds")
                half = 8 * span
                for k in range(span):
                    one[rows, block_cols(b0 + k)] = r[8 * k:8 * k + 8] + c1
                    two[rows, block_cols(b0 + k)] = r[half + 8 * k:half + 8 * k + 8] + c2
                    c1 = c1 + jnp.broadcast_to(s[8 * k:8 * k + 8, 127:128], (8, 128))
                    c2 = c2 + jnp.broadcast_to(s[half + 8 * k:half + 8 * k + 8, 127:128], (8, 128))
                return (c1, c2)

            zero = jnp.zeros((8, 128), jnp.float32)
            c1, c2 = lax.fori_loop(0, groups_n, one_group, (zero, zero))
            pay_b[rows, :] = c1
            pay_b[pl.ds(pl.multiple_of(groups + t * 8, 8), 8), :] = c2
            return carry

        lax.fori_loop(0, tiles, prefix_tile, 0)
        tm_exchange(pay_b, held_b, send_b, recv_b, stage.at[1], ep, me, n)

        def add_earlier(k, total):
            p = lax.rem(me + k, n)
            return total + jnp.where(p < me, held_b[p], 0.0)

        pay_b[...] = lax.fori_loop(1, n, add_earlier, jnp.zeros((2 * groups, 128), jnp.float32))

        def out_tile(t, carry):
            rows = pl.ds(pl.multiple_of(t * 8, 8), 8)
            e1 = jnp.tile(pay_b[rows, :], (1, span))
            e2 = jnp.tile(pay_b[pl.ds(pl.multiple_of(groups + t * 8, 8), 8), :], (1, span))

            def one_group(j, carry):
                cols = pl.ds(pl.multiple_of(j * span * 128, span * 128), span * 128)
                w = weight[rows, cols]
                a1 = one[rows, cols] + e1
                a2 = two[rows, cols] + e2
                observed = ev_ref[rows, cols].astype(jnp.float32)
                g = w * a1 - observed
                h = w * a1 - w * w * a2
                grad_ref[rows, cols] = g
                hess_ref[rows, cols] = h
                both_ref[0, rows, cols] = g.astype(jnp.bfloat16)
                both_ref[1, rows, cols] = h.astype(jnp.bfloat16)
                return carry

            lax.fori_loop(0, groups_n, one_group, 0)
            return carry

        lax.fori_loop(0, tiles, out_tile, 0)

    vmem = pl.BlockSpec(memory_space=pltpu.VMEM)
    return pl.pallas_call(
        kernel,
        out_shape=(
            jax.ShapeDtypeStruct((groups, length), jnp.float32),
            jax.ShapeDtypeStruct((groups, length), jnp.float32),
            jax.ShapeDtypeStruct((2, groups, length), jnp.bfloat16),
        ),
        in_specs=[vmem, vmem, vmem, vmem],
        out_specs=(vmem, vmem, vmem),
        scratch_shapes=[
            pltpu.VMEM((groups, length), jnp.float32),
            pltpu.VMEM((groups, length), jnp.float32),
            pltpu.VMEM((groups, length), jnp.float32),
            pltpu.VMEM((groups, 128), jnp.float32),
            pltpu.VMEM((n, groups, 128), jnp.float32),
            pltpu.VMEM((2 * groups, 128), jnp.float32),
            pltpu.VMEM((n, 2 * groups, 128), jnp.float32),
            pltpu.SemaphoreType.DMA((n,)),
            pltpu.SemaphoreType.DMA((n,)),
            pltpu.SemaphoreType.DMA((n,)),
            pltpu.SemaphoreType.DMA((n,)),
            pltpu.SemaphoreType.DMA((2,)),
        ],
        compiler_params=pltpu.CompilerParams(
            collective_id=0, has_side_effects=True, vmem_limit_bytes=60 * 1024 * 1024
        ),
    )(predictions, events, first_rows, last_rows)


def tie_rows(tie_start):
    length = tie_start.shape[0]
    blocks = length // 128
    starts = tie_start.reshape(blocks, 128)
    labels = jnp.arange(128, dtype=jnp.int32)
    first_local = lax.cummax(jnp.where(starts == 1, labels[None, :], 0), axis=1)
    next_start = jnp.concatenate([starts[:, 1:], jnp.ones((blocks, 1), jnp.int32)], axis=1)
    last_local = lax.cummin(jnp.where(next_start == 1, labels[None, :], 127), axis=1, reverse=True)

    def spread(rows):
        return jnp.broadcast_to(rows[:, None, :], (blocks, 8, 128)).reshape(blocks * 8, 128)

    return spread(first_local), spread(last_local)


def lane_pad(vectors):
    width = vectors.shape[1]
    return jnp.pad(vectors, ((0, 0), (0, 128 - width)))


def tile_matrices(tie_start):
    length = tie_start.shape[0]
    blocks = length // 128
    starts = tie_start.reshape(blocks, 128)
    labels = jnp.arange(128, dtype=jnp.int32)
    first_local = lax.cummax(jnp.where(starts == 1, labels[None, :], 0), axis=1)
    next_start = jnp.concatenate([starts[:, 1:], jnp.ones((blocks, 1), jnp.int32)], axis=1)
    last_local = lax.cummin(jnp.where(next_start == 1, labels[None, :], 127), axis=1, reverse=True)
    backward = (labels[None, :, None] >= first_local[:, None, :]).astype(jnp.float32)
    forward = (labels[None, :, None] <= last_local[:, None, :]).astype(jnp.float32)
    return (backward, forward)


def block_cumsum(values, matrices, from_end):
    groups = values.shape[0]
    length = values.shape[1]
    blocks = length // 128
    shaped = values.reshape(groups, blocks, 128)
    within = jnp.einsum("ebj,bji->ebi", shaped, matrices, precision=lax.Precision.HIGH)
    totals = jnp.sum(shaped, axis=2)
    if from_end:
        offsets = jnp.cumsum(totals[:, ::-1], axis=1)[:, ::-1] - totals
    else:
        offsets = jnp.cumsum(totals, axis=1) - totals
    return (within + offsets[:, :, None]).reshape(groups, length)


def leaf_update(predictions, leaf_index, table):
    groups, length = leaf_index.shape
    tiles = groups // 8
    table = lane_pad(table)

    def kernel(table_ref, pred_ref, leaf_ref, out_ref):
        row = table_ref[...]

        def one(step, carry):
            cols = pl.ds(pl.multiple_of(step * 128, 128), 128)
            picked = jnp.take_along_axis(row, leaf_ref[:, cols], axis=1, mode="promise_in_bounds")
            out_ref[:, cols] = pred_ref[:, cols] + picked
            return carry

        lax.fori_loop(0, length // 128, one, 0, unroll=8)

    spec = pl.BlockSpec((8, length), lambda t: (t, 0))
    return pl.pallas_call(
        kernel,
        grid=(tiles,),
        out_shape=jax.ShapeDtypeStruct((groups, length), jnp.float32),
        in_specs=[pl.BlockSpec((8, 128), lambda t: (t, 0)), spec, spec],
        out_specs=spec,
    )(table, predictions, leaf_index)


def on_device(predictions, leaf_index, events, tie_start):
    first_rows, last_rows = tie_rows(tie_start)
    gradient, hessian, stacked = front(predictions, events, first_rows, last_rows)
    grad_hess, leaf_weights, new_pred = finish(
        stacked, leaf_index, gradient, hessian, predictions, LEAVES, 2
    )
    grad_hess = grad_hess.reshape(2, grad_hess.shape[1], 1, grad_hess.shape[2])
    return (new_pred, leaf_weights, grad_hess)


def solution(mesh):
    placed = (P("ep", "tm"), P("ep", "tm"), P("ep", "tm"), P("tm"))
    return jax.shard_map(
        on_device,
        mesh=mesh,
        in_specs=placed,
        out_specs=(P("ep", "tm"), P("ep", None), P(None, None, "tm", "ep")),
        check_vma=False,
    )
```

```python
import math

import jax
import jax.numpy as jnp
from jax import lax
from jax.experimental import pallas as pl
from jax.experimental.pallas import tpu as pltpu
from jax.sharding import PartitionSpec as P

LEAVES = 64
MESH = pl.DeviceIdType.MESH


def tm_combine(part, mode, cid):
    n = lax.axis_size("tm")
    rows = part.shape[0]

    def kernel(x_ref, out_ref, held, send_sem, recv_sem):
        me = lax.axis_index("tm")
        ep = lax.axis_index("ep")
        barrier = pltpu.get_barrier_semaphore()

        def greet(k, carry):
            p = lax.rem(me + k, n)
            pl.semaphore_signal(barrier, inc=1, device_id=(ep, p), device_id_type=MESH)
            return carry

        lax.fori_loop(1, n, greet, 0)
        pl.semaphore_wait(barrier, n - 1)

        def copy_to(p):
            return pltpu.make_async_remote_copy(
                src_ref=x_ref,
                dst_ref=held.at[me],
                send_sem=send_sem.at[p],
                recv_sem=recv_sem.at[me],
                device_id=(ep, p),
                device_id_type=MESH,
            )

        def copy_from(p):
            return pltpu.make_async_remote_copy(
                src_ref=x_ref,
                dst_ref=held.at[p],
                send_sem=send_sem.at[p],
                recv_sem=recv_sem.at[p],
                device_id=(ep, p),
                device_id_type=MESH,
            )

        def send(k, carry):
            copy_to(lax.rem(me + k, n)).start()
            return carry

        lax.fori_loop(1, n, send, 0)

        def wait(k, carry):
            p = lax.rem(me + k, n)
            copy_to(p).wait_send()
            copy_from(p).wait_recv()
            return carry

        lax.fori_loop(1, n, wait, 0)

        if mode == "all":
            total = x_ref[...]
        else:
            total = jnp.zeros((rows, 128), jnp.float32)

        def add(k, total):
            p = lax.rem(me + k, n)
            if mode == "all":
                keep = True
            elif mode == "later":
                keep = p > me
            else:
                keep = p < me
            return total + jnp.where(keep, held[p], 0.0)

        out_ref[...] = lax.fori_loop(1, n, add, total)

    return pl.pallas_call(
        kernel,
        out_shape=jax.ShapeDtypeStruct((rows, 128), jnp.float32),
        in_specs=[pl.BlockSpec(memory_space=pltpu.VMEM)],
        out_specs=pl.BlockSpec(memory_space=pltpu.VMEM),
        scratch_shapes=[
            pltpu.VMEM((n, rows, 128), jnp.float32),
            pltpu.SemaphoreType.DMA((n,)),
            pltpu.SemaphoreType.DMA((n,)),
        ],
        compiler_params=pltpu.CompilerParams(collective_id=cid, has_side_effects=True),
    )(part)


def exchange_and_sum(stacked, leaf_index, gradient, hessian, leaves, cid):
    m = lax.axis_size("ep")
    two, groups, length = stacked.shape
    width = length // m
    tiles = groups // 8
    side = leaves // 8
    chunk = math.gcd(length, 4096)
    cols_all = side * 4 * 8

    def histogram(leaf_ref, grad_ref, hess_ref, sums_ref):
        row_id = lax.broadcasted_iota(jnp.int32, (side * 8, cols_all), 0)
        col_id = lax.broadcasted_iota(jnp.int32, (side * 8, cols_all), 1)
        diagonal = lax.rem(row_id, 8) == lax.rem(col_id, 8)
        fold = (
            lax.broadcasted_iota(jnp.int32, (cols_all, side * 4), 0) // 8
            == lax.broadcasted_iota(jnp.int32, (cols_all, side * 4), 1)
        ).astype(jnp.float32)

        def one_tile(t, carry):
            rows = pl.ds(pl.multiple_of(t * 8, 8), 8)

            def one_chunk(step, total):
                cols = pl.ds(pl.multiple_of(step * chunk, chunk), chunk)
                leaf = leaf_ref[rows, cols]
                grad = grad_ref[rows, cols]
                hess = hess_ref[rows, cols]
                high = lax.shift_right_logical(leaf, 3)
                low = jnp.bitwise_and(leaf, 7)
                grad_hi = grad.astype(jnp.bfloat16).astype(jnp.float32)
                hess_hi = hess.astype(jnp.bfloat16).astype(jnp.float32)
                values = (grad_hi, grad - grad_hi, hess_hi, hess - hess_hi)
                ones = jnp.concatenate(
                    [jnp.where(high == a, 1.0, 0.0) for a in range(side)], axis=0
                ).astype(jnp.bfloat16)
                pieces = []
                for b in range(side):
                    hit = low == b
                    for value in values:
                        pieces.append(jnp.where(hit, value, 0.0))
                parts = jnp.concatenate(pieces, axis=0).astype(jnp.bfloat16)
                return total + lax.dot_general(
                    ones, parts, (((1,), (1,)), ((), ())), preferred_element_type=jnp.float32
                )

            total = jnp.zeros((side * 8, cols_all), jnp.float32)
            total = lax.fori_loop(0, length // chunk, one_chunk, total)
            total = jnp.where(diagonal, total, 0.0)
            sums_ref[t] = jnp.dot(
                total, fold, precision=lax.Precision.HIGHEST, preferred_element_type=jnp.float32
            )
            return carry

        lax.fori_loop(0, tiles, one_tile, 0)

    def kernel(src_ref, leaf_ref, grad_ref, hess_ref, out_ref, sums_ref, send_sem, recv_sem, local_sem):
        me = lax.axis_index("ep")
        tm = lax.axis_index("tm")
        barrier = pltpu.get_barrier_semaphore()
        for k in range(1, m):
            p = lax.rem(me + k, m)
            pl.semaphore_signal(barrier, inc=1, device_id=(p, tm), device_id_type=MESH)
        pl.semaphore_wait(barrier, m - 1)

        def copy_to(p):
            return pltpu.make_async_remote_copy(
                src_ref=src_ref.at[:, :, pl.ds(p * width, width)],
                dst_ref=out_ref.at[:, pl.ds(me * groups, groups), :],
                send_sem=send_sem.at[p],
                recv_sem=recv_sem.at[me],
                device_id=(p, tm),
                device_id_type=MESH,
            )

        def copy_from(p):
            return pltpu.make_async_remote_copy(
                src_ref=src_ref.at[:, :, pl.ds(me * width, width)],
                dst_ref=out_ref.at[:, pl.ds(p * groups, groups), :],
                send_sem=send_sem.at[p],
                recv_sem=recv_sem.at[p],
                device_id=(p, tm),
                device_id_type=MESH,
            )

        for k in range(1, m):
            copy_to(lax.rem(me + k, m)).start()
        local = pltpu.make_async_copy(
            src_ref.at[:, :, pl.ds(me * width, width)],
            out_ref.at[:, pl.ds(me * groups, groups), :],
            local_sem.at[0],
        )
        local.start()
        histogram(leaf_ref, grad_ref, hess_ref, sums_ref)
        local.wait()
        for k in range(1, m):
            p = lax.rem(me + k, m)
            copy_to(p).wait_send()
            copy_from(p).wait_recv()

    vmem = pl.BlockSpec(memory_space=pltpu.VMEM)
    grad_hess, sums = pl.pallas_call(
        kernel,
        out_shape=(
            jax.ShapeDtypeStruct((two, groups * m, width), stacked.dtype),
            jax.ShapeDtypeStruct((tiles, side * 8, side * 4), jnp.float32),
        ),
        in_specs=[pl.BlockSpec(memory_space=pl.ANY), vmem, vmem, vmem],
        out_specs=(pl.BlockSpec(memory_space=pl.ANY), vmem),
        scratch_shapes=[
            pltpu.SemaphoreType.DMA((m,)),
            pltpu.SemaphoreType.DMA((m,)),
            pltpu.SemaphoreType.DMA((1,)),
        ],
        compiler_params=pltpu.CompilerParams(collective_id=cid, has_side_effects=True),
    )(stacked, leaf_index, gradient, hessian)
    sums = sums.reshape(tiles, side, 8, side, 4).transpose(0, 2, 1, 3, 4)
    sums = sums.reshape(groups, leaves, 4)
    gsum = sums[:, :, 0] + sums[:, :, 1]
    hsum = sums[:, :, 2] + sums[:, :, 3]
    return grad_hess, jnp.stack([gsum, hsum], axis=1)


def finish(stacked, leaf_index, gradient, hessian, predictions, leaves, cid):
    m = lax.axis_size("ep")
    n = lax.axis_size("tm")
    two, groups, length = stacked.shape
    width = length // m
    tiles = groups // 8
    side = leaves // 8
    chunk = math.gcd(length, 4096)
    cols_all = side * 4 * 8

    def histogram(leaf_ref, grad_ref, hess_ref, mine):
        row_id = lax.broadcasted_iota(jnp.int32, (side * 8, cols_all), 0)
        col_id = lax.broadcasted_iota(jnp.int32, (side * 8, cols_all), 1)
        diagonal = lax.rem(row_id, 8) == lax.rem(col_id, 8)
        src = lax.broadcasted_iota(jnp.int32, (cols_all, 2 * leaves), 0)
        dst = lax.broadcasted_iota(jnp.int32, (cols_all, 2 * leaves), 1)
        src_b = src // 32
        src_c = lax.rem(src // 8, 4)

        def one_tile(t, carry):
            rows = pl.ds(pl.multiple_of(t * 8, 8), 8)

            def one_chunk(step, total):
                cols = pl.ds(pl.multiple_of(step * chunk, chunk), chunk)
                leaf = leaf_ref[rows, cols]
                grad = grad_ref[rows, cols]
                hess = hess_ref[rows, cols]
                high = lax.shift_right_logical(leaf, 3)
                low = jnp.bitwise_and(leaf, 7)
                grad_hi = grad.astype(jnp.bfloat16).astype(jnp.float32)
                hess_hi = hess.astype(jnp.bfloat16).astype(jnp.float32)
                values = (grad_hi, grad - grad_hi, hess_hi, hess - hess_hi)
                ones = jnp.concatenate(
                    [jnp.where(high == a, 1.0, 0.0) for a in range(side)], axis=0
                ).astype(jnp.bfloat16)
                pieces = []
                for b in range(side):
                    hit = low == b
                    for value in values:
                        pieces.append(jnp.where(hit, value, 0.0))
                parts = jnp.concatenate(pieces, axis=0).astype(jnp.bfloat16)
                return total + lax.dot_general(
                    ones, parts, (((1,), (1,)), ((), ())), preferred_element_type=jnp.float32
                )

            total = jnp.zeros((side * 8, cols_all), jnp.float32)
            total = lax.fori_loop(0, length // chunk, one_chunk, total)
            total = jnp.where(diagonal, total, 0.0)
            out = jnp.zeros((8, 2 * leaves), jnp.float32)
            for a in range(side):
                fold = (dst == (src_c // 2) * leaves + a * side + src_b).astype(jnp.float32)
                out = out + jnp.dot(
                    total[a * 8:(a + 1) * 8, :], fold,
                    precision=lax.Precision.HIGHEST, preferred_element_type=jnp.float32,
                )
            mine[rows, :] = out
            return carry

        lax.fori_loop(0, tiles, one_tile, 0)

    def kernel(src_ref, leaf_ref, grad_ref, hess_ref, pred_ref,
               out_ref, weights_ref, new_ref,
               mine, held, ep_send, ep_recv, tm_send, tm_recv, local_sem):
        me = lax.axis_index("ep")
        tm = lax.axis_index("tm")
        barrier = pltpu.get_barrier_semaphore()
        for k in range(1, m):
            p = lax.rem(me + k, m)
            pl.semaphore_signal(barrier, inc=1, device_id=(p, tm), device_id_type=MESH)

        def greet(k, carry):
            p = lax.rem(tm + k, n)
            pl.semaphore_signal(barrier, inc=1, device_id=(me, p), device_id_type=MESH)
            return carry

        lax.fori_loop(1, n, greet, 0)
        pl.semaphore_wait(barrier, (m - 1) + (n - 1))

        def ep_to(p):
            return pltpu.make_async_remote_copy(
                src_ref=src_ref.at[:, :, pl.ds(p * width, width)],
                dst_ref=out_ref.at[:, pl.ds(me * groups, groups), :],
                send_sem=ep_send.at[p],
                recv_sem=ep_recv.at[me],
                device_id=(p, tm),
                device_id_type=MESH,
            )

        def ep_from(p):
            return pltpu.make_async_remote_copy(
                src_ref=src_ref.at[:, :, pl.ds(me * width, width)],
                dst_ref=out_ref.at[:, pl.ds(p * groups, groups), :],
                send_sem=ep_send.at[p],
                recv_sem=ep_recv.at[p],
                device_id=(p, tm),
                device_id_type=MESH,
            )

        for k in range(1, m):
            ep_to(lax.rem(me + k, m)).start()
        local = pltpu.make_async_copy(
            src_ref.at[:, :, pl.ds(me * width, width)],
            out_ref.at[:, pl.ds(me * groups, groups), :],
            local_sem.at[0],
        )
        local.start()

        histogram(leaf_ref, grad_ref, hess_ref, mine)
        staged = pltpu.make_async_copy(mine, held.at[tm], local_sem.at[1])
        staged.start()
        staged.wait()

        def tm_to(p):
            return pltpu.make_async_remote_copy(
                src_ref=held.at[tm],
                dst_ref=held.at[tm],
                send_sem=tm_send.at[p],
                recv_sem=tm_recv.at[tm],
                device_id=(me, p),
                device_id_type=MESH,
            )

        def tm_from(p):
            return pltpu.make_async_remote_copy(
                src_ref=held.at[tm],
                dst_ref=held.at[p],
                send_sem=tm_send.at[p],
                recv_sem=tm_recv.at[p],
                device_id=(me, p),
                device_id_type=MESH,
            )

        def send(k, carry):
            tm_to(lax.rem(tm + k, n)).start()
            return carry

        lax.fori_loop(1, n, send, 0)

        def wait(k, carry):
            p = lax.rem(tm + k, n)
            tm_to(p).wait_send()
            tm_from(p).wait_recv()
            return carry

        lax.fori_loop(1, n, wait, 0)

        def add(k, total):
            return total + held[lax.rem(tm + k, n)]

        totals = lax.fori_loop(1, n, add, held[tm])
        lane = lax.broadcasted_iota(jnp.int32, (groups, 2 * leaves), 1)
        hsum = pltpu.roll(totals, leaves, 1)
        table = jnp.where(lane < leaves, -totals / (hsum + 1.0), 0.0)
        weights_ref[...] = table[:, :leaves]

        mine[...] = table

        def one_tile(t, carry):
            rows = pl.ds(pl.multiple_of(t * 8, 8), 8)
            row = mine[rows, :]

            def one(step, carry):
                cols = pl.ds(pl.multiple_of(step * 128, 128), 128)
                picked = jnp.take_along_axis(
                    row, leaf_ref[rows, cols], axis=1, mode="promise_in_bounds"
                )
                new_ref[rows, cols] = pred_ref[rows, cols] + picked
                return carry

            lax.fori_loop(0, length // 128, one, 0, unroll=8)
            return carry

        lax.fori_loop(0, tiles, one_tile, 0)

        local.wait()
        for k in range(1, m):
            p = lax.rem(me + k, m)
            ep_to(p).wait_send()
            ep_from(p).wait_recv()

    vmem = pl.BlockSpec(memory_space=pltpu.VMEM)
    grad_hess, leaf_weights, new_pred = pl.pallas_call(
        kernel,
        out_shape=(
            jax.ShapeDtypeStruct((two, groups * m, width), stacked.dtype),
            jax.ShapeDtypeStruct((groups, leaves), jnp.float32),
            jax.ShapeDtypeStruct((groups, length), jnp.float32),
        ),
        in_specs=[pl.BlockSpec(memory_space=pl.ANY), vmem, vmem, vmem, vmem],
        out_specs=(pl.BlockSpec(memory_space=pl.ANY), vmem, vmem),
        scratch_shapes=[
            pltpu.VMEM((groups, 2 * leaves), jnp.float32),
            pltpu.VMEM((n, groups, 2 * leaves), jnp.float32),
            pltpu.SemaphoreType.DMA((m,)),
            pltpu.SemaphoreType.DMA((m,)),
            pltpu.SemaphoreType.DMA((n,)),
            pltpu.SemaphoreType.DMA((n,)),
            pltpu.SemaphoreType.DMA((2,)),
        ],
        compiler_params=pltpu.CompilerParams(
            collective_id=cid, has_side_effects=True, vmem_limit_bytes=60 * 1024 * 1024
        ),
    )(stacked, leaf_index, gradient, hessian, predictions)
    return grad_hess, leaf_weights, new_pred


def tm_exchange(payload, held, send_sem, recv_sem, stage_sem, ep, me, n):
    staged = pltpu.make_async_copy(payload, held.at[me], stage_sem)
    staged.start()
    staged.wait()

    def copy_to(p):
        return pltpu.make_async_remote_copy(
            src_ref=held.at[me],
            dst_ref=held.at[me],
            send_sem=send_sem.at[p],
            recv_sem=recv_sem.at[me],
            device_id=(ep, p),
            device_id_type=MESH,
        )

    def copy_from(p):
        return pltpu.make_async_remote_copy(
            src_ref=held.at[me],
            dst_ref=held.at[p],
            send_sem=send_sem.at[p],
            recv_sem=recv_sem.at[p],
            device_id=(ep, p),
            device_id_type=MESH,
        )

    def send(k, carry):
        copy_to(lax.rem(me + k, n)).start()
        return carry

    lax.fori_loop(1, n, send, 0)

    def wait(k, carry):
        p = lax.rem(me + k, n)
        copy_to(p).wait_send()
        copy_from(p).wait_recv()
        return carry

    lax.fori_loop(1, n, wait, 0)


def scan_lanes(x, from_end):
    lane = lax.broadcasted_iota(jnp.int32, x.shape, 1)
    k = 1
    while k < 128:
        if from_end:
            moved = pltpu.roll(x, 128 - k, 1)
            x = x + jnp.where(lane < 128 - k, moved, 0.0)
        else:
            moved = pltpu.roll(x, k, 1)
            x = x + jnp.where(lane >= k, moved, 0.0)
        k *= 2
    return x


def front(predictions, events, first_rows, last_rows):
    n = lax.axis_size("tm")
    groups, length = predictions.shape
    tiles = groups // 8
    blocks = length // 128
    span = math.gcd(blocks, 16)
    groups_n = blocks // span

    def kernel(pred_ref, ev_ref, first_ref, last_ref,
               grad_ref, hess_ref, both_ref,
               weight, one, two, pay_a, held_a, pay_b, held_b,
               send_a, recv_a, send_b, recv_b, stage):
        me = lax.axis_index("tm")
        ep = lax.axis_index("ep")
        barrier = pltpu.get_barrier_semaphore()

        def greet(k, carry):
            p = lax.rem(me + k, n)
            pl.semaphore_signal(barrier, inc=1, device_id=(ep, p), device_id_type=MESH)
            return carry

        lax.fori_loop(1, n, greet, 0)
        pl.semaphore_wait(barrier, n - 1)

        lane_j = lax.broadcasted_iota(jnp.int32, (128, 128), 0)
        lane_i = lax.broadcasted_iota(jnp.int32, (128, 128), 1)
        upper = (lane_j >= lane_i).astype(jnp.bfloat16)
        lower = (lane_j <= lane_i).astype(jnp.bfloat16)

        def run_sum(x, matrix):
            hi = x.astype(jnp.bfloat16)
            rest = x - hi.astype(jnp.float32)
            mid = rest.astype(jnp.bfloat16)
            lo = (rest - mid.astype(jnp.float32)).astype(jnp.bfloat16)
            out = jnp.dot(hi, matrix, preferred_element_type=jnp.float32)
            out = out + jnp.dot(mid, matrix, preferred_element_type=jnp.float32)
            return out + jnp.dot(lo, matrix, preferred_element_type=jnp.float32)

        def block_cols(b):
            return pl.ds(pl.multiple_of(b * 128, 128), 128)

        def suffix_tile(t, carry):
            rows = pl.ds(pl.multiple_of(t * 8, 8), 8)

            def one_group(j, later):
                b0 = (groups_n - 1 - j) * span
                pieces = []
                for k in range(span):
                    w = jnp.exp(pred_ref[rows, block_cols(b0 + k)])
                    weight[rows, block_cols(b0 + k)] = w
                    pieces.append(w)
                s = run_sum(jnp.concatenate(pieces, axis=0), upper)
                idx = first_ref[pl.ds(pl.multiple_of(b0 * 8, 8), 8 * span), :]
                r = jnp.take_along_axis(s, idx, axis=1, mode="promise_in_bounds")
                for k in reversed(range(span)):
                    one[rows, block_cols(b0 + k)] = r[8 * k:8 * k + 8] + later
                    later = later + jnp.broadcast_to(s[8 * k:8 * k + 8, 0:1], (8, 128))
                return later

            total = lax.fori_loop(0, groups_n, one_group, jnp.zeros((8, 128), jnp.float32), unroll=2)
            pay_a[rows, :] = total
            return carry

        lax.fori_loop(0, tiles, suffix_tile, 0)
        tm_exchange(pay_a, held_a, send_a, recv_a, stage.at[0], ep, me, n)

        def add_later(k, total):
            p = lax.rem(me + k, n)
            return total + jnp.where(p > me, held_a[p], 0.0)

        pay_a[...] = lax.fori_loop(1, n, add_later, jnp.zeros((groups, 128), jnp.float32))

        def prefix_tile(t, carry):
            rows = pl.ds(pl.multiple_of(t * 8, 8), 8)
            later = pay_a[rows, :]

            def one_group(j, carries):
                c1, c2 = carries
                b0 = j * span
                firsts, seconds = [], []
                for k in range(span):
                    risk = one[rows, block_cols(b0 + k)] + later
                    observed = ev_ref[rows, block_cols(b0 + k)].astype(jnp.float32)
                    inv_one = observed / risk
                    firsts.append(inv_one)
                    seconds.append(inv_one / risk)
                s = run_sum(jnp.concatenate(firsts + seconds, axis=0), lower)
                idx = last_ref[pl.ds(pl.multiple_of(b0 * 8, 8), 8 * span), :]
                idx = jnp.concatenate([idx, idx], axis=0)
                r = jnp.take_along_axis(s, idx, axis=1, mode="promise_in_bounds")
                half = 8 * span
                for k in range(span):
                    one[rows, block_cols(b0 + k)] = r[8 * k:8 * k + 8] + c1
                    two[rows, block_cols(b0 + k)] = r[half + 8 * k:half + 8 * k + 8] + c2
                    c1 = c1 + jnp.broadcast_to(s[8 * k:8 * k + 8, 127:128], (8, 128))
                    c2 = c2 + jnp.broadcast_to(s[half + 8 * k:half + 8 * k + 8, 127:128], (8, 128))
                return (c1, c2)

            zero = jnp.zeros((8, 128), jnp.float32)
            c1, c2 = lax.fori_loop(0, groups_n, one_group, (zero, zero), unroll=2)
            pay_b[rows, :] = c1
            pay_b[pl.ds(pl.multiple_of(groups + t * 8, 8), 8), :] = c2
            return carry

        lax.fori_loop(0, tiles, prefix_tile, 0)
        tm_exchange(pay_b, held_b, send_b, recv_b, stage.at[1], ep, me, n)

        def add_earlier(k, total):
            p = lax.rem(me + k, n)
            return total + jnp.where(p < me, held_b[p], 0.0)

        pay_b[...] = lax.fori_loop(1, n, add_earlier, jnp.zeros((2 * groups, 128), jnp.float32))

        def out_tile(t, carry):
            rows = pl.ds(pl.multiple_of(t * 8, 8), 8)
            e1 = jnp.tile(pay_b[rows, :], (1, span))
            e2 = jnp.tile(pay_b[pl.ds(pl.multiple_of(groups + t * 8, 8), 8), :], (1, span))

            def one_group(j, carry):
                cols = pl.ds(pl.multiple_of(j * span * 128, span * 128), span * 128)
                w = weight[rows, cols]
                a1 = one[rows, cols] + e1
                a2 = two[rows, cols] + e2
                observed = ev_ref[rows, cols].astype(jnp.float32)
                g = w * a1 - observed
                h = w * a1 - w * w * a2
                grad_ref[rows, cols] = g
                hess_ref[rows, cols] = h
                both_ref[0, rows, cols] = g.astype(jnp.bfloat16)
                both_ref[1, rows, cols] = h.astype(jnp.bfloat16)
                return carry

            lax.fori_loop(0, groups_n, one_group, 0)
            return carry

        lax.fori_loop(0, tiles, out_tile, 0)

    vmem = pl.BlockSpec(memory_space=pltpu.VMEM)
    return pl.pallas_call(
        kernel,
        out_shape=(
            jax.ShapeDtypeStruct((groups, length), jnp.float32),
            jax.ShapeDtypeStruct((groups, length), jnp.float32),
            jax.ShapeDtypeStruct((2, groups, length), jnp.bfloat16),
        ),
        in_specs=[vmem, vmem, vmem, vmem],
        out_specs=(vmem, vmem, vmem),
        scratch_shapes=[
            pltpu.VMEM((groups, length), jnp.float32),
            pltpu.VMEM((groups, length), jnp.float32),
            pltpu.VMEM((groups, length), jnp.float32),
            pltpu.VMEM((groups, 128), jnp.float32),
            pltpu.VMEM((n, groups, 128), jnp.float32),
            pltpu.VMEM((2 * groups, 128), jnp.float32),
            pltpu.VMEM((n, 2 * groups, 128), jnp.float32),
            pltpu.SemaphoreType.DMA((n,)),
            pltpu.SemaphoreType.DMA((n,)),
            pltpu.SemaphoreType.DMA((n,)),
            pltpu.SemaphoreType.DMA((n,)),
            pltpu.SemaphoreType.DMA((2,)),
        ],
        compiler_params=pltpu.CompilerParams(
            collective_id=0, has_side_effects=True, vmem_limit_bytes=60 * 1024 * 1024
        ),
    )(predictions, events, first_rows, last_rows)


def tie_rows(tie_start):
    length = tie_start.shape[0]
    blocks = length // 128
    starts = tie_start.reshape(blocks, 128)
    labels = jnp.arange(128, dtype=jnp.int32)
    first_local = lax.cummax(jnp.where(starts == 1, labels[None, :], 0), axis=1)
    next_start = jnp.concatenate([starts[:, 1:], jnp.ones((blocks, 1), jnp.int32)], axis=1)
    last_local = lax.cummin(jnp.where(next_start == 1, labels[None, :], 127), axis=1, reverse=True)

    def spread(rows):
        return jnp.broadcast_to(rows[:, None, :], (blocks, 8, 128)).reshape(blocks * 8, 128)

    return spread(first_local), spread(last_local)


def lane_pad(vectors):
    width = vectors.shape[1]
    return jnp.pad(vectors, ((0, 0), (0, 128 - width)))


def tile_matrices(tie_start):
    length = tie_start.shape[0]
    blocks = length // 128
    starts = tie_start.reshape(blocks, 128)
    labels = jnp.arange(128, dtype=jnp.int32)
    first_local = lax.cummax(jnp.where(starts == 1, labels[None, :], 0), axis=1)
    next_start = jnp.concatenate([starts[:, 1:], jnp.ones((blocks, 1), jnp.int32)], axis=1)
    last_local = lax.cummin(jnp.where(next_start == 1, labels[None, :], 127), axis=1, reverse=True)
    backward = (labels[None, :, None] >= first_local[:, None, :]).astype(jnp.float32)
    forward = (labels[None, :, None] <= last_local[:, None, :]).astype(jnp.float32)
    return (backward, forward)


def block_cumsum(values, matrices, from_end):
    groups = values.shape[0]
    length = values.shape[1]
    blocks = length // 128
    shaped = values.reshape(groups, blocks, 128)
    within = jnp.einsum("ebj,bji->ebi", shaped, matrices, precision=lax.Precision.HIGH)
    totals = jnp.sum(shaped, axis=2)
    if from_end:
        offsets = jnp.cumsum(totals[:, ::-1], axis=1)[:, ::-1] - totals
    else:
        offsets = jnp.cumsum(totals, axis=1) - totals
    return (within + offsets[:, :, None]).reshape(groups, length)


def leaf_update(predictions, leaf_index, table):
    groups, length = leaf_index.shape
    tiles = groups // 8
    table = lane_pad(table)

    def kernel(table_ref, pred_ref, leaf_ref, out_ref):
        row = table_ref[...]

        def one(step, carry):
            cols = pl.ds(pl.multiple_of(step * 128, 128), 128)
            picked = jnp.take_along_axis(row, leaf_ref[:, cols], axis=1, mode="promise_in_bounds")
            out_ref[:, cols] = pred_ref[:, cols] + picked
            return carry

        lax.fori_loop(0, length // 128, one, 0, unroll=8)

    spec = pl.BlockSpec((8, length), lambda t: (t, 0))
    return pl.pallas_call(
        kernel,
        grid=(tiles,),
        out_shape=jax.ShapeDtypeStruct((groups, length), jnp.float32),
        in_specs=[pl.BlockSpec((8, 128), lambda t: (t, 0)), spec, spec],
        out_specs=spec,
    )(table, predictions, leaf_index)


def on_device(predictions, leaf_index, events, tie_start):
    first_rows, last_rows = tie_rows(tie_start)
    gradient, hessian, stacked = front(predictions, events, first_rows, last_rows)
    grad_hess, leaf_weights, new_pred = finish(
        stacked, leaf_index, gradient, hessian, predictions, LEAVES, 2
    )
    grad_hess = grad_hess.reshape(2, grad_hess.shape[1], 1, grad_hess.shape[2])
    return (new_pred, leaf_weights, grad_hess)


def solution(mesh):
    placed = (P("ep", "tm"), P("ep", "tm"), P("ep", "tm"), P("tm"))
    return jax.shard_map(
        on_device,
        mesh=mesh,
        in_specs=placed,
        out_specs=(P("ep", "tm"), P("ep", None), P(None, None, "tm", "ep")),
        check_vma=False,
    )
```

```python
import math

import jax
import jax.numpy as jnp
from jax import lax
from jax.experimental import pallas as pl
from jax.experimental.pallas import tpu as pltpu
from jax.sharding import PartitionSpec as P

LEAVES = 64
MESH = pl.DeviceIdType.MESH


def tm_combine(part, mode, cid):
    n = lax.axis_size("tm")
    rows = part.shape[0]

    def kernel(x_ref, out_ref, held, send_sem, recv_sem):
        me = lax.axis_index("tm")
        ep = lax.axis_index("ep")
        barrier = pltpu.get_barrier_semaphore()

        def greet(k, carry):
            p = lax.rem(me + k, n)
            pl.semaphore_signal(barrier, inc=1, device_id=(ep, p), device_id_type=MESH)
            return carry

        lax.fori_loop(1, n, greet, 0)
        pl.semaphore_wait(barrier, n - 1)

        def copy_to(p):
            return pltpu.make_async_remote_copy(
                src_ref=x_ref,
                dst_ref=held.at[me],
                send_sem=send_sem.at[p],
                recv_sem=recv_sem.at[me],
                device_id=(ep, p),
                device_id_type=MESH,
            )

        def copy_from(p):
            return pltpu.make_async_remote_copy(
                src_ref=x_ref,
                dst_ref=held.at[p],
                send_sem=send_sem.at[p],
                recv_sem=recv_sem.at[p],
                device_id=(ep, p),
                device_id_type=MESH,
            )

        def send(k, carry):
            copy_to(lax.rem(me + k, n)).start()
            return carry

        lax.fori_loop(1, n, send, 0)

        def wait(k, carry):
            p = lax.rem(me + k, n)
            copy_to(p).wait_send()
            copy_from(p).wait_recv()
            return carry

        lax.fori_loop(1, n, wait, 0)

        if mode == "all":
            total = x_ref[...]
        else:
            total = jnp.zeros((rows, 128), jnp.float32)

        def add(k, total):
            p = lax.rem(me + k, n)
            if mode == "all":
                keep = True
            elif mode == "later":
                keep = p > me
            else:
                keep = p < me
            return total + jnp.where(keep, held[p], 0.0)

        out_ref[...] = lax.fori_loop(1, n, add, total)

    return pl.pallas_call(
        kernel,
        out_shape=jax.ShapeDtypeStruct((rows, 128), jnp.float32),
        in_specs=[pl.BlockSpec(memory_space=pltpu.VMEM)],
        out_specs=pl.BlockSpec(memory_space=pltpu.VMEM),
        scratch_shapes=[
            pltpu.VMEM((n, rows, 128), jnp.float32),
            pltpu.SemaphoreType.DMA((n,)),
            pltpu.SemaphoreType.DMA((n,)),
        ],
        compiler_params=pltpu.CompilerParams(collective_id=cid, has_side_effects=True),
    )(part)


def exchange_and_sum(stacked, leaf_index, gradient, hessian, leaves, cid):
    m = lax.axis_size("ep")
    two, groups, length = stacked.shape
    width = length // m
    tiles = groups // 8
    side = leaves // 8
    chunk = math.gcd(length, 4096)
    cols_all = side * 4 * 8

    def histogram(leaf_ref, grad_ref, hess_ref, sums_ref):
        row_id = lax.broadcasted_iota(jnp.int32, (side * 8, cols_all), 0)
        col_id = lax.broadcasted_iota(jnp.int32, (side * 8, cols_all), 1)
        diagonal = lax.rem(row_id, 8) == lax.rem(col_id, 8)
        fold = (
            lax.broadcasted_iota(jnp.int32, (cols_all, side * 4), 0) // 8
            == lax.broadcasted_iota(jnp.int32, (cols_all, side * 4), 1)
        ).astype(jnp.float32)

        def one_tile(t, carry):
            rows = pl.ds(pl.multiple_of(t * 8, 8), 8)

            def one_chunk(step, total):
                cols = pl.ds(pl.multiple_of(step * chunk, chunk), chunk)
                leaf = leaf_ref[rows, cols]
                grad = grad_ref[rows, cols]
                hess = hess_ref[rows, cols]
                high = lax.shift_right_logical(leaf, 3)
                low = jnp.bitwise_and(leaf, 7)
                grad_hi = grad.astype(jnp.bfloat16).astype(jnp.float32)
                hess_hi = hess.astype(jnp.bfloat16).astype(jnp.float32)
                values = (grad_hi, grad - grad_hi, hess_hi, hess - hess_hi)
                ones = jnp.concatenate(
                    [jnp.where(high == a, 1.0, 0.0) for a in range(side)], axis=0
                ).astype(jnp.bfloat16)
                pieces = []
                for b in range(side):
                    hit = low == b
                    for value in values:
                        pieces.append(jnp.where(hit, value, 0.0))
                parts = jnp.concatenate(pieces, axis=0).astype(jnp.bfloat16)
                return total + lax.dot_general(
                    ones, parts, (((1,), (1,)), ((), ())), preferred_element_type=jnp.float32
                )

            total = jnp.zeros((side * 8, cols_all), jnp.float32)
            total = lax.fori_loop(0, length // chunk, one_chunk, total)
            total = jnp.where(diagonal, total, 0.0)
            sums_ref[t] = jnp.dot(
                total, fold, precision=lax.Precision.HIGHEST, preferred_element_type=jnp.float32
            )
            return carry

        lax.fori_loop(0, tiles, one_tile, 0)

    def kernel(src_ref, leaf_ref, grad_ref, hess_ref, out_ref, sums_ref, send_sem, recv_sem, local_sem):
        me = lax.axis_index("ep")
        tm = lax.axis_index("tm")
        barrier = pltpu.get_barrier_semaphore()
        for k in range(1, m):
            p = lax.rem(me + k, m)
            pl.semaphore_signal(barrier, inc=1, device_id=(p, tm), device_id_type=MESH)
        pl.semaphore_wait(barrier, m - 1)

        def copy_to(p):
            return pltpu.make_async_remote_copy(
                src_ref=src_ref.at[:, :, pl.ds(p * width, width)],
                dst_ref=out_ref.at[:, pl.ds(me * groups, groups), :],
                send_sem=send_sem.at[p],
                recv_sem=recv_sem.at[me],
                device_id=(p, tm),
                device_id_type=MESH,
            )

        def copy_from(p):
            return pltpu.make_async_remote_copy(
                src_ref=src_ref.at[:, :, pl.ds(me * width, width)],
                dst_ref=out_ref.at[:, pl.ds(p * groups, groups), :],
                send_sem=send_sem.at[p],
                recv_sem=recv_sem.at[p],
                device_id=(p, tm),
                device_id_type=MESH,
            )

        for k in range(1, m):
            copy_to(lax.rem(me + k, m)).start()
        local = pltpu.make_async_copy(
            src_ref.at[:, :, pl.ds(me * width, width)],
            out_ref.at[:, pl.ds(me * groups, groups), :],
            local_sem.at[0],
        )
        local.start()
        histogram(leaf_ref, grad_ref, hess_ref, sums_ref)
        local.wait()
        for k in range(1, m):
            p = lax.rem(me + k, m)
            copy_to(p).wait_send()
            copy_from(p).wait_recv()

    vmem = pl.BlockSpec(memory_space=pltpu.VMEM)
    grad_hess, sums = pl.pallas_call(
        kernel,
        out_shape=(
            jax.ShapeDtypeStruct((two, groups * m, width), stacked.dtype),
            jax.ShapeDtypeStruct((tiles, side * 8, side * 4), jnp.float32),
        ),
        in_specs=[pl.BlockSpec(memory_space=pl.ANY), vmem, vmem, vmem],
        out_specs=(pl.BlockSpec(memory_space=pl.ANY), vmem),
        scratch_shapes=[
            pltpu.SemaphoreType.DMA((m,)),
            pltpu.SemaphoreType.DMA((m,)),
            pltpu.SemaphoreType.DMA((1,)),
        ],
        compiler_params=pltpu.CompilerParams(collective_id=cid, has_side_effects=True),
    )(stacked, leaf_index, gradient, hessian)
    sums = sums.reshape(tiles, side, 8, side, 4).transpose(0, 2, 1, 3, 4)
    sums = sums.reshape(groups, leaves, 4)
    gsum = sums[:, :, 0] + sums[:, :, 1]
    hsum = sums[:, :, 2] + sums[:, :, 3]
    return grad_hess, jnp.stack([gsum, hsum], axis=1)


def finish(stacked, leaf_index, gradient, hessian, predictions, leaves, cid):
    m = lax.axis_size("ep")
    n = lax.axis_size("tm")
    two, groups, length = stacked.shape
    width = length // m
    tiles = groups // 8
    side = leaves // 8
    chunk = math.gcd(length, 4096)
    cols_all = side * 4 * 8

    def histogram(leaf_ref, grad_ref, hess_ref, mine):
        row_id = lax.broadcasted_iota(jnp.int32, (side * 8, cols_all), 0)
        col_id = lax.broadcasted_iota(jnp.int32, (side * 8, cols_all), 1)
        diagonal = lax.rem(row_id, 8) == lax.rem(col_id, 8)
        src = lax.broadcasted_iota(jnp.int32, (cols_all, 2 * leaves), 0)
        dst = lax.broadcasted_iota(jnp.int32, (cols_all, 2 * leaves), 1)
        src_b = src // 32
        src_c = lax.rem(src // 8, 4)

        def one_tile(t, carry):
            rows = pl.ds(pl.multiple_of(t * 8, 8), 8)

            def one_chunk(step, total):
                cols = pl.ds(pl.multiple_of(step * chunk, chunk), chunk)
                leaf = leaf_ref[rows, cols]
                grad = grad_ref[rows, cols]
                hess = hess_ref[rows, cols]
                high = lax.shift_right_logical(leaf, 3)
                low = jnp.bitwise_and(leaf, 7)
                grad_hi = grad.astype(jnp.bfloat16).astype(jnp.float32)
                hess_hi = hess.astype(jnp.bfloat16).astype(jnp.float32)
                values = (grad_hi, grad - grad_hi, hess_hi, hess - hess_hi)
                ones = jnp.concatenate(
                    [jnp.where(high == a, 1.0, 0.0) for a in range(side)], axis=0
                ).astype(jnp.bfloat16)
                pieces = []
                for b in range(side):
                    hit = low == b
                    for value in values:
                        pieces.append(jnp.where(hit, value, 0.0))
                parts = jnp.concatenate(pieces, axis=0).astype(jnp.bfloat16)
                return total + lax.dot_general(
                    ones, parts, (((1,), (1,)), ((), ())), preferred_element_type=jnp.float32
                )

            total = jnp.zeros((side * 8, cols_all), jnp.float32)
            total = lax.fori_loop(0, length // chunk, one_chunk, total)
            total = jnp.where(diagonal, total, 0.0)
            out = jnp.zeros((8, 2 * leaves), jnp.float32)
            for a in range(side):
                fold = (dst == (src_c // 2) * leaves + a * side + src_b).astype(jnp.float32)
                out = out + jnp.dot(
                    total[a * 8:(a + 1) * 8, :], fold,
                    precision=lax.Precision.HIGHEST, preferred_element_type=jnp.float32,
                )
            mine[rows, :] = out
            return carry

        lax.fori_loop(0, tiles, one_tile, 0)

    def kernel(src_ref, leaf_ref, grad_ref, hess_ref, pred_ref,
               out_ref, weights_ref, new_ref,
               mine, held, ep_send, ep_recv, tm_send, tm_recv, local_sem):
        me = lax.axis_index("ep")
        tm = lax.axis_index("tm")
        barrier = pltpu.get_barrier_semaphore()
        for k in range(1, m):
            p = lax.rem(me + k, m)
            pl.semaphore_signal(barrier, inc=1, device_id=(p, tm), device_id_type=MESH)

        def greet(k, carry):
            p = lax.rem(tm + k, n)
            pl.semaphore_signal(barrier, inc=1, device_id=(me, p), device_id_type=MESH)
            return carry

        lax.fori_loop(1, n, greet, 0)
        pl.semaphore_wait(barrier, (m - 1) + (n - 1))

        def ep_to(p):
            return pltpu.make_async_remote_copy(
                src_ref=src_ref.at[:, :, pl.ds(p * width, width)],
                dst_ref=out_ref.at[:, pl.ds(me * groups, groups), :],
                send_sem=ep_send.at[p],
                recv_sem=ep_recv.at[me],
                device_id=(p, tm),
                device_id_type=MESH,
            )

        def ep_from(p):
            return pltpu.make_async_remote_copy(
                src_ref=src_ref.at[:, :, pl.ds(me * width, width)],
                dst_ref=out_ref.at[:, pl.ds(p * groups, groups), :],
                send_sem=ep_send.at[p],
                recv_sem=ep_recv.at[p],
                device_id=(p, tm),
                device_id_type=MESH,
            )

        for k in range(1, m):
            ep_to(lax.rem(me + k, m)).start()
        local = pltpu.make_async_copy(
            src_ref.at[:, :, pl.ds(me * width, width)],
            out_ref.at[:, pl.ds(me * groups, groups), :],
            local_sem.at[0],
        )
        local.start()

        histogram(leaf_ref, grad_ref, hess_ref, mine)
        staged = pltpu.make_async_copy(mine, held.at[tm], local_sem.at[1])
        staged.start()
        staged.wait()

        def tm_to(p):
            return pltpu.make_async_remote_copy(
                src_ref=held.at[tm],
                dst_ref=held.at[tm],
                send_sem=tm_send.at[p],
                recv_sem=tm_recv.at[tm],
                device_id=(me, p),
                device_id_type=MESH,
            )

        def tm_from(p):
            return pltpu.make_async_remote_copy(
                src_ref=held.at[tm],
                dst_ref=held.at[p],
                send_sem=tm_send.at[p],
                recv_sem=tm_recv.at[p],
                device_id=(me, p),
                device_id_type=MESH,
            )

        def send(k, carry):
            tm_to(lax.rem(tm + k, n)).start()
            return carry

        lax.fori_loop(1, n, send, 0)

        def wait(k, carry):
            p = lax.rem(tm + k, n)
            tm_to(p).wait_send()
            tm_from(p).wait_recv()
            return carry

        lax.fori_loop(1, n, wait, 0)

        def add(k, total):
            return total + held[lax.rem(tm + k, n)]

        totals = lax.fori_loop(1, n, add, held[tm])
        lane = lax.broadcasted_iota(jnp.int32, (groups, 2 * leaves), 1)
        hsum = pltpu.roll(totals, leaves, 1)
        table = jnp.where(lane < leaves, -totals / (hsum + 1.0), 0.0)
        weights_ref[...] = table[:, :leaves]

        mine[...] = table

        def one_tile(t, carry):
            rows = pl.ds(pl.multiple_of(t * 8, 8), 8)
            row = mine[rows, :]

            def one(step, carry):
                cols = pl.ds(pl.multiple_of(step * 128, 128), 128)
                picked = jnp.take_along_axis(
                    row, leaf_ref[rows, cols], axis=1, mode="promise_in_bounds"
                )
                new_ref[rows, cols] = pred_ref[rows, cols] + picked
                return carry

            lax.fori_loop(0, length // 128, one, 0, unroll=8)
            return carry

        lax.fori_loop(0, tiles, one_tile, 0)

        local.wait()
        for k in range(1, m):
            p = lax.rem(me + k, m)
            ep_to(p).wait_send()
            ep_from(p).wait_recv()

    vmem = pl.BlockSpec(memory_space=pltpu.VMEM)
    grad_hess, leaf_weights, new_pred = pl.pallas_call(
        kernel,
        out_shape=(
            jax.ShapeDtypeStruct((two, groups * m, width), stacked.dtype),
            jax.ShapeDtypeStruct((groups, leaves), jnp.float32),
            jax.ShapeDtypeStruct((groups, length), jnp.float32),
        ),
        in_specs=[pl.BlockSpec(memory_space=pl.ANY), vmem, vmem, vmem, vmem],
        out_specs=(pl.BlockSpec(memory_space=pl.ANY), vmem, vmem),
        scratch_shapes=[
            pltpu.VMEM((groups, 2 * leaves), jnp.float32),
            pltpu.VMEM((n, groups, 2 * leaves), jnp.float32),
            pltpu.SemaphoreType.DMA((m,)),
            pltpu.SemaphoreType.DMA((m,)),
            pltpu.SemaphoreType.DMA((n,)),
            pltpu.SemaphoreType.DMA((n,)),
            pltpu.SemaphoreType.DMA((2,)),
        ],
        compiler_params=pltpu.CompilerParams(
            collective_id=cid, has_side_effects=True, vmem_limit_bytes=60 * 1024 * 1024
        ),
    )(stacked, leaf_index, gradient, hessian, predictions)
    return grad_hess, leaf_weights, new_pred


def tm_exchange(payload, held, send_sem, recv_sem, stage_sem, ep, me, n):
    staged = pltpu.make_async_copy(payload, held.at[me], stage_sem)
    staged.start()
    staged.wait()

    def copy_to(p):
        return pltpu.make_async_remote_copy(
            src_ref=held.at[me],
            dst_ref=held.at[me],
            send_sem=send_sem.at[p],
            recv_sem=recv_sem.at[me],
            device_id=(ep, p),
            device_id_type=MESH,
        )

    def copy_from(p):
        return pltpu.make_async_remote_copy(
            src_ref=held.at[me],
            dst_ref=held.at[p],
            send_sem=send_sem.at[p],
            recv_sem=recv_sem.at[p],
            device_id=(ep, p),
            device_id_type=MESH,
        )

    def send(k, carry):
        copy_to(lax.rem(me + k, n)).start()
        return carry

    lax.fori_loop(1, n, send, 0)

    def wait(k, carry):
        p = lax.rem(me + k, n)
        copy_to(p).wait_send()
        copy_from(p).wait_recv()
        return carry

    lax.fori_loop(1, n, wait, 0)


def scan_lanes(x, from_end):
    lane = lax.broadcasted_iota(jnp.int32, x.shape, 1)
    k = 1
    while k < 128:
        if from_end:
            moved = pltpu.roll(x, 128 - k, 1)
            x = x + jnp.where(lane < 128 - k, moved, 0.0)
        else:
            moved = pltpu.roll(x, k, 1)
            x = x + jnp.where(lane >= k, moved, 0.0)
        k *= 2
    return x


def front(predictions, events, first_rows, last_rows):
    n = lax.axis_size("tm")
    groups, length = predictions.shape
    tiles = groups // 8
    blocks = length // 128
    span = math.gcd(blocks, 32)
    groups_n = blocks // span

    def kernel(pred_ref, ev_ref, first_ref, last_ref,
               grad_ref, hess_ref, both_ref,
               weight, one, two, pay_a, held_a, pay_b, held_b,
               send_a, recv_a, send_b, recv_b, stage):
        me = lax.axis_index("tm")
        ep = lax.axis_index("ep")
        barrier = pltpu.get_barrier_semaphore()

        def greet(k, carry):
            p = lax.rem(me + k, n)
            pl.semaphore_signal(barrier, inc=1, device_id=(ep, p), device_id_type=MESH)
            return carry

        lax.fori_loop(1, n, greet, 0)
        pl.semaphore_wait(barrier, n - 1)

        lane_j = lax.broadcasted_iota(jnp.int32, (128, 128), 0)
        lane_i = lax.broadcasted_iota(jnp.int32, (128, 128), 1)
        upper = (lane_j >= lane_i).astype(jnp.bfloat16)
        lower = (lane_j <= lane_i).astype(jnp.bfloat16)

        def run_sum(x, matrix):
            hi = x.astype(jnp.bfloat16)
            rest = x - hi.astype(jnp.float32)
            mid = rest.astype(jnp.bfloat16)
            lo = (rest - mid.astype(jnp.float32)).astype(jnp.bfloat16)
            out = jnp.dot(hi, matrix, preferred_element_type=jnp.float32)
            out = out + jnp.dot(mid, matrix, preferred_element_type=jnp.float32)
            return out + jnp.dot(lo, matrix, preferred_element_type=jnp.float32)

        def block_cols(b):
            return pl.ds(pl.multiple_of(b * 128, 128), 128)

        def suffix_tile(t, carry):
            rows = pl.ds(pl.multiple_of(t * 8, 8), 8)

            def one_group(j, later):
                b0 = (groups_n - 1 - j) * span
                pieces = []
                for k in range(span):
                    w = jnp.exp(pred_ref[rows, block_cols(b0 + k)])
                    weight[rows, block_cols(b0 + k)] = w
                    pieces.append(w)
                s = run_sum(jnp.concatenate(pieces, axis=0), upper)
                idx = first_ref[pl.ds(pl.multiple_of(b0 * 8, 8), 8 * span), :]
                r = jnp.take_along_axis(s, idx, axis=1, mode="promise_in_bounds")
                for k in reversed(range(span)):
                    one[rows, block_cols(b0 + k)] = r[8 * k:8 * k + 8] + later
                    later = later + jnp.broadcast_to(s[8 * k:8 * k + 8, 0:1], (8, 128))
                return later

            total = lax.fori_loop(0, groups_n, one_group, jnp.zeros((8, 128), jnp.float32), unroll=2)
            pay_a[rows, :] = total
            return carry

        lax.fori_loop(0, tiles, suffix_tile, 0)
        tm_exchange(pay_a, held_a, send_a, recv_a, stage.at[0], ep, me, n)

        def add_later(k, total):
            p = lax.rem(me + k, n)
            return total + jnp.where(p > me, held_a[p], 0.0)

        pay_a[...] = lax.fori_loop(1, n, add_later, jnp.zeros((groups, 128), jnp.float32))

        def prefix_tile(t, carry):
            rows = pl.ds(pl.multiple_of(t * 8, 8), 8)
            later = pay_a[rows, :]

            def one_group(j, carries):
                c1, c2 = carries
                b0 = j * span
                firsts, seconds = [], []
                for k in range(span):
                    risk = one[rows, block_cols(b0 + k)] + later
                    observed = ev_ref[rows, block_cols(b0 + k)].astype(jnp.float32)
                    inv_one = observed / risk
                    firsts.append(inv_one)
                    seconds.append(inv_one / risk)
                s = run_sum(jnp.concatenate(firsts + seconds, axis=0), lower)
                idx = last_ref[pl.ds(pl.multiple_of(b0 * 8, 8), 8 * span), :]
                idx = jnp.concatenate([idx, idx], axis=0)
                r = jnp.take_along_axis(s, idx, axis=1, mode="promise_in_bounds")
                half = 8 * span
                for k in range(span):
                    one[rows, block_cols(b0 + k)] = r[8 * k:8 * k + 8] + c1
                    two[rows, block_cols(b0 + k)] = r[half + 8 * k:half + 8 * k + 8] + c2
                    c1 = c1 + jnp.broadcast_to(s[8 * k:8 * k + 8, 127:128], (8, 128))
                    c2 = c2 + jnp.broadcast_to(s[half + 8 * k:half + 8 * k + 8, 127:128], (8, 128))
                return (c1, c2)

            zero = jnp.zeros((8, 128), jnp.float32)
            c1, c2 = lax.fori_loop(0, groups_n, one_group, (zero, zero), unroll=2)
            pay_b[rows, :] = c1
            pay_b[pl.ds(pl.multiple_of(groups + t * 8, 8), 8), :] = c2
            return carry

        lax.fori_loop(0, tiles, prefix_tile, 0)
        tm_exchange(pay_b, held_b, send_b, recv_b, stage.at[1], ep, me, n)

        def add_earlier(k, total):
            p = lax.rem(me + k, n)
            return total + jnp.where(p < me, held_b[p], 0.0)

        pay_b[...] = lax.fori_loop(1, n, add_earlier, jnp.zeros((2 * groups, 128), jnp.float32))

        def out_tile(t, carry):
            rows = pl.ds(pl.multiple_of(t * 8, 8), 8)
            e1 = jnp.tile(pay_b[rows, :], (1, span))
            e2 = jnp.tile(pay_b[pl.ds(pl.multiple_of(groups + t * 8, 8), 8), :], (1, span))

            def one_group(j, carry):
                cols = pl.ds(pl.multiple_of(j * span * 128, span * 128), span * 128)
                w = weight[rows, cols]
                a1 = one[rows, cols] + e1
                a2 = two[rows, cols] + e2
                observed = ev_ref[rows, cols].astype(jnp.float32)
                g = w * a1 - observed
                h = w * a1 - w * w * a2
                grad_ref[rows, cols] = g
                hess_ref[rows, cols] = h
                both_ref[0, rows, cols] = g.astype(jnp.bfloat16)
                both_ref[1, rows, cols] = h.astype(jnp.bfloat16)
                return carry

            lax.fori_loop(0, groups_n, one_group, 0)
            return carry

        lax.fori_loop(0, tiles, out_tile, 0)

    vmem = pl.BlockSpec(memory_space=pltpu.VMEM)
    return pl.pallas_call(
        kernel,
        out_shape=(
            jax.ShapeDtypeStruct((groups, length), jnp.float32),
            jax.ShapeDtypeStruct((groups, length), jnp.float32),
            jax.ShapeDtypeStruct((2, groups, length), jnp.bfloat16),
        ),
        in_specs=[vmem, vmem, vmem, vmem],
        out_specs=(vmem, vmem, vmem),
        scratch_shapes=[
            pltpu.VMEM((groups, length), jnp.float32),
            pltpu.VMEM((groups, length), jnp.float32),
            pltpu.VMEM((groups, length), jnp.float32),
            pltpu.VMEM((groups, 128), jnp.float32),
            pltpu.VMEM((n, groups, 128), jnp.float32),
            pltpu.VMEM((2 * groups, 128), jnp.float32),
            pltpu.VMEM((n, 2 * groups, 128), jnp.float32),
            pltpu.SemaphoreType.DMA((n,)),
            pltpu.SemaphoreType.DMA((n,)),
            pltpu.SemaphoreType.DMA((n,)),
            pltpu.SemaphoreType.DMA((n,)),
            pltpu.SemaphoreType.DMA((2,)),
        ],
        compiler_params=pltpu.CompilerParams(
            collective_id=0, has_side_effects=True, vmem_limit_bytes=60 * 1024 * 1024
        ),
    )(predictions, events, first_rows, last_rows)


def tie_rows(tie_start):
    length = tie_start.shape[0]
    blocks = length // 128
    starts = tie_start.reshape(blocks, 128)
    labels = jnp.arange(128, dtype=jnp.int32)
    first_local = lax.cummax(jnp.where(starts == 1, labels[None, :], 0), axis=1)
    next_start = jnp.concatenate([starts[:, 1:], jnp.ones((blocks, 1), jnp.int32)], axis=1)
    last_local = lax.cummin(jnp.where(next_start == 1, labels[None, :], 127), axis=1, reverse=True)

    def spread(rows):
        return jnp.broadcast_to(rows[:, None, :], (blocks, 8, 128)).reshape(blocks * 8, 128)

    return spread(first_local), spread(last_local)


def lane_pad(vectors):
    width = vectors.shape[1]
    return jnp.pad(vectors, ((0, 0), (0, 128 - width)))


def tile_matrices(tie_start):
    length = tie_start.shape[0]
    blocks = length // 128
    starts = tie_start.reshape(blocks, 128)
    labels = jnp.arange(128, dtype=jnp.int32)
    first_local = lax.cummax(jnp.where(starts == 1, labels[None, :], 0), axis=1)
    next_start = jnp.concatenate([starts[:, 1:], jnp.ones((blocks, 1), jnp.int32)], axis=1)
    last_local = lax.cummin(jnp.where(next_start == 1, labels[None, :], 127), axis=1, reverse=True)
    backward = (labels[None, :, None] >= first_local[:, None, :]).astype(jnp.float32)
    forward = (labels[None, :, None] <= last_local[:, None, :]).astype(jnp.float32)
    return (backward, forward)


def block_cumsum(values, matrices, from_end):
    groups = values.shape[0]
    length = values.shape[1]
    blocks = length // 128
    shaped = values.reshape(groups, blocks, 128)
    within = jnp.einsum("ebj,bji->ebi", shaped, matrices, precision=lax.Precision.HIGH)
    totals = jnp.sum(shaped, axis=2)
    if from_end:
        offsets = jnp.cumsum(totals[:, ::-1], axis=1)[:, ::-1] - totals
    else:
        offsets = jnp.cumsum(totals, axis=1) - totals
    return (within + offsets[:, :, None]).reshape(groups, length)


def leaf_update(predictions, leaf_index, table):
    groups, length = leaf_index.shape
    tiles = groups // 8
    table = lane_pad(table)

    def kernel(table_ref, pred_ref, leaf_ref, out_ref):
        row = table_ref[...]

        def one(step, carry):
            cols = pl.ds(pl.multiple_of(step * 128, 128), 128)
            picked = jnp.take_along_axis(row, leaf_ref[:, cols], axis=1, mode="promise_in_bounds")
            out_ref[:, cols] = pred_ref[:, cols] + picked
            return carry

        lax.fori_loop(0, length // 128, one, 0, unroll=8)

    spec = pl.BlockSpec((8, length), lambda t: (t, 0))
    return pl.pallas_call(
        kernel,
        grid=(tiles,),
        out_shape=jax.ShapeDtypeStruct((groups, length), jnp.float32),
        in_specs=[pl.BlockSpec((8, 128), lambda t: (t, 0)), spec, spec],
        out_specs=spec,
    )(table, predictions, leaf_index)


def on_device(predictions, leaf_index, events, tie_start):
    first_rows, last_rows = tie_rows(tie_start)
    gradient, hessian, stacked = front(predictions, events, first_rows, last_rows)
    grad_hess, leaf_weights, new_pred = finish(
        stacked, leaf_index, gradient, hessian, predictions, LEAVES, 2
    )
    grad_hess = grad_hess.reshape(2, grad_hess.shape[1], 1, grad_hess.shape[2])
    return (new_pred, leaf_weights, grad_hess)


def solution(mesh):
    placed = (P("ep", "tm"), P("ep", "tm"), P("ep", "tm"), P("tm"))
    return jax.shard_map(
        on_device,
        mesh=mesh,
        in_specs=placed,
        out_specs=(P("ep", "tm"), P("ep", None), P(None, None, "tm", "ep")),
        check_vma=False,
    )
```

```python
import math

import jax
import jax.numpy as jnp
from jax import lax
from jax.experimental import pallas as pl
from jax.experimental.pallas import tpu as pltpu
from jax.sharding import PartitionSpec as P

LEAVES = 64
MESH = pl.DeviceIdType.MESH


def tm_combine(part, mode, cid):
    n = lax.axis_size("tm")
    rows = part.shape[0]

    def kernel(x_ref, out_ref, held, send_sem, recv_sem):
        me = lax.axis_index("tm")
        ep = lax.axis_index("ep")
        barrier = pltpu.get_barrier_semaphore()

        def greet(k, carry):
            p = lax.rem(me + k, n)
            pl.semaphore_signal(barrier, inc=1, device_id=(ep, p), device_id_type=MESH)
            return carry

        lax.fori_loop(1, n, greet, 0)
        pl.semaphore_wait(barrier, n - 1)

        def copy_to(p):
            return pltpu.make_async_remote_copy(
                src_ref=x_ref,
                dst_ref=held.at[me],
                send_sem=send_sem.at[p],
                recv_sem=recv_sem.at[me],
                device_id=(ep, p),
                device_id_type=MESH,
            )

        def copy_from(p):
            return pltpu.make_async_remote_copy(
                src_ref=x_ref,
                dst_ref=held.at[p],
                send_sem=send_sem.at[p],
                recv_sem=recv_sem.at[p],
                device_id=(ep, p),
                device_id_type=MESH,
            )

        def send(k, carry):
            copy_to(lax.rem(me + k, n)).start()
            return carry

        lax.fori_loop(1, n, send, 0)

        def wait(k, carry):
            p = lax.rem(me + k, n)
            copy_to(p).wait_send()
            copy_from(p).wait_recv()
            return carry

        lax.fori_loop(1, n, wait, 0)

        if mode == "all":
            total = x_ref[...]
        else:
            total = jnp.zeros((rows, 128), jnp.float32)

        def add(k, total):
            p = lax.rem(me + k, n)
            if mode == "all":
                keep = True
            elif mode == "later":
                keep = p > me
            else:
                keep = p < me
            return total + jnp.where(keep, held[p], 0.0)

        out_ref[...] = lax.fori_loop(1, n, add, total)

    return pl.pallas_call(
        kernel,
        out_shape=jax.ShapeDtypeStruct((rows, 128), jnp.float32),
        in_specs=[pl.BlockSpec(memory_space=pltpu.VMEM)],
        out_specs=pl.BlockSpec(memory_space=pltpu.VMEM),
        scratch_shapes=[
            pltpu.VMEM((n, rows, 128), jnp.float32),
            pltpu.SemaphoreType.DMA((n,)),
            pltpu.SemaphoreType.DMA((n,)),
        ],
        compiler_params=pltpu.CompilerParams(collective_id=cid, has_side_effects=True),
    )(part)


def exchange_and_sum(stacked, leaf_index, gradient, hessian, leaves, cid):
    m = lax.axis_size("ep")
    two, groups, length = stacked.shape
    width = length // m
    tiles = groups // 8
    side = leaves // 8
    chunk = math.gcd(length, 4096)
    cols_all = side * 4 * 8

    def histogram(leaf_ref, grad_ref, hess_ref, sums_ref):
        row_id = lax.broadcasted_iota(jnp.int32, (side * 8, cols_all), 0)
        col_id = lax.broadcasted_iota(jnp.int32, (side * 8, cols_all), 1)
        diagonal = lax.rem(row_id, 8) == lax.rem(col_id, 8)
        fold = (
            lax.broadcasted_iota(jnp.int32, (cols_all, side * 4), 0) // 8
            == lax.broadcasted_iota(jnp.int32, (cols_all, side * 4), 1)
        ).astype(jnp.float32)

        def one_tile(t, carry):
            rows = pl.ds(pl.multiple_of(t * 8, 8), 8)

            def one_chunk(step, total):
                cols = pl.ds(pl.multiple_of(step * chunk, chunk), chunk)
                leaf = leaf_ref[rows, cols]
                grad = grad_ref[rows, cols]
                hess = hess_ref[rows, cols]
                high = lax.shift_right_logical(leaf, 3)
                low = jnp.bitwise_and(leaf, 7)
                grad_hi = grad.astype(jnp.bfloat16).astype(jnp.float32)
                hess_hi = hess.astype(jnp.bfloat16).astype(jnp.float32)
                values = (grad_hi, grad - grad_hi, hess_hi, hess - hess_hi)
                ones = jnp.concatenate(
                    [jnp.where(high == a, 1.0, 0.0) for a in range(side)], axis=0
                ).astype(jnp.bfloat16)
                pieces = []
                for b in range(side):
                    hit = low == b
                    for value in values:
                        pieces.append(jnp.where(hit, value, 0.0))
                parts = jnp.concatenate(pieces, axis=0).astype(jnp.bfloat16)
                return total + lax.dot_general(
                    ones, parts, (((1,), (1,)), ((), ())), preferred_element_type=jnp.float32
                )

            total = jnp.zeros((side * 8, cols_all), jnp.float32)
            total = lax.fori_loop(0, length // chunk, one_chunk, total)
            total = jnp.where(diagonal, total, 0.0)
            sums_ref[t] = jnp.dot(
                total, fold, precision=lax.Precision.HIGHEST, preferred_element_type=jnp.float32
            )
            return carry

        lax.fori_loop(0, tiles, one_tile, 0)

    def kernel(src_ref, leaf_ref, grad_ref, hess_ref, out_ref, sums_ref, send_sem, recv_sem, local_sem):
        me = lax.axis_index("ep")
        tm = lax.axis_index("tm")
        barrier = pltpu.get_barrier_semaphore()
        for k in range(1, m):
            p = lax.rem(me + k, m)
            pl.semaphore_signal(barrier, inc=1, device_id=(p, tm), device_id_type=MESH)
        pl.semaphore_wait(barrier, m - 1)

        def copy_to(p):
            return pltpu.make_async_remote_copy(
                src_ref=src_ref.at[:, :, pl.ds(p * width, width)],
                dst_ref=out_ref.at[:, pl.ds(me * groups, groups), :],
                send_sem=send_sem.at[p],
                recv_sem=recv_sem.at[me],
                device_id=(p, tm),
                device_id_type=MESH,
            )

        def copy_from(p):
            return pltpu.make_async_remote_copy(
                src_ref=src_ref.at[:, :, pl.ds(me * width, width)],
                dst_ref=out_ref.at[:, pl.ds(p * groups, groups), :],
                send_sem=send_sem.at[p],
                recv_sem=recv_sem.at[p],
                device_id=(p, tm),
                device_id_type=MESH,
            )

        for k in range(1, m):
            copy_to(lax.rem(me + k, m)).start()
        local = pltpu.make_async_copy(
            src_ref.at[:, :, pl.ds(me * width, width)],
            out_ref.at[:, pl.ds(me * groups, groups), :],
            local_sem.at[0],
        )
        local.start()
        histogram(leaf_ref, grad_ref, hess_ref, sums_ref)
        local.wait()
        for k in range(1, m):
            p = lax.rem(me + k, m)
            copy_to(p).wait_send()
            copy_from(p).wait_recv()

    vmem = pl.BlockSpec(memory_space=pltpu.VMEM)
    grad_hess, sums = pl.pallas_call(
        kernel,
        out_shape=(
            jax.ShapeDtypeStruct((two, groups * m, width), stacked.dtype),
            jax.ShapeDtypeStruct((tiles, side * 8, side * 4), jnp.float32),
        ),
        in_specs=[pl.BlockSpec(memory_space=pl.ANY), vmem, vmem, vmem],
        out_specs=(pl.BlockSpec(memory_space=pl.ANY), vmem),
        scratch_shapes=[
            pltpu.SemaphoreType.DMA((m,)),
            pltpu.SemaphoreType.DMA((m,)),
            pltpu.SemaphoreType.DMA((1,)),
        ],
        compiler_params=pltpu.CompilerParams(collective_id=cid, has_side_effects=True),
    )(stacked, leaf_index, gradient, hessian)
    sums = sums.reshape(tiles, side, 8, side, 4).transpose(0, 2, 1, 3, 4)
    sums = sums.reshape(groups, leaves, 4)
    gsum = sums[:, :, 0] + sums[:, :, 1]
    hsum = sums[:, :, 2] + sums[:, :, 3]
    return grad_hess, jnp.stack([gsum, hsum], axis=1)


def finish(stacked, leaf_index, gradient, hessian, predictions, leaves, cid):
    m = lax.axis_size("ep")
    n = lax.axis_size("tm")
    two, groups, length = stacked.shape
    width = length // m
    tiles = groups // 8
    side = leaves // 8
    chunk = math.gcd(length, 4096)
    cols_all = side * 4 * 8

    def histogram(leaf_ref, grad_ref, hess_ref, mine):
        row_id = lax.broadcasted_iota(jnp.int32, (side * 8, cols_all), 0)
        col_id = lax.broadcasted_iota(jnp.int32, (side * 8, cols_all), 1)
        diagonal = lax.rem(row_id, 8) == lax.rem(col_id, 8)
        src = lax.broadcasted_iota(jnp.int32, (cols_all, 2 * leaves), 0)
        dst = lax.broadcasted_iota(jnp.int32, (cols_all, 2 * leaves), 1)
        src_b = src // 32
        src_c = lax.rem(src // 8, 4)

        def one_tile(t, carry):
            rows = pl.ds(pl.multiple_of(t * 8, 8), 8)

            def one_chunk(step, total):
                cols = pl.ds(pl.multiple_of(step * chunk, chunk), chunk)
                leaf = leaf_ref[rows, cols]
                grad = grad_ref[rows, cols]
                hess = hess_ref[rows, cols]
                high = lax.shift_right_logical(leaf, 3)
                low = jnp.bitwise_and(leaf, 7)
                grad_hi = grad.astype(jnp.bfloat16).astype(jnp.float32)
                hess_hi = hess.astype(jnp.bfloat16).astype(jnp.float32)
                values = (grad_hi, grad - grad_hi, hess_hi, hess - hess_hi)
                ones = jnp.concatenate(
                    [jnp.where(high == a, 1.0, 0.0) for a in range(side)], axis=0
                ).astype(jnp.bfloat16)
                pieces = []
                for b in range(side):
                    hit = low == b
                    for value in values:
                        pieces.append(jnp.where(hit, value, 0.0))
                parts = jnp.concatenate(pieces, axis=0).astype(jnp.bfloat16)
                return total + lax.dot_general(
                    ones, parts, (((1,), (1,)), ((), ())), preferred_element_type=jnp.float32
                )

            total = jnp.zeros((side * 8, cols_all), jnp.float32)
            total = lax.fori_loop(0, length // chunk, one_chunk, total)
            total = jnp.where(diagonal, total, 0.0)
            out = jnp.zeros((8, 2 * leaves), jnp.float32)
            for a in range(side):
                fold = (dst == (src_c // 2) * leaves + a * side + src_b).astype(jnp.float32)
                out = out + jnp.dot(
                    total[a * 8:(a + 1) * 8, :], fold,
                    precision=lax.Precision.HIGHEST, preferred_element_type=jnp.float32,
                )
            mine[rows, :] = out
            return carry

        lax.fori_loop(0, tiles, one_tile, 0)

    def kernel(src_ref, leaf_ref, grad_ref, hess_ref, pred_ref,
               out_ref, weights_ref, new_ref,
               mine, held, ep_send, ep_recv, tm_send, tm_recv, local_sem):
        me = lax.axis_index("ep")
        tm = lax.axis_index("tm")
        barrier = pltpu.get_barrier_semaphore()
        for k in range(1, m):
            p = lax.rem(me + k, m)
            pl.semaphore_signal(barrier, inc=1, device_id=(p, tm), device_id_type=MESH)

        def greet(k, carry):
            p = lax.rem(tm + k, n)
            pl.semaphore_signal(barrier, inc=1, device_id=(me, p), device_id_type=MESH)
            return carry

        lax.fori_loop(1, n, greet, 0)
        pl.semaphore_wait(barrier, (m - 1) + (n - 1))

        def ep_to(p):
            return pltpu.make_async_remote_copy(
                src_ref=src_ref.at[:, :, pl.ds(p * width, width)],
                dst_ref=out_ref.at[:, pl.ds(me * groups, groups), :],
                send_sem=ep_send.at[p],
                recv_sem=ep_recv.at[me],
                device_id=(p, tm),
                device_id_type=MESH,
            )

        def ep_from(p):
            return pltpu.make_async_remote_copy(
                src_ref=src_ref.at[:, :, pl.ds(me * width, width)],
                dst_ref=out_ref.at[:, pl.ds(p * groups, groups), :],
                send_sem=ep_send.at[p],
                recv_sem=ep_recv.at[p],
                device_id=(p, tm),
                device_id_type=MESH,
            )

        for k in range(1, m):
            ep_to(lax.rem(me + k, m)).start()
        local = pltpu.make_async_copy(
            src_ref.at[:, :, pl.ds(me * width, width)],
            out_ref.at[:, pl.ds(me * groups, groups), :],
            local_sem.at[0],
        )
        local.start()

        histogram(leaf_ref, grad_ref, hess_ref, mine)
        staged = pltpu.make_async_copy(mine, held.at[tm], local_sem.at[1])
        staged.start()
        staged.wait()

        def tm_to(p):
            return pltpu.make_async_remote_copy(
                src_ref=held.at[tm],
                dst_ref=held.at[tm],
                send_sem=tm_send.at[p],
                recv_sem=tm_recv.at[tm],
                device_id=(me, p),
                device_id_type=MESH,
            )

        def tm_from(p):
            return pltpu.make_async_remote_copy(
                src_ref=held.at[tm],
                dst_ref=held.at[p],
                send_sem=tm_send.at[p],
                recv_sem=tm_recv.at[p],
                device_id=(me, p),
                device_id_type=MESH,
            )

        def send(k, carry):
            tm_to(lax.rem(tm + k, n)).start()
            return carry

        lax.fori_loop(1, n, send, 0)

        def wait(k, carry):
            p = lax.rem(tm + k, n)
            tm_to(p).wait_send()
            tm_from(p).wait_recv()
            return carry

        lax.fori_loop(1, n, wait, 0)

        def add(k, total):
            return total + held[lax.rem(tm + k, n)]

        totals = lax.fori_loop(1, n, add, held[tm])
        lane = lax.broadcasted_iota(jnp.int32, (groups, 2 * leaves), 1)
        hsum = pltpu.roll(totals, leaves, 1)
        table = jnp.where(lane < leaves, -totals / (hsum + 1.0), 0.0)
        weights_ref[...] = table[:, :leaves]

        mine[...] = table

        def one_tile(t, carry):
            rows = pl.ds(pl.multiple_of(t * 8, 8), 8)
            row = mine[rows, :]

            def one(step, carry):
                cols = pl.ds(pl.multiple_of(step * 128, 128), 128)
                picked = jnp.take_along_axis(
                    row, leaf_ref[rows, cols], axis=1, mode="promise_in_bounds"
                )
                new_ref[rows, cols] = pred_ref[rows, cols] + picked
                return carry

            lax.fori_loop(0, length // 128, one, 0, unroll=8)
            return carry

        lax.fori_loop(0, tiles, one_tile, 0)

        local.wait()
        for k in range(1, m):
            p = lax.rem(me + k, m)
            ep_to(p).wait_send()
            ep_from(p).wait_recv()

    vmem = pl.BlockSpec(memory_space=pltpu.VMEM)
    grad_hess, leaf_weights, new_pred = pl.pallas_call(
        kernel,
        out_shape=(
            jax.ShapeDtypeStruct((two, groups * m, width), stacked.dtype),
            jax.ShapeDtypeStruct((groups, leaves), jnp.float32),
            jax.ShapeDtypeStruct((groups, length), jnp.float32),
        ),
        in_specs=[pl.BlockSpec(memory_space=pl.ANY), vmem, vmem, vmem, vmem],
        out_specs=(pl.BlockSpec(memory_space=pl.ANY), vmem, vmem),
        scratch_shapes=[
            pltpu.VMEM((groups, 2 * leaves), jnp.float32),
            pltpu.VMEM((n, groups, 2 * leaves), jnp.float32),
            pltpu.SemaphoreType.DMA((m,)),
            pltpu.SemaphoreType.DMA((m,)),
            pltpu.SemaphoreType.DMA((n,)),
            pltpu.SemaphoreType.DMA((n,)),
            pltpu.SemaphoreType.DMA((2,)),
        ],
        compiler_params=pltpu.CompilerParams(
            collective_id=cid, has_side_effects=True, vmem_limit_bytes=60 * 1024 * 1024
        ),
    )(stacked, leaf_index, gradient, hessian, predictions)
    return grad_hess, leaf_weights, new_pred


def tm_exchange(payload, held, send_sem, recv_sem, stage_sem, ep, me, n):
    staged = pltpu.make_async_copy(payload, held.at[me], stage_sem)
    staged.start()
    staged.wait()

    def copy_to(p):
        return pltpu.make_async_remote_copy(
            src_ref=held.at[me],
            dst_ref=held.at[me],
            send_sem=send_sem.at[p],
            recv_sem=recv_sem.at[me],
            device_id=(ep, p),
            device_id_type=MESH,
        )

    def copy_from(p):
        return pltpu.make_async_remote_copy(
            src_ref=held.at[me],
            dst_ref=held.at[p],
            send_sem=send_sem.at[p],
            recv_sem=recv_sem.at[p],
            device_id=(ep, p),
            device_id_type=MESH,
        )

    def send(k, carry):
        copy_to(lax.rem(me + k, n)).start()
        return carry

    lax.fori_loop(1, n, send, 0)

    def wait(k, carry):
        p = lax.rem(me + k, n)
        copy_to(p).wait_send()
        copy_from(p).wait_recv()
        return carry

    lax.fori_loop(1, n, wait, 0)


def scan_lanes(x, from_end):
    lane = lax.broadcasted_iota(jnp.int32, x.shape, 1)
    k = 1
    while k < 128:
        if from_end:
            moved = pltpu.roll(x, 128 - k, 1)
            x = x + jnp.where(lane < 128 - k, moved, 0.0)
        else:
            moved = pltpu.roll(x, k, 1)
            x = x + jnp.where(lane >= k, moved, 0.0)
        k *= 2
    return x


def front(predictions, events, first_rows, last_rows):
    n = lax.axis_size("tm")
    groups, length = predictions.shape
    tiles = groups // 8
    blocks = length // 128
    span = math.gcd(blocks, 16)
    groups_n = blocks // span

    def kernel(pred_ref, ev_ref, first_ref, last_ref,
               grad_ref, hess_ref, both_ref,
               weight, one, two, pay_a, held_a, pay_b, held_b,
               send_a, recv_a, send_b, recv_b, stage):
        me = lax.axis_index("tm")
        ep = lax.axis_index("ep")
        barrier = pltpu.get_barrier_semaphore()

        def greet(k, carry):
            p = lax.rem(me + k, n)
            pl.semaphore_signal(barrier, inc=1, device_id=(ep, p), device_id_type=MESH)
            return carry

        lax.fori_loop(1, n, greet, 0)
        pl.semaphore_wait(barrier, n - 1)

        lane_j = lax.broadcasted_iota(jnp.int32, (128, 128), 0)
        lane_i = lax.broadcasted_iota(jnp.int32, (128, 128), 1)
        upper = (lane_j >= lane_i).astype(jnp.bfloat16)
        lower = (lane_j <= lane_i).astype(jnp.bfloat16)

        def run_sum(x, matrix):
            hi = x.astype(jnp.bfloat16)
            rest = x - hi.astype(jnp.float32)
            mid = rest.astype(jnp.bfloat16)
            lo = (rest - mid.astype(jnp.float32)).astype(jnp.bfloat16)
            out = jnp.dot(hi, matrix, preferred_element_type=jnp.float32)
            out = out + jnp.dot(mid, matrix, preferred_element_type=jnp.float32)
            return out + jnp.dot(lo, matrix, preferred_element_type=jnp.float32)

        def block_cols(b):
            return pl.ds(pl.multiple_of(b * 128, 128), 128)

        def suffix_group(j, carries):
            b0 = (groups_n - 1 - j) * span
            idx = first_ref[pl.ds(pl.multiple_of(b0 * 8, 8), 8 * span), :]
            out = []
            for t in range(tiles):
                rows = pl.ds(t * 8, 8)
                later = carries[t]
                pieces = []
                for k in range(span):
                    w = jnp.exp(pred_ref[rows, block_cols(b0 + k)])
                    weight[rows, block_cols(b0 + k)] = w
                    pieces.append(w)
                s = run_sum(jnp.concatenate(pieces, axis=0), upper)
                r = jnp.take_along_axis(s, idx, axis=1, mode="promise_in_bounds")
                for k in reversed(range(span)):
                    one[rows, block_cols(b0 + k)] = r[8 * k:8 * k + 8] + later
                    later = later + jnp.broadcast_to(s[8 * k:8 * k + 8, 0:1], (8, 128))
                out.append(later)
            return tuple(out)

        zero = jnp.zeros((8, 128), jnp.float32)
        totals = lax.fori_loop(0, groups_n, suffix_group, (zero,) * tiles)
        for t in range(tiles):
            pay_a[pl.ds(t * 8, 8), :] = totals[t]
        tm_exchange(pay_a, held_a, send_a, recv_a, stage.at[0], ep, me, n)

        def add_later(k, total):
            p = lax.rem(me + k, n)
            return total + jnp.where(p > me, held_a[p], 0.0)

        pay_a[...] = lax.fori_loop(1, n, add_later, jnp.zeros((groups, 128), jnp.float32))

        def prefix_group(j, carries):
            b0 = j * span
            idx = last_ref[pl.ds(pl.multiple_of(b0 * 8, 8), 8 * span), :]
            idx = jnp.concatenate([idx, idx], axis=0)
            half = 8 * span
            out = []
            for t in range(tiles):
                rows = pl.ds(t * 8, 8)
                later = pay_a[rows, :]
                c1, c2 = carries[2 * t], carries[2 * t + 1]
                firsts, seconds = [], []
                for k in range(span):
                    risk = one[rows, block_cols(b0 + k)] + later
                    observed = ev_ref[rows, block_cols(b0 + k)].astype(jnp.float32)
                    inv_one = observed / risk
                    firsts.append(inv_one)
                    seconds.append(inv_one / risk)
                s = run_sum(jnp.concatenate(firsts + seconds, axis=0), lower)
                r = jnp.take_along_axis(s, idx, axis=1, mode="promise_in_bounds")
                for k in range(span):
                    one[rows, block_cols(b0 + k)] = r[8 * k:8 * k + 8] + c1
                    two[rows, block_cols(b0 + k)] = r[half + 8 * k:half + 8 * k + 8] + c2
                    c1 = c1 + jnp.broadcast_to(s[8 * k:8 * k + 8, 127:128], (8, 128))
                    c2 = c2 + jnp.broadcast_to(s[half + 8 * k:half + 8 * k + 8, 127:128], (8, 128))
                out += [c1, c2]
            return tuple(out)

        sums = lax.fori_loop(0, groups_n, prefix_group, (zero,) * (2 * tiles))
        for t in range(tiles):
            pay_b[pl.ds(t * 8, 8), :] = sums[2 * t]
            pay_b[pl.ds(groups + t * 8, 8), :] = sums[2 * t + 1]
        tm_exchange(pay_b, held_b, send_b, recv_b, stage.at[1], ep, me, n)

        def add_earlier(k, total):
            p = lax.rem(me + k, n)
            return total + jnp.where(p < me, held_b[p], 0.0)

        pay_b[...] = lax.fori_loop(1, n, add_earlier, jnp.zeros((2 * groups, 128), jnp.float32))

        def out_tile(t, carry):
            rows = pl.ds(pl.multiple_of(t * 8, 8), 8)
            e1 = jnp.tile(pay_b[rows, :], (1, span))
            e2 = jnp.tile(pay_b[pl.ds(pl.multiple_of(groups + t * 8, 8), 8), :], (1, span))

            def one_group(j, carry):
                cols = pl.ds(pl.multiple_of(j * span * 128, span * 128), span * 128)
                w = weight[rows, cols]
                a1 = one[rows, cols] + e1
                a2 = two[rows, cols] + e2
                observed = ev_ref[rows, cols].astype(jnp.float32)
                g = w * a1 - observed
                h = w * a1 - w * w * a2
                grad_ref[rows, cols] = g
                hess_ref[rows, cols] = h
                both_ref[0, rows, cols] = g.astype(jnp.bfloat16)
                both_ref[1, rows, cols] = h.astype(jnp.bfloat16)
                return carry

            lax.fori_loop(0, groups_n, one_group, 0)
            return carry

        lax.fori_loop(0, tiles, out_tile, 0)

    vmem = pl.BlockSpec(memory_space=pltpu.VMEM)
    return pl.pallas_call(
        kernel,
        out_shape=(
            jax.ShapeDtypeStruct((groups, length), jnp.float32),
            jax.ShapeDtypeStruct((groups, length), jnp.float32),
            jax.ShapeDtypeStruct((2, groups, length), jnp.bfloat16),
        ),
        in_specs=[vmem, vmem, vmem, vmem],
        out_specs=(vmem, vmem, vmem),
        scratch_shapes=[
            pltpu.VMEM((groups, length), jnp.float32),
            pltpu.VMEM((groups, length), jnp.float32),
            pltpu.VMEM((groups, length), jnp.float32),
            pltpu.VMEM((groups, 128), jnp.float32),
            pltpu.VMEM((n, groups, 128), jnp.float32),
            pltpu.VMEM((2 * groups, 128), jnp.float32),
            pltpu.VMEM((n, 2 * groups, 128), jnp.float32),
            pltpu.SemaphoreType.DMA((n,)),
            pltpu.SemaphoreType.DMA((n,)),
            pltpu.SemaphoreType.DMA((n,)),
            pltpu.SemaphoreType.DMA((n,)),
            pltpu.SemaphoreType.DMA((2,)),
        ],
        compiler_params=pltpu.CompilerParams(
            collective_id=0, has_side_effects=True, vmem_limit_bytes=60 * 1024 * 1024
        ),
    )(predictions, events, first_rows, last_rows)


def tie_rows(tie_start):
    length = tie_start.shape[0]
    blocks = length // 128
    starts = tie_start.reshape(blocks, 128)
    labels = jnp.arange(128, dtype=jnp.int32)
    first_local = lax.cummax(jnp.where(starts == 1, labels[None, :], 0), axis=1)
    next_start = jnp.concatenate([starts[:, 1:], jnp.ones((blocks, 1), jnp.int32)], axis=1)
    last_local = lax.cummin(jnp.where(next_start == 1, labels[None, :], 127), axis=1, reverse=True)

    def spread(rows):
        return jnp.broadcast_to(rows[:, None, :], (blocks, 8, 128)).reshape(blocks * 8, 128)

    return spread(first_local), spread(last_local)


def lane_pad(vectors):
    width = vectors.shape[1]
    return jnp.pad(vectors, ((0, 0), (0, 128 - width)))


def tile_matrices(tie_start):
    length = tie_start.shape[0]
    blocks = length // 128
    starts = tie_start.reshape(blocks, 128)
    labels = jnp.arange(128, dtype=jnp.int32)
    first_local = lax.cummax(jnp.where(starts == 1, labels[None, :], 0), axis=1)
    next_start = jnp.concatenate([starts[:, 1:], jnp.ones((blocks, 1), jnp.int32)], axis=1)
    last_local = lax.cummin(jnp.where(next_start == 1, labels[None, :], 127), axis=1, reverse=True)
    backward = (labels[None, :, None] >= first_local[:, None, :]).astype(jnp.float32)
    forward = (labels[None, :, None] <= last_local[:, None, :]).astype(jnp.float32)
    return (backward, forward)


def block_cumsum(values, matrices, from_end):
    groups = values.shape[0]
    length = values.shape[1]
    blocks = length // 128
    shaped = values.reshape(groups, blocks, 128)
    within = jnp.einsum("ebj,bji->ebi", shaped, matrices, precision=lax.Precision.HIGH)
    totals = jnp.sum(shaped, axis=2)
    if from_end:
        offsets = jnp.cumsum(totals[:, ::-1], axis=1)[:, ::-1] - totals
    else:
        offsets = jnp.cumsum(totals, axis=1) - totals
    return (within + offsets[:, :, None]).reshape(groups, length)


def leaf_update(predictions, leaf_index, table):
    groups, length = leaf_index.shape
    tiles = groups // 8
    table = lane_pad(table)

    def kernel(table_ref, pred_ref, leaf_ref, out_ref):
        row = table_ref[...]

        def one(step, carry):
            cols = pl.ds(pl.multiple_of(step * 128, 128), 128)
            picked = jnp.take_along_axis(row, leaf_ref[:, cols], axis=1, mode="promise_in_bounds")
            out_ref[:, cols] = pred_ref[:, cols] + picked
            return carry

        lax.fori_loop(0, length // 128, one, 0, unroll=8)

    spec = pl.BlockSpec((8, length), lambda t: (t, 0))
    return pl.pallas_call(
        kernel,
        grid=(tiles,),
        out_shape=jax.ShapeDtypeStruct((groups, length), jnp.float32),
        in_specs=[pl.BlockSpec((8, 128), lambda t: (t, 0)), spec, spec],
        out_specs=spec,
    )(table, predictions, leaf_index)


def on_device(predictions, leaf_index, events, tie_start):
    first_rows, last_rows = tie_rows(tie_start)
    gradient, hessian, stacked = front(predictions, events, first_rows, last_rows)
    grad_hess, leaf_weights, new_pred = finish(
        stacked, leaf_index, gradient, hessian, predictions, LEAVES, 2
    )
    grad_hess = grad_hess.reshape(2, grad_hess.shape[1], 1, grad_hess.shape[2])
    return (new_pred, leaf_weights, grad_hess)


def solution(mesh):
    placed = (P("ep", "tm"), P("ep", "tm"), P("ep", "tm"), P("tm"))
    return jax.shard_map(
        on_device,
        mesh=mesh,
        in_specs=placed,
        out_specs=(P("ep", "tm"), P("ep", None), P(None, None, "tm", "ep")),
        check_vma=False,
    )
```

```python
import math

import jax
import jax.numpy as jnp
from jax import lax
from jax.experimental import pallas as pl
from jax.experimental.pallas import tpu as pltpu
from jax.sharding import PartitionSpec as P

LEAVES = 64
MESH = pl.DeviceIdType.MESH


def tm_combine(part, mode, cid):
    n = lax.axis_size("tm")
    rows = part.shape[0]

    def kernel(x_ref, out_ref, held, send_sem, recv_sem):
        me = lax.axis_index("tm")
        ep = lax.axis_index("ep")
        barrier = pltpu.get_barrier_semaphore()

        def greet(k, carry):
            p = lax.rem(me + k, n)
            pl.semaphore_signal(barrier, inc=1, device_id=(ep, p), device_id_type=MESH)
            return carry

        lax.fori_loop(1, n, greet, 0)
        pl.semaphore_wait(barrier, n - 1)

        def copy_to(p):
            return pltpu.make_async_remote_copy(
                src_ref=x_ref,
                dst_ref=held.at[me],
                send_sem=send_sem.at[p],
                recv_sem=recv_sem.at[me],
                device_id=(ep, p),
                device_id_type=MESH,
            )

        def copy_from(p):
            return pltpu.make_async_remote_copy(
                src_ref=x_ref,
                dst_ref=held.at[p],
                send_sem=send_sem.at[p],
                recv_sem=recv_sem.at[p],
                device_id=(ep, p),
                device_id_type=MESH,
            )

        def send(k, carry):
            copy_to(lax.rem(me + k, n)).start()
            return carry

        lax.fori_loop(1, n, send, 0)

        def wait(k, carry):
            p = lax.rem(me + k, n)
            copy_to(p).wait_send()
            copy_from(p).wait_recv()
            return carry

        lax.fori_loop(1, n, wait, 0)

        if mode == "all":
            total = x_ref[...]
        else:
            total = jnp.zeros((rows, 128), jnp.float32)

        def add(k, total):
            p = lax.rem(me + k, n)
            if mode == "all":
                keep = True
            elif mode == "later":
                keep = p > me
            else:
                keep = p < me
            return total + jnp.where(keep, held[p], 0.0)

        out_ref[...] = lax.fori_loop(1, n, add, total)

    return pl.pallas_call(
        kernel,
        out_shape=jax.ShapeDtypeStruct((rows, 128), jnp.float32),
        in_specs=[pl.BlockSpec(memory_space=pltpu.VMEM)],
        out_specs=pl.BlockSpec(memory_space=pltpu.VMEM),
        scratch_shapes=[
            pltpu.VMEM((n, rows, 128), jnp.float32),
            pltpu.SemaphoreType.DMA((n,)),
            pltpu.SemaphoreType.DMA((n,)),
        ],
        compiler_params=pltpu.CompilerParams(collective_id=cid, has_side_effects=True),
    )(part)


def exchange_and_sum(stacked, leaf_index, gradient, hessian, leaves, cid):
    m = lax.axis_size("ep")
    two, groups, length = stacked.shape
    width = length // m
    tiles = groups // 8
    side = leaves // 8
    chunk = math.gcd(length, 4096)
    cols_all = side * 4 * 8

    def histogram(leaf_ref, grad_ref, hess_ref, sums_ref):
        row_id = lax.broadcasted_iota(jnp.int32, (side * 8, cols_all), 0)
        col_id = lax.broadcasted_iota(jnp.int32, (side * 8, cols_all), 1)
        diagonal = lax.rem(row_id, 8) == lax.rem(col_id, 8)
        fold = (
            lax.broadcasted_iota(jnp.int32, (cols_all, side * 4), 0) // 8
            == lax.broadcasted_iota(jnp.int32, (cols_all, side * 4), 1)
        ).astype(jnp.float32)

        def one_tile(t, carry):
            rows = pl.ds(pl.multiple_of(t * 8, 8), 8)

            def one_chunk(step, total):
                cols = pl.ds(pl.multiple_of(step * chunk, chunk), chunk)
                leaf = leaf_ref[rows, cols]
                grad = grad_ref[rows, cols]
                hess = hess_ref[rows, cols]
                high = lax.shift_right_logical(leaf, 3)
                low = jnp.bitwise_and(leaf, 7)
                grad_hi = grad.astype(jnp.bfloat16).astype(jnp.float32)
                hess_hi = hess.astype(jnp.bfloat16).astype(jnp.float32)
                values = (grad_hi, grad - grad_hi, hess_hi, hess - hess_hi)
                ones = jnp.concatenate(
                    [jnp.where(high == a, 1.0, 0.0) for a in range(side)], axis=0
                ).astype(jnp.bfloat16)
                pieces = []
                for b in range(side):
                    hit = low == b
                    for value in values:
                        pieces.append(jnp.where(hit, value, 0.0))
                parts = jnp.concatenate(pieces, axis=0).astype(jnp.bfloat16)
                return total + lax.dot_general(
                    ones, parts, (((1,), (1,)), ((), ())), preferred_element_type=jnp.float32
                )

            total = jnp.zeros((side * 8, cols_all), jnp.float32)
            total = lax.fori_loop(0, length // chunk, one_chunk, total)
            total = jnp.where(diagonal, total, 0.0)
            sums_ref[t] = jnp.dot(
                total, fold, precision=lax.Precision.HIGHEST, preferred_element_type=jnp.float32
            )
            return carry

        lax.fori_loop(0, tiles, one_tile, 0)

    def kernel(src_ref, leaf_ref, grad_ref, hess_ref, out_ref, sums_ref, send_sem, recv_sem, local_sem):
        me = lax.axis_index("ep")
        tm = lax.axis_index("tm")
        barrier = pltpu.get_barrier_semaphore()
        for k in range(1, m):
            p = lax.rem(me + k, m)
            pl.semaphore_signal(barrier, inc=1, device_id=(p, tm), device_id_type=MESH)
        pl.semaphore_wait(barrier, m - 1)

        def copy_to(p):
            return pltpu.make_async_remote_copy(
                src_ref=src_ref.at[:, :, pl.ds(p * width, width)],
                dst_ref=out_ref.at[:, pl.ds(me * groups, groups), :],
                send_sem=send_sem.at[p],
                recv_sem=recv_sem.at[me],
                device_id=(p, tm),
                device_id_type=MESH,
            )

        def copy_from(p):
            return pltpu.make_async_remote_copy(
                src_ref=src_ref.at[:, :, pl.ds(me * width, width)],
                dst_ref=out_ref.at[:, pl.ds(p * groups, groups), :],
                send_sem=send_sem.at[p],
                recv_sem=recv_sem.at[p],
                device_id=(p, tm),
                device_id_type=MESH,
            )

        for k in range(1, m):
            copy_to(lax.rem(me + k, m)).start()
        local = pltpu.make_async_copy(
            src_ref.at[:, :, pl.ds(me * width, width)],
            out_ref.at[:, pl.ds(me * groups, groups), :],
            local_sem.at[0],
        )
        local.start()
        histogram(leaf_ref, grad_ref, hess_ref, sums_ref)
        local.wait()
        for k in range(1, m):
            p = lax.rem(me + k, m)
            copy_to(p).wait_send()
            copy_from(p).wait_recv()

    vmem = pl.BlockSpec(memory_space=pltpu.VMEM)
    grad_hess, sums = pl.pallas_call(
        kernel,
        out_shape=(
            jax.ShapeDtypeStruct((two, groups * m, width), stacked.dtype),
            jax.ShapeDtypeStruct((tiles, side * 8, side * 4), jnp.float32),
        ),
        in_specs=[pl.BlockSpec(memory_space=pl.ANY), vmem, vmem, vmem],
        out_specs=(pl.BlockSpec(memory_space=pl.ANY), vmem),
        scratch_shapes=[
            pltpu.SemaphoreType.DMA((m,)),
            pltpu.SemaphoreType.DMA((m,)),
            pltpu.SemaphoreType.DMA((1,)),
        ],
        compiler_params=pltpu.CompilerParams(collective_id=cid, has_side_effects=True),
    )(stacked, leaf_index, gradient, hessian)
    sums = sums.reshape(tiles, side, 8, side, 4).transpose(0, 2, 1, 3, 4)
    sums = sums.reshape(groups, leaves, 4)
    gsum = sums[:, :, 0] + sums[:, :, 1]
    hsum = sums[:, :, 2] + sums[:, :, 3]
    return grad_hess, jnp.stack([gsum, hsum], axis=1)


def finish(stacked, leaf_index, gradient, hessian, predictions, leaves, cid):
    m = lax.axis_size("ep")
    n = lax.axis_size("tm")
    two, groups, length = stacked.shape
    width = length // m
    tiles = groups // 8
    side = leaves // 8
    chunk = math.gcd(length, 4096)
    cols_all = side * 4 * 8

    def histogram(leaf_ref, grad_ref, hess_ref, mine):
        row_id = lax.broadcasted_iota(jnp.int32, (side * 8, cols_all), 0)
        col_id = lax.broadcasted_iota(jnp.int32, (side * 8, cols_all), 1)
        diagonal = lax.rem(row_id, 8) == lax.rem(col_id, 8)
        src = lax.broadcasted_iota(jnp.int32, (cols_all, 2 * leaves), 0)
        dst = lax.broadcasted_iota(jnp.int32, (cols_all, 2 * leaves), 1)
        src_b = src // 32
        src_c = lax.rem(src // 8, 4)

        def one_tile(t, carry):
            rows = pl.ds(pl.multiple_of(t * 8, 8), 8)

            def one_chunk(step, total):
                cols = pl.ds(pl.multiple_of(step * chunk, chunk), chunk)
                leaf = leaf_ref[rows, cols]
                grad = grad_ref[rows, cols]
                hess = hess_ref[rows, cols]
                high = lax.shift_right_logical(leaf, 3)
                low = jnp.bitwise_and(leaf, 7)
                grad_hi = grad.astype(jnp.bfloat16).astype(jnp.float32)
                hess_hi = hess.astype(jnp.bfloat16).astype(jnp.float32)
                values = (grad_hi, grad - grad_hi, hess_hi, hess - hess_hi)
                ones = jnp.concatenate(
                    [jnp.where(high == a, 1.0, 0.0) for a in range(side)], axis=0
                ).astype(jnp.bfloat16)
                pieces = []
                for b in range(side):
                    hit = low == b
                    for value in values:
                        pieces.append(jnp.where(hit, value, 0.0))
                parts = jnp.concatenate(pieces, axis=0).astype(jnp.bfloat16)
                return total + lax.dot_general(
                    ones, parts, (((1,), (1,)), ((), ())), preferred_element_type=jnp.float32
                )

            total = jnp.zeros((side * 8, cols_all), jnp.float32)
            total = lax.fori_loop(0, length // chunk, one_chunk, total)
            total = jnp.where(diagonal, total, 0.0)
            out = jnp.zeros((8, 2 * leaves), jnp.float32)
            for a in range(side):
                fold = (dst == (src_c // 2) * leaves + a * side + src_b).astype(jnp.float32)
                out = out + jnp.dot(
                    total[a * 8:(a + 1) * 8, :], fold,
                    precision=lax.Precision.HIGHEST, preferred_element_type=jnp.float32,
                )
            mine[rows, :] = out
            return carry

        lax.fori_loop(0, tiles, one_tile, 0)

    def kernel(src_ref, leaf_ref, grad_ref, hess_ref, pred_ref,
               out_ref, weights_ref, new_ref,
               mine, held, ep_send, ep_recv, tm_send, tm_recv, local_sem):
        me = lax.axis_index("ep")
        tm = lax.axis_index("tm")
        barrier = pltpu.get_barrier_semaphore()
        for k in range(1, m):
            p = lax.rem(me + k, m)
            pl.semaphore_signal(barrier, inc=1, device_id=(p, tm), device_id_type=MESH)

        def greet(k, carry):
            p = lax.rem(tm + k, n)
            pl.semaphore_signal(barrier, inc=1, device_id=(me, p), device_id_type=MESH)
            return carry

        lax.fori_loop(1, n, greet, 0)
        pl.semaphore_wait(barrier, (m - 1) + (n - 1))

        def ep_to(p):
            return pltpu.make_async_remote_copy(
                src_ref=src_ref.at[:, :, pl.ds(p * width, width)],
                dst_ref=out_ref.at[:, pl.ds(me * groups, groups), :],
                send_sem=ep_send.at[p],
                recv_sem=ep_recv.at[me],
                device_id=(p, tm),
                device_id_type=MESH,
            )

        def ep_from(p):
            return pltpu.make_async_remote_copy(
                src_ref=src_ref.at[:, :, pl.ds(me * width, width)],
                dst_ref=out_ref.at[:, pl.ds(p * groups, groups), :],
                send_sem=ep_send.at[p],
                recv_sem=ep_recv.at[p],
                device_id=(p, tm),
                device_id_type=MESH,
            )

        for k in range(1, m):
            ep_to(lax.rem(me + k, m)).start()
        local = pltpu.make_async_copy(
            src_ref.at[:, :, pl.ds(me * width, width)],
            out_ref.at[:, pl.ds(me * groups, groups), :],
            local_sem.at[0],
        )
        local.start()

        histogram(leaf_ref, grad_ref, hess_ref, mine)
        staged = pltpu.make_async_copy(mine, held.at[tm], local_sem.at[1])
        staged.start()
        staged.wait()

        def tm_to(p):
            return pltpu.make_async_remote_copy(
                src_ref=held.at[tm],
                dst_ref=held.at[tm],
                send_sem=tm_send.at[p],
                recv_sem=tm_recv.at[tm],
                device_id=(me, p),
                device_id_type=MESH,
            )

        def tm_from(p):
            return pltpu.make_async_remote_copy(
                src_ref=held.at[tm],
                dst_ref=held.at[p],
                send_sem=tm_send.at[p],
                recv_sem=tm_recv.at[p],
                device_id=(me, p),
                device_id_type=MESH,
            )

        def send(k, carry):
            tm_to(lax.rem(tm + k, n)).start()
            return carry

        lax.fori_loop(1, n, send, 0)

        def wait(k, carry):
            p = lax.rem(tm + k, n)
            tm_to(p).wait_send()
            tm_from(p).wait_recv()
            return carry

        lax.fori_loop(1, n, wait, 0)

        def add(k, total):
            return total + held[lax.rem(tm + k, n)]

        totals = lax.fori_loop(1, n, add, held[tm])
        lane = lax.broadcasted_iota(jnp.int32, (groups, 2 * leaves), 1)
        hsum = pltpu.roll(totals, leaves, 1)
        table = jnp.where(lane < leaves, -totals / (hsum + 1.0), 0.0)
        weights_ref[...] = table[:, :leaves]

        mine[...] = table

        def one_tile(t, carry):
            rows = pl.ds(pl.multiple_of(t * 8, 8), 8)
            row = mine[rows, :]

            def one(step, carry):
                cols = pl.ds(pl.multiple_of(step * 128, 128), 128)
                picked = jnp.take_along_axis(
                    row, leaf_ref[rows, cols], axis=1, mode="promise_in_bounds"
                )
                new_ref[rows, cols] = pred_ref[rows, cols] + picked
                return carry

            lax.fori_loop(0, length // 128, one, 0, unroll=8)
            return carry

        lax.fori_loop(0, tiles, one_tile, 0)

        local.wait()
        for k in range(1, m):
            p = lax.rem(me + k, m)
            ep_to(p).wait_send()
            ep_from(p).wait_recv()

    vmem = pl.BlockSpec(memory_space=pltpu.VMEM)
    grad_hess, leaf_weights, new_pred = pl.pallas_call(
        kernel,
        out_shape=(
            jax.ShapeDtypeStruct((two, groups * m, width), stacked.dtype),
            jax.ShapeDtypeStruct((groups, leaves), jnp.float32),
            jax.ShapeDtypeStruct((groups, length), jnp.float32),
        ),
        in_specs=[pl.BlockSpec(memory_space=pl.ANY), vmem, vmem, vmem, vmem],
        out_specs=(pl.BlockSpec(memory_space=pl.ANY), vmem, vmem),
        scratch_shapes=[
            pltpu.VMEM((groups, 2 * leaves), jnp.float32),
            pltpu.VMEM((n, groups, 2 * leaves), jnp.float32),
            pltpu.SemaphoreType.DMA((m,)),
            pltpu.SemaphoreType.DMA((m,)),
            pltpu.SemaphoreType.DMA((n,)),
            pltpu.SemaphoreType.DMA((n,)),
            pltpu.SemaphoreType.DMA((2,)),
        ],
        compiler_params=pltpu.CompilerParams(
            collective_id=cid, has_side_effects=True, vmem_limit_bytes=60 * 1024 * 1024
        ),
    )(stacked, leaf_index, gradient, hessian, predictions)
    return grad_hess, leaf_weights, new_pred


def tm_exchange(payload, held, send_sem, recv_sem, stage_sem, ep, me, n):
    staged = pltpu.make_async_copy(payload, held.at[me], stage_sem)
    staged.start()
    staged.wait()

    def copy_to(p):
        return pltpu.make_async_remote_copy(
            src_ref=held.at[me],
            dst_ref=held.at[me],
            send_sem=send_sem.at[p],
            recv_sem=recv_sem.at[me],
            device_id=(ep, p),
            device_id_type=MESH,
        )

    def copy_from(p):
        return pltpu.make_async_remote_copy(
            src_ref=held.at[me],
            dst_ref=held.at[p],
            send_sem=send_sem.at[p],
            recv_sem=recv_sem.at[p],
            device_id=(ep, p),
            device_id_type=MESH,
        )

    def send(k, carry):
        copy_to(lax.rem(me + k, n)).start()
        return carry

    lax.fori_loop(1, n, send, 0)

    def wait(k, carry):
        p = lax.rem(me + k, n)
        copy_to(p).wait_send()
        copy_from(p).wait_recv()
        return carry

    lax.fori_loop(1, n, wait, 0)


def scan_lanes(x, from_end):
    lane = lax.broadcasted_iota(jnp.int32, x.shape, 1)
    k = 1
    while k < 128:
        if from_end:
            moved = pltpu.roll(x, 128 - k, 1)
            x = x + jnp.where(lane < 128 - k, moved, 0.0)
        else:
            moved = pltpu.roll(x, k, 1)
            x = x + jnp.where(lane >= k, moved, 0.0)
        k *= 2
    return x


def front(predictions, events, first_rows, last_rows):
    n = lax.axis_size("tm")
    groups, length = predictions.shape
    tiles = groups // 8
    blocks = length // 128
    span = math.gcd(blocks, 32)
    groups_n = blocks // span

    def kernel(pred_ref, ev_ref, first_ref, last_ref,
               grad_ref, hess_ref, both_ref,
               weight, one, two, pay_a, held_a, pay_b, held_b,
               send_a, recv_a, send_b, recv_b, stage):
        me = lax.axis_index("tm")
        ep = lax.axis_index("ep")
        barrier = pltpu.get_barrier_semaphore()

        def greet(k, carry):
            p = lax.rem(me + k, n)
            pl.semaphore_signal(barrier, inc=1, device_id=(ep, p), device_id_type=MESH)
            return carry

        lax.fori_loop(1, n, greet, 0)
        pl.semaphore_wait(barrier, n - 1)

        lane_j = lax.broadcasted_iota(jnp.int32, (128, 128), 0)
        lane_i = lax.broadcasted_iota(jnp.int32, (128, 128), 1)
        upper = (lane_j >= lane_i).astype(jnp.bfloat16)
        lower = (lane_j <= lane_i).astype(jnp.bfloat16)

        def run_sum(x, matrix):
            hi = x.astype(jnp.bfloat16)
            rest = x - hi.astype(jnp.float32)
            mid = rest.astype(jnp.bfloat16)
            lo = (rest - mid.astype(jnp.float32)).astype(jnp.bfloat16)
            out = jnp.dot(hi, matrix, preferred_element_type=jnp.float32)
            out = out + jnp.dot(mid, matrix, preferred_element_type=jnp.float32)
            return out + jnp.dot(lo, matrix, preferred_element_type=jnp.float32)

        def block_cols(b):
            return pl.ds(pl.multiple_of(b * 128, 128), 128)

        def suffix_tile(t, carry):
            rows = pl.ds(pl.multiple_of(t * 8, 8), 8)

            def one_group(j, later):
                b0 = (groups_n - 1 - j) * span
                pieces = []
                for k in range(span):
                    w = jnp.exp(pred_ref[rows, block_cols(b0 + k)])
                    weight[rows, block_cols(b0 + k)] = w
                    pieces.append(w)
                s = run_sum(jnp.concatenate(pieces, axis=0), upper)
                idx = first_ref[pl.ds(pl.multiple_of(b0 * 8, 8), 8 * span), :]
                r = jnp.take_along_axis(s, idx, axis=1, mode="promise_in_bounds")
                for k in reversed(range(span)):
                    one[rows, block_cols(b0 + k)] = r[8 * k:8 * k + 8] + later
                    later = later + jnp.broadcast_to(s[8 * k:8 * k + 8, 0:1], (8, 128))
                return later

            total = lax.fori_loop(0, groups_n, one_group, jnp.zeros((8, 128), jnp.float32), unroll=2)
            pay_a[rows, :] = total
            return carry

        lax.fori_loop(0, tiles, suffix_tile, 0)
        tm_exchange(pay_a, held_a, send_a, recv_a, stage.at[0], ep, me, n)

        def add_later(k, total):
            p = lax.rem(me + k, n)
            return total + jnp.where(p > me, held_a[p], 0.0)

        pay_a[...] = lax.fori_loop(1, n, add_later, jnp.zeros((groups, 128), jnp.float32))

        def prefix_tile(t, carry):
            rows = pl.ds(pl.multiple_of(t * 8, 8), 8)
            later = pay_a[rows, :]

            def one_group(j, carries):
                c1, c2 = carries
                b0 = j * span
                firsts, seconds = [], []
                for k in range(span):
                    risk = one[rows, block_cols(b0 + k)] + later
                    observed = ev_ref[rows, block_cols(b0 + k)].astype(jnp.float32)
                    scale = 1.0 / risk
                    inv_one = observed * scale
                    firsts.append(inv_one)
                    seconds.append(inv_one * scale)
                s = run_sum(jnp.concatenate(firsts + seconds, axis=0), lower)
                idx = last_ref[pl.ds(pl.multiple_of(b0 * 8, 8), 8 * span), :]
                idx = jnp.concatenate([idx, idx], axis=0)
                r = jnp.take_along_axis(s, idx, axis=1, mode="promise_in_bounds")
                half = 8 * span
                for k in range(span):
                    one[rows, block_cols(b0 + k)] = r[8 * k:8 * k + 8] + c1
                    two[rows, block_cols(b0 + k)] = r[half + 8 * k:half + 8 * k + 8] + c2
                    c1 = c1 + jnp.broadcast_to(s[8 * k:8 * k + 8, 127:128], (8, 128))
                    c2 = c2 + jnp.broadcast_to(s[half + 8 * k:half + 8 * k + 8, 127:128], (8, 128))
                return (c1, c2)

            zero = jnp.zeros((8, 128), jnp.float32)
            c1, c2 = lax.fori_loop(0, groups_n, one_group, (zero, zero), unroll=2)
            pay_b[rows, :] = c1
            pay_b[pl.ds(pl.multiple_of(groups + t * 8, 8), 8), :] = c2
            return carry

        lax.fori_loop(0, tiles, prefix_tile, 0)
        tm_exchange(pay_b, held_b, send_b, recv_b, stage.at[1], ep, me, n)

        def add_earlier(k, total):
            p = lax.rem(me + k, n)
            return total + jnp.where(p < me, held_b[p], 0.0)

        pay_b[...] = lax.fori_loop(1, n, add_earlier, jnp.zeros((2 * groups, 128), jnp.float32))

        def out_tile(t, carry):
            rows = pl.ds(pl.multiple_of(t * 8, 8), 8)
            e1 = jnp.tile(pay_b[rows, :], (1, span))
            e2 = jnp.tile(pay_b[pl.ds(pl.multiple_of(groups + t * 8, 8), 8), :], (1, span))

            def one_group(j, carry):
                cols = pl.ds(pl.multiple_of(j * span * 128, span * 128), span * 128)
                w = weight[rows, cols]
                a1 = one[rows, cols] + e1
                a2 = two[rows, cols] + e2
                observed = ev_ref[rows, cols].astype(jnp.float32)
                g = w * a1 - observed
                h = w * a1 - w * w * a2
                grad_ref[rows, cols] = g
                hess_ref[rows, cols] = h
                both_ref[0, rows, cols] = g.astype(jnp.bfloat16)
                both_ref[1, rows, cols] = h.astype(jnp.bfloat16)
                return carry

            lax.fori_loop(0, groups_n, one_group, 0)
            return carry

        lax.fori_loop(0, tiles, out_tile, 0)

    vmem = pl.BlockSpec(memory_space=pltpu.VMEM)
    return pl.pallas_call(
        kernel,
        out_shape=(
            jax.ShapeDtypeStruct((groups, length), jnp.float32),
            jax.ShapeDtypeStruct((groups, length), jnp.float32),
            jax.ShapeDtypeStruct((2, groups, length), jnp.bfloat16),
        ),
        in_specs=[vmem, vmem, vmem, vmem],
        out_specs=(vmem, vmem, vmem),
        scratch_shapes=[
            pltpu.VMEM((groups, length), jnp.float32),
            pltpu.VMEM((groups, length), jnp.float32),
            pltpu.VMEM((groups, length), jnp.float32),
            pltpu.VMEM((groups, 128), jnp.float32),
            pltpu.VMEM((n, groups, 128), jnp.float32),
            pltpu.VMEM((2 * groups, 128), jnp.float32),
            pltpu.VMEM((n, 2 * groups, 128), jnp.float32),
            pltpu.SemaphoreType.DMA((n,)),
            pltpu.SemaphoreType.DMA((n,)),
            pltpu.SemaphoreType.DMA((n,)),
            pltpu.SemaphoreType.DMA((n,)),
            pltpu.SemaphoreType.DMA((2,)),
        ],
        compiler_params=pltpu.CompilerParams(
            collective_id=0, has_side_effects=True, vmem_limit_bytes=60 * 1024 * 1024
        ),
    )(predictions, events, first_rows, last_rows)


def tie_rows(tie_start):
    length = tie_start.shape[0]
    blocks = length // 128
    starts = tie_start.reshape(blocks, 128)
    labels = jnp.arange(128, dtype=jnp.int32)
    first_local = lax.cummax(jnp.where(starts == 1, labels[None, :], 0), axis=1)
    next_start = jnp.concatenate([starts[:, 1:], jnp.ones((blocks, 1), jnp.int32)], axis=1)
    last_local = lax.cummin(jnp.where(next_start == 1, labels[None, :], 127), axis=1, reverse=True)

    def spread(rows):
        return jnp.broadcast_to(rows[:, None, :], (blocks, 8, 128)).reshape(blocks * 8, 128)

    return spread(first_local), spread(last_local)


def lane_pad(vectors):
    width = vectors.shape[1]
    return jnp.pad(vectors, ((0, 0), (0, 128 - width)))


def tile_matrices(tie_start):
    length = tie_start.shape[0]
    blocks = length // 128
    starts = tie_start.reshape(blocks, 128)
    labels = jnp.arange(128, dtype=jnp.int32)
    first_local = lax.cummax(jnp.where(starts == 1, labels[None, :], 0), axis=1)
    next_start = jnp.concatenate([starts[:, 1:], jnp.ones((blocks, 1), jnp.int32)], axis=1)
    last_local = lax.cummin(jnp.where(next_start == 1, labels[None, :], 127), axis=1, reverse=True)
    backward = (labels[None, :, None] >= first_local[:, None, :]).astype(jnp.float32)
    forward = (labels[None, :, None] <= last_local[:, None, :]).astype(jnp.float32)
    return (backward, forward)


def block_cumsum(values, matrices, from_end):
    groups = values.shape[0]
    length = values.shape[1]
    blocks = length // 128
    shaped = values.reshape(groups, blocks, 128)
    within = jnp.einsum("ebj,bji->ebi", shaped, matrices, precision=lax.Precision.HIGH)
    totals = jnp.sum(shaped, axis=2)
    if from_end:
        offsets = jnp.cumsum(totals[:, ::-1], axis=1)[:, ::-1] - totals
    else:
        offsets = jnp.cumsum(totals, axis=1) - totals
    return (within + offsets[:, :, None]).reshape(groups, length)


def leaf_update(predictions, leaf_index, table):
    groups, length = leaf_index.shape
    tiles = groups // 8
    table = lane_pad(table)

    def kernel(table_ref, pred_ref, leaf_ref, out_ref):
        row = table_ref[...]

        def one(step, carry):
            cols = pl.ds(pl.multiple_of(step * 128, 128), 128)
            picked = jnp.take_along_axis(row, leaf_ref[:, cols], axis=1, mode="promise_in_bounds")
            out_ref[:, cols] = pred_ref[:, cols] + picked
            return carry

        lax.fori_loop(0, length // 128, one, 0, unroll=8)

    spec = pl.BlockSpec((8, length), lambda t: (t, 0))
    return pl.pallas_call(
        kernel,
        grid=(tiles,),
        out_shape=jax.ShapeDtypeStruct((groups, length), jnp.float32),
        in_specs=[pl.BlockSpec((8, 128), lambda t: (t, 0)), spec, spec],
        out_specs=spec,
    )(table, predictions, leaf_index)


def on_device(predictions, leaf_index, events, tie_start):
    first_rows, last_rows = tie_rows(tie_start)
    gradient, hessian, stacked = front(predictions, events, first_rows, last_rows)
    grad_hess, leaf_weights, new_pred = finish(
        stacked, leaf_index, gradient, hessian, predictions, LEAVES, 2
    )
    grad_hess = grad_hess.reshape(2, grad_hess.shape[1], 1, grad_hess.shape[2])
    return (new_pred, leaf_weights, grad_hess)


def solution(mesh):
    placed = (P("ep", "tm"), P("ep", "tm"), P("ep", "tm"), P("tm"))
    return jax.shard_map(
        on_device,
        mesh=mesh,
        in_specs=placed,
        out_specs=(P("ep", "tm"), P("ep", None), P(None, None, "tm", "ep")),
        check_vma=False,
    )
```

```python
import math

import jax
import jax.numpy as jnp
from jax import lax
from jax.experimental import pallas as pl
from jax.experimental.pallas import tpu as pltpu
from jax.sharding import PartitionSpec as P

LEAVES = 64
MESH = pl.DeviceIdType.MESH


def tm_combine(part, mode, cid):
    n = lax.axis_size("tm")
    rows = part.shape[0]

    def kernel(x_ref, out_ref, held, send_sem, recv_sem):
        me = lax.axis_index("tm")
        ep = lax.axis_index("ep")
        barrier = pltpu.get_barrier_semaphore()

        def greet(k, carry):
            p = lax.rem(me + k, n)
            pl.semaphore_signal(barrier, inc=1, device_id=(ep, p), device_id_type=MESH)
            return carry

        lax.fori_loop(1, n, greet, 0)
        pl.semaphore_wait(barrier, n - 1)

        def copy_to(p):
            return pltpu.make_async_remote_copy(
                src_ref=x_ref,
                dst_ref=held.at[me],
                send_sem=send_sem.at[p],
                recv_sem=recv_sem.at[me],
                device_id=(ep, p),
                device_id_type=MESH,
            )

        def copy_from(p):
            return pltpu.make_async_remote_copy(
                src_ref=x_ref,
                dst_ref=held.at[p],
                send_sem=send_sem.at[p],
                recv_sem=recv_sem.at[p],
                device_id=(ep, p),
                device_id_type=MESH,
            )

        def send(k, carry):
            copy_to(lax.rem(me + k, n)).start()
            return carry

        lax.fori_loop(1, n, send, 0)

        def wait(k, carry):
            p = lax.rem(me + k, n)
            copy_to(p).wait_send()
            copy_from(p).wait_recv()
            return carry

        lax.fori_loop(1, n, wait, 0)

        if mode == "all":
            total = x_ref[...]
        else:
            total = jnp.zeros((rows, 128), jnp.float32)

        def add(k, total):
            p = lax.rem(me + k, n)
            if mode == "all":
                keep = True
            elif mode == "later":
                keep = p > me
            else:
                keep = p < me
            return total + jnp.where(keep, held[p], 0.0)

        out_ref[...] = lax.fori_loop(1, n, add, total)

    return pl.pallas_call(
        kernel,
        out_shape=jax.ShapeDtypeStruct((rows, 128), jnp.float32),
        in_specs=[pl.BlockSpec(memory_space=pltpu.VMEM)],
        out_specs=pl.BlockSpec(memory_space=pltpu.VMEM),
        scratch_shapes=[
            pltpu.VMEM((n, rows, 128), jnp.float32),
            pltpu.SemaphoreType.DMA((n,)),
            pltpu.SemaphoreType.DMA((n,)),
        ],
        compiler_params=pltpu.CompilerParams(collective_id=cid, has_side_effects=True),
    )(part)


def exchange_and_sum(stacked, leaf_index, gradient, hessian, leaves, cid):
    m = lax.axis_size("ep")
    two, groups, length = stacked.shape
    width = length // m
    tiles = groups // 8
    side = leaves // 8
    chunk = math.gcd(length, 4096)
    cols_all = side * 4 * 8

    def histogram(leaf_ref, grad_ref, hess_ref, sums_ref):
        row_id = lax.broadcasted_iota(jnp.int32, (side * 8, cols_all), 0)
        col_id = lax.broadcasted_iota(jnp.int32, (side * 8, cols_all), 1)
        diagonal = lax.rem(row_id, 8) == lax.rem(col_id, 8)
        fold = (
            lax.broadcasted_iota(jnp.int32, (cols_all, side * 4), 0) // 8
            == lax.broadcasted_iota(jnp.int32, (cols_all, side * 4), 1)
        ).astype(jnp.float32)

        def one_tile(t, carry):
            rows = pl.ds(pl.multiple_of(t * 8, 8), 8)

            def one_chunk(step, total):
                cols = pl.ds(pl.multiple_of(step * chunk, chunk), chunk)
                leaf = leaf_ref[rows, cols]
                grad = grad_ref[rows, cols]
                hess = hess_ref[rows, cols]
                high = lax.shift_right_logical(leaf, 3)
                low = jnp.bitwise_and(leaf, 7)
                grad_hi = grad.astype(jnp.bfloat16).astype(jnp.float32)
                hess_hi = hess.astype(jnp.bfloat16).astype(jnp.float32)
                values = (grad_hi, grad - grad_hi, hess_hi, hess - hess_hi)
                ones = jnp.concatenate(
                    [jnp.where(high == a, 1.0, 0.0) for a in range(side)], axis=0
                ).astype(jnp.bfloat16)
                pieces = []
                for b in range(side):
                    hit = low == b
                    for value in values:
                        pieces.append(jnp.where(hit, value, 0.0))
                parts = jnp.concatenate(pieces, axis=0).astype(jnp.bfloat16)
                return total + lax.dot_general(
                    ones, parts, (((1,), (1,)), ((), ())), preferred_element_type=jnp.float32
                )

            total = jnp.zeros((side * 8, cols_all), jnp.float32)
            total = lax.fori_loop(0, length // chunk, one_chunk, total)
            total = jnp.where(diagonal, total, 0.0)
            sums_ref[t] = jnp.dot(
                total, fold, precision=lax.Precision.HIGHEST, preferred_element_type=jnp.float32
            )
            return carry

        lax.fori_loop(0, tiles, one_tile, 0)

    def kernel(src_ref, leaf_ref, grad_ref, hess_ref, out_ref, sums_ref, send_sem, recv_sem, local_sem):
        me = lax.axis_index("ep")
        tm = lax.axis_index("tm")
        barrier = pltpu.get_barrier_semaphore()
        for k in range(1, m):
            p = lax.rem(me + k, m)
            pl.semaphore_signal(barrier, inc=1, device_id=(p, tm), device_id_type=MESH)
        pl.semaphore_wait(barrier, m - 1)

        def copy_to(p):
            return pltpu.make_async_remote_copy(
                src_ref=src_ref.at[:, :, pl.ds(p * width, width)],
                dst_ref=out_ref.at[:, pl.ds(me * groups, groups), :],
                send_sem=send_sem.at[p],
                recv_sem=recv_sem.at[me],
                device_id=(p, tm),
                device_id_type=MESH,
            )

        def copy_from(p):
            return pltpu.make_async_remote_copy(
                src_ref=src_ref.at[:, :, pl.ds(me * width, width)],
                dst_ref=out_ref.at[:, pl.ds(p * groups, groups), :],
                send_sem=send_sem.at[p],
                recv_sem=recv_sem.at[p],
                device_id=(p, tm),
                device_id_type=MESH,
            )

        for k in range(1, m):
            copy_to(lax.rem(me + k, m)).start()
        local = pltpu.make_async_copy(
            src_ref.at[:, :, pl.ds(me * width, width)],
            out_ref.at[:, pl.ds(me * groups, groups), :],
            local_sem.at[0],
        )
        local.start()
        histogram(leaf_ref, grad_ref, hess_ref, sums_ref)
        local.wait()
        for k in range(1, m):
            p = lax.rem(me + k, m)
            copy_to(p).wait_send()
            copy_from(p).wait_recv()

    vmem = pl.BlockSpec(memory_space=pltpu.VMEM)
    grad_hess, sums = pl.pallas_call(
        kernel,
        out_shape=(
            jax.ShapeDtypeStruct((two, groups * m, width), stacked.dtype),
            jax.ShapeDtypeStruct((tiles, side * 8, side * 4), jnp.float32),
        ),
        in_specs=[pl.BlockSpec(memory_space=pl.ANY), vmem, vmem, vmem],
        out_specs=(pl.BlockSpec(memory_space=pl.ANY), vmem),
        scratch_shapes=[
            pltpu.SemaphoreType.DMA((m,)),
            pltpu.SemaphoreType.DMA((m,)),
            pltpu.SemaphoreType.DMA((1,)),
        ],
        compiler_params=pltpu.CompilerParams(collective_id=cid, has_side_effects=True),
    )(stacked, leaf_index, gradient, hessian)
    sums = sums.reshape(tiles, side, 8, side, 4).transpose(0, 2, 1, 3, 4)
    sums = sums.reshape(groups, leaves, 4)
    gsum = sums[:, :, 0] + sums[:, :, 1]
    hsum = sums[:, :, 2] + sums[:, :, 3]
    return grad_hess, jnp.stack([gsum, hsum], axis=1)


def finish(stacked, leaf_index, gradient, hessian, predictions, leaves, cid):
    m = lax.axis_size("ep")
    n = lax.axis_size("tm")
    two, groups, length = stacked.shape
    width = length // m
    tiles = groups // 8
    side = leaves // 8
    chunk = math.gcd(length, 4096)
    cols_all = side * 4 * 8

    def histogram(leaf_ref, grad_ref, hess_ref, mine):
        row_id = lax.broadcasted_iota(jnp.int32, (side * 8, cols_all), 0)
        col_id = lax.broadcasted_iota(jnp.int32, (side * 8, cols_all), 1)
        diagonal = lax.rem(row_id, 8) == lax.rem(col_id, 8)
        src = lax.broadcasted_iota(jnp.int32, (cols_all, 2 * leaves), 0)
        dst = lax.broadcasted_iota(jnp.int32, (cols_all, 2 * leaves), 1)
        src_b = src // 32
        src_c = lax.rem(src // 8, 4)

        def one_tile(t, carry):
            rows = pl.ds(pl.multiple_of(t * 8, 8), 8)

            def one_chunk(step, total):
                cols = pl.ds(pl.multiple_of(step * chunk, chunk), chunk)
                leaf = leaf_ref[rows, cols]
                grad = grad_ref[rows, cols]
                hess = hess_ref[rows, cols]
                high = lax.shift_right_logical(leaf, 3)
                low = jnp.bitwise_and(leaf, 7)
                grad_hi = grad.astype(jnp.bfloat16).astype(jnp.float32)
                hess_hi = hess.astype(jnp.bfloat16).astype(jnp.float32)
                values = (grad_hi, grad - grad_hi, hess_hi, hess - hess_hi)
                ones = jnp.concatenate(
                    [jnp.where(high == a, 1.0, 0.0) for a in range(side)], axis=0
                ).astype(jnp.bfloat16)
                pieces = []
                for b in range(side):
                    hit = low == b
                    for value in values:
                        pieces.append(jnp.where(hit, value, 0.0))
                parts = jnp.concatenate(pieces, axis=0).astype(jnp.bfloat16)
                return total + lax.dot_general(
                    ones, parts, (((1,), (1,)), ((), ())), preferred_element_type=jnp.float32
                )

            total = jnp.zeros((side * 8, cols_all), jnp.float32)
            total = lax.fori_loop(0, length // chunk, one_chunk, total)
            total = jnp.where(diagonal, total, 0.0)
            out = jnp.zeros((8, 2 * leaves), jnp.float32)
            for a in range(side):
                fold = (dst == (src_c // 2) * leaves + a * side + src_b).astype(jnp.float32)
                out = out + jnp.dot(
                    total[a * 8:(a + 1) * 8, :], fold,
                    precision=lax.Precision.HIGHEST, preferred_element_type=jnp.float32,
                )
            mine[rows, :] = out
            return carry

        lax.fori_loop(0, tiles, one_tile, 0)

    def kernel(src_ref, leaf_ref, grad_ref, hess_ref, pred_ref,
               out_ref, weights_ref, new_ref,
               mine, held, ep_send, ep_recv, tm_send, tm_recv, local_sem):
        me = lax.axis_index("ep")
        tm = lax.axis_index("tm")
        barrier = pltpu.get_barrier_semaphore()
        for k in range(1, m):
            p = lax.rem(me + k, m)
            pl.semaphore_signal(barrier, inc=1, device_id=(p, tm), device_id_type=MESH)

        def greet(k, carry):
            p = lax.rem(tm + k, n)
            pl.semaphore_signal(barrier, inc=1, device_id=(me, p), device_id_type=MESH)
            return carry

        lax.fori_loop(1, n, greet, 0)
        pl.semaphore_wait(barrier, (m - 1) + (n - 1))

        def ep_to(p):
            return pltpu.make_async_remote_copy(
                src_ref=src_ref.at[:, :, pl.ds(p * width, width)],
                dst_ref=out_ref.at[:, pl.ds(me * groups, groups), :],
                send_sem=ep_send.at[p],
                recv_sem=ep_recv.at[me],
                device_id=(p, tm),
                device_id_type=MESH,
            )

        def ep_from(p):
            return pltpu.make_async_remote_copy(
                src_ref=src_ref.at[:, :, pl.ds(me * width, width)],
                dst_ref=out_ref.at[:, pl.ds(p * groups, groups), :],
                send_sem=ep_send.at[p],
                recv_sem=ep_recv.at[p],
                device_id=(p, tm),
                device_id_type=MESH,
            )

        for k in range(1, m):
            ep_to(lax.rem(me + k, m)).start()
        local = pltpu.make_async_copy(
            src_ref.at[:, :, pl.ds(me * width, width)],
            out_ref.at[:, pl.ds(me * groups, groups), :],
            local_sem.at[0],
        )
        local.start()

        histogram(leaf_ref, grad_ref, hess_ref, mine)
        staged = pltpu.make_async_copy(mine, held.at[tm], local_sem.at[1])
        staged.start()
        staged.wait()

        def tm_to(p):
            return pltpu.make_async_remote_copy(
                src_ref=held.at[tm],
                dst_ref=held.at[tm],
                send_sem=tm_send.at[p],
                recv_sem=tm_recv.at[tm],
                device_id=(me, p),
                device_id_type=MESH,
            )

        def tm_from(p):
            return pltpu.make_async_remote_copy(
                src_ref=held.at[tm],
                dst_ref=held.at[p],
                send_sem=tm_send.at[p],
                recv_sem=tm_recv.at[p],
                device_id=(me, p),
                device_id_type=MESH,
            )

        def send(k, carry):
            tm_to(lax.rem(tm + k, n)).start()
            return carry

        lax.fori_loop(1, n, send, 0)

        def wait(k, carry):
            p = lax.rem(tm + k, n)
            tm_to(p).wait_send()
            tm_from(p).wait_recv()
            return carry

        lax.fori_loop(1, n, wait, 0)

        def add(k, total):
            return total + held[lax.rem(tm + k, n)]

        totals = lax.fori_loop(1, n, add, held[tm])
        lane = lax.broadcasted_iota(jnp.int32, (groups, 2 * leaves), 1)
        hsum = pltpu.roll(totals, leaves, 1)
        table = jnp.where(lane < leaves, -totals / (hsum + 1.0), 0.0)
        weights_ref[...] = table[:, :leaves]

        mine[...] = table

        def one_tile(t, carry):
            rows = pl.ds(pl.multiple_of(t * 8, 8), 8)
            row = mine[rows, :]

            def one(step, carry):
                cols = pl.ds(pl.multiple_of(step * 128, 128), 128)
                picked = jnp.take_along_axis(
                    row, leaf_ref[rows, cols], axis=1, mode="promise_in_bounds"
                )
                new_ref[rows, cols] = pred_ref[rows, cols] + picked
                return carry

            lax.fori_loop(0, length // 128, one, 0, unroll=8)
            return carry

        lax.fori_loop(0, tiles, one_tile, 0)

        local.wait()
        for k in range(1, m):
            p = lax.rem(me + k, m)
            ep_to(p).wait_send()
            ep_from(p).wait_recv()

    vmem = pl.BlockSpec(memory_space=pltpu.VMEM)
    grad_hess, leaf_weights, new_pred = pl.pallas_call(
        kernel,
        out_shape=(
            jax.ShapeDtypeStruct((two, groups * m, width), stacked.dtype),
            jax.ShapeDtypeStruct((groups, leaves), jnp.float32),
            jax.ShapeDtypeStruct((groups, length), jnp.float32),
        ),
        in_specs=[pl.BlockSpec(memory_space=pl.ANY), vmem, vmem, vmem, vmem],
        out_specs=(pl.BlockSpec(memory_space=pl.ANY), vmem, vmem),
        scratch_shapes=[
            pltpu.VMEM((groups, 2 * leaves), jnp.float32),
            pltpu.VMEM((n, groups, 2 * leaves), jnp.float32),
            pltpu.SemaphoreType.DMA((m,)),
            pltpu.SemaphoreType.DMA((m,)),
            pltpu.SemaphoreType.DMA((n,)),
            pltpu.SemaphoreType.DMA((n,)),
            pltpu.SemaphoreType.DMA((2,)),
        ],
        compiler_params=pltpu.CompilerParams(
            collective_id=cid, has_side_effects=True, vmem_limit_bytes=60 * 1024 * 1024
        ),
    )(stacked, leaf_index, gradient, hessian, predictions)
    return grad_hess, leaf_weights, new_pred


def tm_exchange(payload, held, send_sem, recv_sem, stage_sem, ep, me, n):
    staged = pltpu.make_async_copy(payload, held.at[me], stage_sem)
    staged.start()
    staged.wait()

    def copy_to(p):
        return pltpu.make_async_remote_copy(
            src_ref=held.at[me],
            dst_ref=held.at[me],
            send_sem=send_sem.at[p],
            recv_sem=recv_sem.at[me],
            device_id=(ep, p),
            device_id_type=MESH,
        )

    def copy_from(p):
        return pltpu.make_async_remote_copy(
            src_ref=held.at[me],
            dst_ref=held.at[p],
            send_sem=send_sem.at[p],
            recv_sem=recv_sem.at[p],
            device_id=(ep, p),
            device_id_type=MESH,
        )

    def send(k, carry):
        copy_to(lax.rem(me + k, n)).start()
        return carry

    lax.fori_loop(1, n, send, 0)

    def wait(k, carry):
        p = lax.rem(me + k, n)
        copy_to(p).wait_send()
        copy_from(p).wait_recv()
        return carry

    lax.fori_loop(1, n, wait, 0)


def scan_lanes(x, from_end):
    lane = lax.broadcasted_iota(jnp.int32, x.shape, 1)
    k = 1
    while k < 128:
        if from_end:
            moved = pltpu.roll(x, 128 - k, 1)
            x = x + jnp.where(lane < 128 - k, moved, 0.0)
        else:
            moved = pltpu.roll(x, k, 1)
            x = x + jnp.where(lane >= k, moved, 0.0)
        k *= 2
    return x


def front(predictions, events, first_rows, last_rows):
    n = lax.axis_size("tm")
    groups, length = predictions.shape
    tiles = groups // 8
    blocks = length // 128
    span = math.gcd(blocks, 32)
    groups_n = blocks // span

    def kernel(pred_ref, ev_ref, first_ref, last_ref,
               grad_ref, hess_ref, both_ref,
               weight, one, two, pay_a, held_a, pay_b, held_b,
               send_a, recv_a, send_b, recv_b, stage):
        me = lax.axis_index("tm")
        ep = lax.axis_index("ep")
        barrier = pltpu.get_barrier_semaphore()

        def greet(k, carry):
            p = lax.rem(me + k, n)
            pl.semaphore_signal(barrier, inc=1, device_id=(ep, p), device_id_type=MESH)
            return carry

        lax.fori_loop(1, n, greet, 0)
        pl.semaphore_wait(barrier, n - 1)

        lane_j = lax.broadcasted_iota(jnp.int32, (128, 128), 0)
        lane_i = lax.broadcasted_iota(jnp.int32, (128, 128), 1)
        upper = (lane_j >= lane_i).astype(jnp.bfloat16)
        lower = (lane_j <= lane_i).astype(jnp.bfloat16)

        def run_sum(x, matrix):
            hi = x.astype(jnp.bfloat16)
            lo = (x - hi.astype(jnp.float32)).astype(jnp.bfloat16)
            out = jnp.dot(hi, matrix, preferred_element_type=jnp.float32)
            return out + jnp.dot(lo, matrix, preferred_element_type=jnp.float32)

        def block_cols(b):
            return pl.ds(pl.multiple_of(b * 128, 128), 128)

        def suffix_tile(t, carry):
            rows = pl.ds(pl.multiple_of(t * 8, 8), 8)

            def one_group(j, later):
                b0 = (groups_n - 1 - j) * span
                pieces = []
                for k in range(span):
                    w = jnp.exp(pred_ref[rows, block_cols(b0 + k)])
                    weight[rows, block_cols(b0 + k)] = w
                    pieces.append(w)
                s = run_sum(jnp.concatenate(pieces, axis=0), upper)
                idx = first_ref[pl.ds(pl.multiple_of(b0 * 8, 8), 8 * span), :]
                r = jnp.take_along_axis(s, idx, axis=1, mode="promise_in_bounds")
                for k in reversed(range(span)):
                    one[rows, block_cols(b0 + k)] = r[8 * k:8 * k + 8] + later
                    later = later + jnp.broadcast_to(s[8 * k:8 * k + 8, 0:1], (8, 128))
                return later

            total = lax.fori_loop(0, groups_n, one_group, jnp.zeros((8, 128), jnp.float32), unroll=2)
            pay_a[rows, :] = total
            return carry

        lax.fori_loop(0, tiles, suffix_tile, 0)
        tm_exchange(pay_a, held_a, send_a, recv_a, stage.at[0], ep, me, n)

        def add_later(k, total):
            p = lax.rem(me + k, n)
            return total + jnp.where(p > me, held_a[p], 0.0)

        pay_a[...] = lax.fori_loop(1, n, add_later, jnp.zeros((groups, 128), jnp.float32))

        def prefix_tile(t, carry):
            rows = pl.ds(pl.multiple_of(t * 8, 8), 8)
            later = pay_a[rows, :]

            def one_group(j, carries):
                c1, c2 = carries
                b0 = j * span
                firsts, seconds = [], []
                for k in range(span):
                    risk = one[rows, block_cols(b0 + k)] + later
                    observed = ev_ref[rows, block_cols(b0 + k)].astype(jnp.float32)
                    scale = 1.0 / risk
                    inv_one = observed * scale
                    firsts.append(inv_one)
                    seconds.append(inv_one * scale)
                s = run_sum(jnp.concatenate(firsts + seconds, axis=0), lower)
                idx = last_ref[pl.ds(pl.multiple_of(b0 * 8, 8), 8 * span), :]
                idx = jnp.concatenate([idx, idx], axis=0)
                r = jnp.take_along_axis(s, idx, axis=1, mode="promise_in_bounds")
                half = 8 * span
                for k in range(span):
                    one[rows, block_cols(b0 + k)] = r[8 * k:8 * k + 8] + c1
                    two[rows, block_cols(b0 + k)] = r[half + 8 * k:half + 8 * k + 8] + c2
                    c1 = c1 + jnp.broadcast_to(s[8 * k:8 * k + 8, 127:128], (8, 128))
                    c2 = c2 + jnp.broadcast_to(s[half + 8 * k:half + 8 * k + 8, 127:128], (8, 128))
                return (c1, c2)

            zero = jnp.zeros((8, 128), jnp.float32)
            c1, c2 = lax.fori_loop(0, groups_n, one_group, (zero, zero), unroll=2)
            pay_b[rows, :] = c1
            pay_b[pl.ds(pl.multiple_of(groups + t * 8, 8), 8), :] = c2
            return carry

        lax.fori_loop(0, tiles, prefix_tile, 0)
        tm_exchange(pay_b, held_b, send_b, recv_b, stage.at[1], ep, me, n)

        def add_earlier(k, total):
            p = lax.rem(me + k, n)
            return total + jnp.where(p < me, held_b[p], 0.0)

        pay_b[...] = lax.fori_loop(1, n, add_earlier, jnp.zeros((2 * groups, 128), jnp.float32))

        def out_tile(t, carry):
            rows = pl.ds(pl.multiple_of(t * 8, 8), 8)
            e1 = jnp.tile(pay_b[rows, :], (1, span))
            e2 = jnp.tile(pay_b[pl.ds(pl.multiple_of(groups + t * 8, 8), 8), :], (1, span))

            def one_group(j, carry):
                cols = pl.ds(pl.multiple_of(j * span * 128, span * 128), span * 128)
                w = weight[rows, cols]
                a1 = one[rows, cols] + e1
                a2 = two[rows, cols] + e2
                observed = ev_ref[rows, cols].astype(jnp.float32)
                g = w * a1 - observed
                h = w * a1 - w * w * a2
                grad_ref[rows, cols] = g
                hess_ref[rows, cols] = h
                both_ref[0, rows, cols] = g.astype(jnp.bfloat16)
                both_ref[1, rows, cols] = h.astype(jnp.bfloat16)
                return carry

            lax.fori_loop(0, groups_n, one_group, 0)
            return carry

        lax.fori_loop(0, tiles, out_tile, 0)

    vmem = pl.BlockSpec(memory_space=pltpu.VMEM)
    return pl.pallas_call(
        kernel,
        out_shape=(
            jax.ShapeDtypeStruct((groups, length), jnp.float32),
            jax.ShapeDtypeStruct((groups, length), jnp.float32),
            jax.ShapeDtypeStruct((2, groups, length), jnp.bfloat16),
        ),
        in_specs=[vmem, vmem, vmem, vmem],
        out_specs=(vmem, vmem, vmem),
        scratch_shapes=[
            pltpu.VMEM((groups, length), jnp.float32),
            pltpu.VMEM((groups, length), jnp.float32),
            pltpu.VMEM((groups, length), jnp.float32),
            pltpu.VMEM((groups, 128), jnp.float32),
            pltpu.VMEM((n, groups, 128), jnp.float32),
            pltpu.VMEM((2 * groups, 128), jnp.float32),
            pltpu.VMEM((n, 2 * groups, 128), jnp.float32),
            pltpu.SemaphoreType.DMA((n,)),
            pltpu.SemaphoreType.DMA((n,)),
            pltpu.SemaphoreType.DMA((n,)),
            pltpu.SemaphoreType.DMA((n,)),
            pltpu.SemaphoreType.DMA((2,)),
        ],
        compiler_params=pltpu.CompilerParams(
            collective_id=0, has_side_effects=True, vmem_limit_bytes=60 * 1024 * 1024
        ),
    )(predictions, events, first_rows, last_rows)


def tie_rows(tie_start):
    length = tie_start.shape[0]
    blocks = length // 128
    starts = tie_start.reshape(blocks, 128)
    labels = jnp.arange(128, dtype=jnp.int32)
    first_local = lax.cummax(jnp.where(starts == 1, labels[None, :], 0), axis=1)
    next_start = jnp.concatenate([starts[:, 1:], jnp.ones((blocks, 1), jnp.int32)], axis=1)
    last_local = lax.cummin(jnp.where(next_start == 1, labels[None, :], 127), axis=1, reverse=True)

    def spread(rows):
        return jnp.broadcast_to(rows[:, None, :], (blocks, 8, 128)).reshape(blocks * 8, 128)

    return spread(first_local), spread(last_local)


def lane_pad(vectors):
    width = vectors.shape[1]
    return jnp.pad(vectors, ((0, 0), (0, 128 - width)))


def tile_matrices(tie_start):
    length = tie_start.shape[0]
    blocks = length // 128
    starts = tie_start.reshape(blocks, 128)
    labels = jnp.arange(128, dtype=jnp.int32)
    first_local = lax.cummax(jnp.where(starts == 1, labels[None, :], 0), axis=1)
    next_start = jnp.concatenate([starts[:, 1:], jnp.ones((blocks, 1), jnp.int32)], axis=1)
    last_local = lax.cummin(jnp.where(next_start == 1, labels[None, :], 127), axis=1, reverse=True)
    backward = (labels[None, :, None] >= first_local[:, None, :]).astype(jnp.float32)
    forward = (labels[None, :, None] <= last_local[:, None, :]).astype(jnp.float32)
    return (backward, forward)


def block_cumsum(values, matrices, from_end):
    groups = values.shape[0]
    length = values.shape[1]
    blocks = length // 128
    shaped = values.reshape(groups, blocks, 128)
    within = jnp.einsum("ebj,bji->ebi", shaped, matrices, precision=lax.Precision.HIGH)
    totals = jnp.sum(shaped, axis=2)
    if from_end:
        offsets = jnp.cumsum(totals[:, ::-1], axis=1)[:, ::-1] - totals
    else:
        offsets = jnp.cumsum(totals, axis=1) - totals
    return (within + offsets[:, :, None]).reshape(groups, length)


def leaf_update(predictions, leaf_index, table):
    groups, length = leaf_index.shape
    tiles = groups // 8
    table = lane_pad(table)

    def kernel(table_ref, pred_ref, leaf_ref, out_ref):
        row = table_ref[...]

        def one(step, carry):
            cols = pl.ds(pl.multiple_of(step * 128, 128), 128)
            picked = jnp.take_along_axis(row, leaf_ref[:, cols], axis=1, mode="promise_in_bounds")
            out_ref[:, cols] = pred_ref[:, cols] + picked
            return carry

        lax.fori_loop(0, length // 128, one, 0, unroll=8)

    spec = pl.BlockSpec((8, length), lambda t: (t, 0))
    return pl.pallas_call(
        kernel,
        grid=(tiles,),
        out_shape=jax.ShapeDtypeStruct((groups, length), jnp.float32),
        in_specs=[pl.BlockSpec((8, 128), lambda t: (t, 0)), spec, spec],
        out_specs=spec,
    )(table, predictions, leaf_index)


def on_device(predictions, leaf_index, events, tie_start):
    first_rows, last_rows = tie_rows(tie_start)
    gradient, hessian, stacked = front(predictions, events, first_rows, last_rows)
    grad_hess, leaf_weights, new_pred = finish(
        stacked, leaf_index, gradient, hessian, predictions, LEAVES, 2
    )
    grad_hess = grad_hess.reshape(2, grad_hess.shape[1], 1, grad_hess.shape[2])
    return (new_pred, leaf_weights, grad_hess)


def solution(mesh):
    placed = (P("ep", "tm"), P("ep", "tm"), P("ep", "tm"), P("tm"))
    return jax.shard_map(
        on_device,
        mesh=mesh,
        in_specs=placed,
        out_specs=(P("ep", "tm"), P("ep", None), P(None, None, "tm", "ep")),
        check_vma=False,
    )
```

```python
import math

import jax
import jax.numpy as jnp
from jax import lax
from jax.experimental import pallas as pl
from jax.experimental.pallas import tpu as pltpu
from jax.sharding import PartitionSpec as P

LEAVES = 64
MESH = pl.DeviceIdType.MESH


def tm_combine(part, mode, cid):
    n = lax.axis_size("tm")
    rows = part.shape[0]

    def kernel(x_ref, out_ref, held, send_sem, recv_sem):
        me = lax.axis_index("tm")
        ep = lax.axis_index("ep")
        barrier = pltpu.get_barrier_semaphore()

        def greet(k, carry):
            p = lax.rem(me + k, n)
            pl.semaphore_signal(barrier, inc=1, device_id=(ep, p), device_id_type=MESH)
            return carry

        lax.fori_loop(1, n, greet, 0)
        pl.semaphore_wait(barrier, n - 1)

        def copy_to(p):
            return pltpu.make_async_remote_copy(
                src_ref=x_ref,
                dst_ref=held.at[me],
                send_sem=send_sem.at[p],
                recv_sem=recv_sem.at[me],
                device_id=(ep, p),
                device_id_type=MESH,
            )

        def copy_from(p):
            return pltpu.make_async_remote_copy(
                src_ref=x_ref,
                dst_ref=held.at[p],
                send_sem=send_sem.at[p],
                recv_sem=recv_sem.at[p],
                device_id=(ep, p),
                device_id_type=MESH,
            )

        def send(k, carry):
            copy_to(lax.rem(me + k, n)).start()
            return carry

        lax.fori_loop(1, n, send, 0)

        def wait(k, carry):
            p = lax.rem(me + k, n)
            copy_to(p).wait_send()
            copy_from(p).wait_recv()
            return carry

        lax.fori_loop(1, n, wait, 0)

        if mode == "all":
            total = x_ref[...]
        else:
            total = jnp.zeros((rows, 128), jnp.float32)

        def add(k, total):
            p = lax.rem(me + k, n)
            if mode == "all":
                keep = True
            elif mode == "later":
                keep = p > me
            else:
                keep = p < me
            return total + jnp.where(keep, held[p], 0.0)

        out_ref[...] = lax.fori_loop(1, n, add, total)

    return pl.pallas_call(
        kernel,
        out_shape=jax.ShapeDtypeStruct((rows, 128), jnp.float32),
        in_specs=[pl.BlockSpec(memory_space=pltpu.VMEM)],
        out_specs=pl.BlockSpec(memory_space=pltpu.VMEM),
        scratch_shapes=[
            pltpu.VMEM((n, rows, 128), jnp.float32),
            pltpu.SemaphoreType.DMA((n,)),
            pltpu.SemaphoreType.DMA((n,)),
        ],
        compiler_params=pltpu.CompilerParams(collective_id=cid, has_side_effects=True),
    )(part)


def exchange_and_sum(stacked, leaf_index, gradient, hessian, leaves, cid):
    m = lax.axis_size("ep")
    two, groups, length = stacked.shape
    width = length // m
    tiles = groups // 8
    side = leaves // 8
    chunk = math.gcd(length, 4096)
    cols_all = side * 4 * 8

    def histogram(leaf_ref, grad_ref, hess_ref, sums_ref):
        row_id = lax.broadcasted_iota(jnp.int32, (side * 8, cols_all), 0)
        col_id = lax.broadcasted_iota(jnp.int32, (side * 8, cols_all), 1)
        diagonal = lax.rem(row_id, 8) == lax.rem(col_id, 8)
        fold = (
            lax.broadcasted_iota(jnp.int32, (cols_all, side * 4), 0) // 8
            == lax.broadcasted_iota(jnp.int32, (cols_all, side * 4), 1)
        ).astype(jnp.float32)

        def one_tile(t, carry):
            rows = pl.ds(pl.multiple_of(t * 8, 8), 8)

            def one_chunk(step, total):
                cols = pl.ds(pl.multiple_of(step * chunk, chunk), chunk)
                leaf = leaf_ref[rows, cols]
                grad = grad_ref[rows, cols]
                hess = hess_ref[rows, cols]
                high = lax.shift_right_logical(leaf, 3)
                low = jnp.bitwise_and(leaf, 7)
                grad_hi = grad.astype(jnp.bfloat16).astype(jnp.float32)
                hess_hi = hess.astype(jnp.bfloat16).astype(jnp.float32)
                values = (grad_hi, grad - grad_hi, hess_hi, hess - hess_hi)
                ones = jnp.concatenate(
                    [jnp.where(high == a, 1.0, 0.0) for a in range(side)], axis=0
                ).astype(jnp.bfloat16)
                pieces = []
                for b in range(side):
                    hit = low == b
                    for value in values:
                        pieces.append(jnp.where(hit, value, 0.0))
                parts = jnp.concatenate(pieces, axis=0).astype(jnp.bfloat16)
                return total + lax.dot_general(
                    ones, parts, (((1,), (1,)), ((), ())), preferred_element_type=jnp.float32
                )

            total = jnp.zeros((side * 8, cols_all), jnp.float32)
            total = lax.fori_loop(0, length // chunk, one_chunk, total)
            total = jnp.where(diagonal, total, 0.0)
            sums_ref[t] = jnp.dot(
                total, fold, precision=lax.Precision.HIGHEST, preferred_element_type=jnp.float32
            )
            return carry

        lax.fori_loop(0, tiles, one_tile, 0)

    def kernel(src_ref, leaf_ref, grad_ref, hess_ref, out_ref, sums_ref, send_sem, recv_sem, local_sem):
        me = lax.axis_index("ep")
        tm = lax.axis_index("tm")
        barrier = pltpu.get_barrier_semaphore()
        for k in range(1, m):
            p = lax.rem(me + k, m)
            pl.semaphore_signal(barrier, inc=1, device_id=(p, tm), device_id_type=MESH)
        pl.semaphore_wait(barrier, m - 1)

        def copy_to(p):
            return pltpu.make_async_remote_copy(
                src_ref=src_ref.at[:, :, pl.ds(p * width, width)],
                dst_ref=out_ref.at[:, pl.ds(me * groups, groups), :],
                send_sem=send_sem.at[p],
                recv_sem=recv_sem.at[me],
                device_id=(p, tm),
                device_id_type=MESH,
            )

        def copy_from(p):
            return pltpu.make_async_remote_copy(
                src_ref=src_ref.at[:, :, pl.ds(me * width, width)],
                dst_ref=out_ref.at[:, pl.ds(p * groups, groups), :],
                send_sem=send_sem.at[p],
                recv_sem=recv_sem.at[p],
                device_id=(p, tm),
                device_id_type=MESH,
            )

        for k in range(1, m):
            copy_to(lax.rem(me + k, m)).start()
        local = pltpu.make_async_copy(
            src_ref.at[:, :, pl.ds(me * width, width)],
            out_ref.at[:, pl.ds(me * groups, groups), :],
            local_sem.at[0],
        )
        local.start()
        histogram(leaf_ref, grad_ref, hess_ref, sums_ref)
        local.wait()
        for k in range(1, m):
            p = lax.rem(me + k, m)
            copy_to(p).wait_send()
            copy_from(p).wait_recv()

    vmem = pl.BlockSpec(memory_space=pltpu.VMEM)
    grad_hess, sums = pl.pallas_call(
        kernel,
        out_shape=(
            jax.ShapeDtypeStruct((two, groups * m, width), stacked.dtype),
            jax.ShapeDtypeStruct((tiles, side * 8, side * 4), jnp.float32),
        ),
        in_specs=[pl.BlockSpec(memory_space=pl.ANY), vmem, vmem, vmem],
        out_specs=(pl.BlockSpec(memory_space=pl.ANY), vmem),
        scratch_shapes=[
            pltpu.SemaphoreType.DMA((m,)),
            pltpu.SemaphoreType.DMA((m,)),
            pltpu.SemaphoreType.DMA((1,)),
        ],
        compiler_params=pltpu.CompilerParams(collective_id=cid, has_side_effects=True),
    )(stacked, leaf_index, gradient, hessian)
    sums = sums.reshape(tiles, side, 8, side, 4).transpose(0, 2, 1, 3, 4)
    sums = sums.reshape(groups, leaves, 4)
    gsum = sums[:, :, 0] + sums[:, :, 1]
    hsum = sums[:, :, 2] + sums[:, :, 3]
    return grad_hess, jnp.stack([gsum, hsum], axis=1)


def finish(stacked, leaf_index, gradient, hessian, predictions, leaves, cid):
    m = lax.axis_size("ep")
    n = lax.axis_size("tm")
    two, groups, length = stacked.shape
    width = length // m
    tiles = groups // 8
    side = leaves // 8
    chunk = math.gcd(length, 8192)
    cols_all = side * 4 * 8

    def histogram(leaf_ref, grad_ref, hess_ref, mine):
        row_id = lax.broadcasted_iota(jnp.int32, (side * 8, cols_all), 0)
        col_id = lax.broadcasted_iota(jnp.int32, (side * 8, cols_all), 1)
        diagonal = lax.rem(row_id, 8) == lax.rem(col_id, 8)
        src = lax.broadcasted_iota(jnp.int32, (cols_all, 2 * leaves), 0)
        dst = lax.broadcasted_iota(jnp.int32, (cols_all, 2 * leaves), 1)
        src_b = src // 32
        src_c = lax.rem(src // 8, 4)

        def one_tile(t, carry):
            rows = pl.ds(pl.multiple_of(t * 8, 8), 8)

            def one_chunk(step, total):
                cols = pl.ds(pl.multiple_of(step * chunk, chunk), chunk)
                leaf = leaf_ref[rows, cols]
                grad = grad_ref[rows, cols]
                hess = hess_ref[rows, cols]
                high = lax.shift_right_logical(leaf, 3)
                low = jnp.bitwise_and(leaf, 7)
                grad_hi = grad.astype(jnp.bfloat16).astype(jnp.float32)
                hess_hi = hess.astype(jnp.bfloat16).astype(jnp.float32)
                values = (grad_hi, grad - grad_hi, hess_hi, hess - hess_hi)
                ones = jnp.concatenate(
                    [jnp.where(high == a, 1.0, 0.0) for a in range(side)], axis=0
                ).astype(jnp.bfloat16)
                pieces = []
                for b in range(side):
                    hit = low == b
                    for value in values:
                        pieces.append(jnp.where(hit, value, 0.0))
                parts = jnp.concatenate(pieces, axis=0).astype(jnp.bfloat16)
                return total + lax.dot_general(
                    ones, parts, (((1,), (1,)), ((), ())), preferred_element_type=jnp.float32
                )

            total = jnp.zeros((side * 8, cols_all), jnp.float32)
            total = lax.fori_loop(0, length // chunk, one_chunk, total)
            total = jnp.where(diagonal, total, 0.0)
            out = jnp.zeros((8, 2 * leaves), jnp.float32)
            for a in range(side):
                fold = (dst == (src_c // 2) * leaves + a * side + src_b).astype(jnp.float32)
                out = out + jnp.dot(
                    total[a * 8:(a + 1) * 8, :], fold,
                    precision=lax.Precision.HIGHEST, preferred_element_type=jnp.float32,
                )
            mine[rows, :] = out
            return carry

        lax.fori_loop(0, tiles, one_tile, 0)

    def kernel(src_ref, leaf_ref, grad_ref, hess_ref, pred_ref,
               out_ref, weights_ref, new_ref,
               mine, held, ep_send, ep_recv, tm_send, tm_recv, local_sem):
        me = lax.axis_index("ep")
        tm = lax.axis_index("tm")
        barrier = pltpu.get_barrier_semaphore()
        for k in range(1, m):
            p = lax.rem(me + k, m)
            pl.semaphore_signal(barrier, inc=1, device_id=(p, tm), device_id_type=MESH)

        def greet(k, carry):
            p = lax.rem(tm + k, n)
            pl.semaphore_signal(barrier, inc=1, device_id=(me, p), device_id_type=MESH)
            return carry

        lax.fori_loop(1, n, greet, 0)
        pl.semaphore_wait(barrier, (m - 1) + (n - 1))

        def ep_to(p):
            return pltpu.make_async_remote_copy(
                src_ref=src_ref.at[:, :, pl.ds(p * width, width)],
                dst_ref=out_ref.at[:, pl.ds(me * groups, groups), :],
                send_sem=ep_send.at[p],
                recv_sem=ep_recv.at[me],
                device_id=(p, tm),
                device_id_type=MESH,
            )

        def ep_from(p):
            return pltpu.make_async_remote_copy(
                src_ref=src_ref.at[:, :, pl.ds(me * width, width)],
                dst_ref=out_ref.at[:, pl.ds(p * groups, groups), :],
                send_sem=ep_send.at[p],
                recv_sem=ep_recv.at[p],
                device_id=(p, tm),
                device_id_type=MESH,
            )

        for k in range(1, m):
            ep_to(lax.rem(me + k, m)).start()
        local = pltpu.make_async_copy(
            src_ref.at[:, :, pl.ds(me * width, width)],
            out_ref.at[:, pl.ds(me * groups, groups), :],
            local_sem.at[0],
        )
        local.start()

        histogram(leaf_ref, grad_ref, hess_ref, mine)
        staged = pltpu.make_async_copy(mine, held.at[tm], local_sem.at[1])
        staged.start()
        staged.wait()

        def tm_to(p):
            return pltpu.make_async_remote_copy(
                src_ref=held.at[tm],
                dst_ref=held.at[tm],
                send_sem=tm_send.at[p],
                recv_sem=tm_recv.at[tm],
                device_id=(me, p),
                device_id_type=MESH,
            )

        def tm_from(p):
            return pltpu.make_async_remote_copy(
                src_ref=held.at[tm],
                dst_ref=held.at[p],
                send_sem=tm_send.at[p],
                recv_sem=tm_recv.at[p],
                device_id=(me, p),
                device_id_type=MESH,
            )

        def send(k, carry):
            tm_to(lax.rem(tm + k, n)).start()
            return carry

        lax.fori_loop(1, n, send, 0)

        def wait(k, carry):
            p = lax.rem(tm + k, n)
            tm_to(p).wait_send()
            tm_from(p).wait_recv()
            return carry

        lax.fori_loop(1, n, wait, 0)

        def add(k, total):
            return total + held[lax.rem(tm + k, n)]

        totals = lax.fori_loop(1, n, add, held[tm])
        lane = lax.broadcasted_iota(jnp.int32, (groups, 2 * leaves), 1)
        hsum = pltpu.roll(totals, leaves, 1)
        table = jnp.where(lane < leaves, -totals / (hsum + 1.0), 0.0)
        weights_ref[...] = table[:, :leaves]

        mine[...] = table

        def one_tile(t, carry):
            rows = pl.ds(pl.multiple_of(t * 8, 8), 8)
            row = mine[rows, :]

            wide = math.gcd(length, 2048)

            def one(step, carry):
                cols = pl.ds(pl.multiple_of(step * wide, wide), wide)
                leaf = leaf_ref[rows, cols]
                picked = jnp.concatenate(
                    [
                        jnp.take_along_axis(
                            row, leaf[:, k * 128:(k + 1) * 128], axis=1, mode="promise_in_bounds"
                        )
                        for k in range(wide // 128)
                    ],
                    axis=1,
                )
                new_ref[rows, cols] = pred_ref[rows, cols] + picked
                return carry

            lax.fori_loop(0, length // wide, one, 0)
            return carry

        lax.fori_loop(0, tiles, one_tile, 0)

        local.wait()
        for k in range(1, m):
            p = lax.rem(me + k, m)
            ep_to(p).wait_send()
            ep_from(p).wait_recv()

    vmem = pl.BlockSpec(memory_space=pltpu.VMEM)
    grad_hess, leaf_weights, new_pred = pl.pallas_call(
        kernel,
        out_shape=(
            jax.ShapeDtypeStruct((two, groups * m, width), stacked.dtype),
            jax.ShapeDtypeStruct((groups, leaves), jnp.float32),
            jax.ShapeDtypeStruct((groups, length), jnp.float32),
        ),
        in_specs=[pl.BlockSpec(memory_space=pl.ANY), vmem, vmem, vmem, vmem],
        out_specs=(pl.BlockSpec(memory_space=pl.ANY), vmem, vmem),
        scratch_shapes=[
            pltpu.VMEM((groups, 2 * leaves), jnp.float32),
            pltpu.VMEM((n, groups, 2 * leaves), jnp.float32),
            pltpu.SemaphoreType.DMA((m,)),
            pltpu.SemaphoreType.DMA((m,)),
            pltpu.SemaphoreType.DMA((n,)),
            pltpu.SemaphoreType.DMA((n,)),
            pltpu.SemaphoreType.DMA((2,)),
        ],
        compiler_params=pltpu.CompilerParams(
            collective_id=cid, has_side_effects=True, vmem_limit_bytes=60 * 1024 * 1024
        ),
    )(stacked, leaf_index, gradient, hessian, predictions)
    return grad_hess, leaf_weights, new_pred


def tm_exchange(payload, held, send_sem, recv_sem, stage_sem, ep, me, n):
    staged = pltpu.make_async_copy(payload, held.at[me], stage_sem)
    staged.start()
    staged.wait()

    def copy_to(p):
        return pltpu.make_async_remote_copy(
            src_ref=held.at[me],
            dst_ref=held.at[me],
            send_sem=send_sem.at[p],
            recv_sem=recv_sem.at[me],
            device_id=(ep, p),
            device_id_type=MESH,
        )

    def copy_from(p):
        return pltpu.make_async_remote_copy(
            src_ref=held.at[me],
            dst_ref=held.at[p],
            send_sem=send_sem.at[p],
            recv_sem=recv_sem.at[p],
            device_id=(ep, p),
            device_id_type=MESH,
        )

    def send(k, carry):
        copy_to(lax.rem(me + k, n)).start()
        return carry

    lax.fori_loop(1, n, send, 0)

    def wait(k, carry):
        p = lax.rem(me + k, n)
        copy_to(p).wait_send()
        copy_from(p).wait_recv()
        return carry

    lax.fori_loop(1, n, wait, 0)


def scan_lanes(x, from_end):
    lane = lax.broadcasted_iota(jnp.int32, x.shape, 1)
    k = 1
    while k < 128:
        if from_end:
            moved = pltpu.roll(x, 128 - k, 1)
            x = x + jnp.where(lane < 128 - k, moved, 0.0)
        else:
            moved = pltpu.roll(x, k, 1)
            x = x + jnp.where(lane >= k, moved, 0.0)
        k *= 2
    return x


def front(predictions, events, first_rows, last_rows):
    n = lax.axis_size("tm")
    groups, length = predictions.shape
    tiles = groups // 8
    blocks = length // 128
    span = math.gcd(blocks, 32)
    groups_n = blocks // span

    def kernel(pred_ref, ev_ref, first_ref, last_ref,
               grad_ref, hess_ref, both_ref,
               weight, one, two, pay_a, held_a, pay_b, held_b,
               send_a, recv_a, send_b, recv_b, stage):
        me = lax.axis_index("tm")
        ep = lax.axis_index("ep")
        barrier = pltpu.get_barrier_semaphore()

        def greet(k, carry):
            p = lax.rem(me + k, n)
            pl.semaphore_signal(barrier, inc=1, device_id=(ep, p), device_id_type=MESH)
            return carry

        lax.fori_loop(1, n, greet, 0)
        pl.semaphore_wait(barrier, n - 1)

        lane_j = lax.broadcasted_iota(jnp.int32, (128, 128), 0)
        lane_i = lax.broadcasted_iota(jnp.int32, (128, 128), 1)
        upper = (lane_j >= lane_i).astype(jnp.bfloat16)
        lower = (lane_j <= lane_i).astype(jnp.bfloat16)

        def run_sum(x, matrix):
            hi = x.astype(jnp.bfloat16)
            lo = (x - hi.astype(jnp.float32)).astype(jnp.bfloat16)
            out = jnp.dot(hi, matrix, preferred_element_type=jnp.float32)
            return out + jnp.dot(lo, matrix, preferred_element_type=jnp.float32)

        def block_cols(b):
            return pl.ds(pl.multiple_of(b * 128, 128), 128)

        def suffix_tile(t, carry):
            rows = pl.ds(pl.multiple_of(t * 8, 8), 8)

            def one_group(j, later):
                b0 = (groups_n - 1 - j) * span
                pieces = []
                for k in range(span):
                    w = jnp.exp(pred_ref[rows, block_cols(b0 + k)])
                    weight[rows, block_cols(b0 + k)] = w
                    pieces.append(w)
                s = run_sum(jnp.concatenate(pieces, axis=0), upper)
                idx = first_ref[pl.ds(pl.multiple_of(b0 * 8, 8), 8 * span), :]
                r = jnp.take_along_axis(s, idx, axis=1, mode="promise_in_bounds")
                for k in reversed(range(span)):
                    one[rows, block_cols(b0 + k)] = r[8 * k:8 * k + 8] + later
                    later = later + jnp.broadcast_to(s[8 * k:8 * k + 8, 0:1], (8, 128))
                return later

            total = lax.fori_loop(0, groups_n, one_group, jnp.zeros((8, 128), jnp.float32), unroll=2)
            pay_a[rows, :] = total
            return carry

        lax.fori_loop(0, tiles, suffix_tile, 0)
        tm_exchange(pay_a, held_a, send_a, recv_a, stage.at[0], ep, me, n)

        def add_later(k, total):
            p = lax.rem(me + k, n)
            return total + jnp.where(p > me, held_a[p], 0.0)

        pay_a[...] = lax.fori_loop(1, n, add_later, jnp.zeros((groups, 128), jnp.float32))

        def prefix_tile(t, carry):
            rows = pl.ds(pl.multiple_of(t * 8, 8), 8)
            later = pay_a[rows, :]

            def one_group(j, carries):
                c1, c2 = carries
                b0 = j * span
                firsts, seconds = [], []
                for k in range(span):
                    risk = one[rows, block_cols(b0 + k)] + later
                    observed = ev_ref[rows, block_cols(b0 + k)].astype(jnp.float32)
                    scale = 1.0 / risk
                    inv_one = observed * scale
                    firsts.append(inv_one)
                    seconds.append(inv_one * scale)
                s = run_sum(jnp.concatenate(firsts + seconds, axis=0), lower)
                idx = last_ref[pl.ds(pl.multiple_of(b0 * 8, 8), 8 * span), :]
                idx = jnp.concatenate([idx, idx], axis=0)
                r = jnp.take_along_axis(s, idx, axis=1, mode="promise_in_bounds")
                half = 8 * span
                for k in range(span):
                    one[rows, block_cols(b0 + k)] = r[8 * k:8 * k + 8] + c1
                    two[rows, block_cols(b0 + k)] = r[half + 8 * k:half + 8 * k + 8] + c2
                    c1 = c1 + jnp.broadcast_to(s[8 * k:8 * k + 8, 127:128], (8, 128))
                    c2 = c2 + jnp.broadcast_to(s[half + 8 * k:half + 8 * k + 8, 127:128], (8, 128))
                return (c1, c2)

            zero = jnp.zeros((8, 128), jnp.float32)
            c1, c2 = lax.fori_loop(0, groups_n, one_group, (zero, zero), unroll=2)
            pay_b[rows, :] = c1
            pay_b[pl.ds(pl.multiple_of(groups + t * 8, 8), 8), :] = c2
            return carry

        lax.fori_loop(0, tiles, prefix_tile, 0)
        tm_exchange(pay_b, held_b, send_b, recv_b, stage.at[1], ep, me, n)

        def add_earlier(k, total):
            p = lax.rem(me + k, n)
            return total + jnp.where(p < me, held_b[p], 0.0)

        pay_b[...] = lax.fori_loop(1, n, add_earlier, jnp.zeros((2 * groups, 128), jnp.float32))

        def out_tile(t, carry):
            rows = pl.ds(pl.multiple_of(t * 8, 8), 8)
            e1 = jnp.tile(pay_b[rows, :], (1, span))
            e2 = jnp.tile(pay_b[pl.ds(pl.multiple_of(groups + t * 8, 8), 8), :], (1, span))

            def one_group(j, carry):
                cols = pl.ds(pl.multiple_of(j * span * 128, span * 128), span * 128)
                w = weight[rows, cols]
                a1 = one[rows, cols] + e1
                a2 = two[rows, cols] + e2
                observed = ev_ref[rows, cols].astype(jnp.float32)
                g = w * a1 - observed
                h = w * a1 - w * w * a2
                grad_ref[rows, cols] = g
                hess_ref[rows, cols] = h
                both_ref[0, rows, cols] = g.astype(jnp.bfloat16)
                both_ref[1, rows, cols] = h.astype(jnp.bfloat16)
                return carry

            lax.fori_loop(0, groups_n, one_group, 0)
            return carry

        lax.fori_loop(0, tiles, out_tile, 0)

    vmem = pl.BlockSpec(memory_space=pltpu.VMEM)
    return pl.pallas_call(
        kernel,
        out_shape=(
            jax.ShapeDtypeStruct((groups, length), jnp.float32),
            jax.ShapeDtypeStruct((groups, length), jnp.float32),
            jax.ShapeDtypeStruct((2, groups, length), jnp.bfloat16),
        ),
        in_specs=[vmem, vmem, vmem, vmem],
        out_specs=(vmem, vmem, vmem),
        scratch_shapes=[
            pltpu.VMEM((groups, length), jnp.float32),
            pltpu.VMEM((groups, length), jnp.float32),
            pltpu.VMEM((groups, length), jnp.float32),
            pltpu.VMEM((groups, 128), jnp.float32),
            pltpu.VMEM((n, groups, 128), jnp.float32),
            pltpu.VMEM((2 * groups, 128), jnp.float32),
            pltpu.VMEM((n, 2 * groups, 128), jnp.float32),
            pltpu.SemaphoreType.DMA((n,)),
            pltpu.SemaphoreType.DMA((n,)),
            pltpu.SemaphoreType.DMA((n,)),
            pltpu.SemaphoreType.DMA((n,)),
            pltpu.SemaphoreType.DMA((2,)),
        ],
        compiler_params=pltpu.CompilerParams(
            collective_id=0, has_side_effects=True, vmem_limit_bytes=60 * 1024 * 1024
        ),
    )(predictions, events, first_rows, last_rows)


def tie_rows(tie_start):
    length = tie_start.shape[0]
    blocks = length // 128
    starts = tie_start.reshape(blocks, 128)
    labels = jnp.arange(128, dtype=jnp.int32)
    first_local = lax.cummax(jnp.where(starts == 1, labels[None, :], 0), axis=1)
    next_start = jnp.concatenate([starts[:, 1:], jnp.ones((blocks, 1), jnp.int32)], axis=1)
    last_local = lax.cummin(jnp.where(next_start == 1, labels[None, :], 127), axis=1, reverse=True)

    def spread(rows):
        return jnp.broadcast_to(rows[:, None, :], (blocks, 8, 128)).reshape(blocks * 8, 128)

    return spread(first_local), spread(last_local)


def lane_pad(vectors):
    width = vectors.shape[1]
    return jnp.pad(vectors, ((0, 0), (0, 128 - width)))


def tile_matrices(tie_start):
    length = tie_start.shape[0]
    blocks = length // 128
    starts = tie_start.reshape(blocks, 128)
    labels = jnp.arange(128, dtype=jnp.int32)
    first_local = lax.cummax(jnp.where(starts == 1, labels[None, :], 0), axis=1)
    next_start = jnp.concatenate([starts[:, 1:], jnp.ones((blocks, 1), jnp.int32)], axis=1)
    last_local = lax.cummin(jnp.where(next_start == 1, labels[None, :], 127), axis=1, reverse=True)
    backward = (labels[None, :, None] >= first_local[:, None, :]).astype(jnp.float32)
    forward = (labels[None, :, None] <= last_local[:, None, :]).astype(jnp.float32)
    return (backward, forward)


def block_cumsum(values, matrices, from_end):
    groups = values.shape[0]
    length = values.shape[1]
    blocks = length // 128
    shaped = values.reshape(groups, blocks, 128)
    within = jnp.einsum("ebj,bji->ebi", shaped, matrices, precision=lax.Precision.HIGH)
    totals = jnp.sum(shaped, axis=2)
    if from_end:
        offsets = jnp.cumsum(totals[:, ::-1], axis=1)[:, ::-1] - totals
    else:
        offsets = jnp.cumsum(totals, axis=1) - totals
    return (within + offsets[:, :, None]).reshape(groups, length)


def leaf_update(predictions, leaf_index, table):
    groups, length = leaf_index.shape
    tiles = groups // 8
    table = lane_pad(table)

    def kernel(table_ref, pred_ref, leaf_ref, out_ref):
        row = table_ref[...]

        def one(step, carry):
            cols = pl.ds(pl.multiple_of(step * 128, 128), 128)
            picked = jnp.take_along_axis(row, leaf_ref[:, cols], axis=1, mode="promise_in_bounds")
            out_ref[:, cols] = pred_ref[:, cols] + picked
            return carry

        lax.fori_loop(0, length // 128, one, 0, unroll=8)

    spec = pl.BlockSpec((8, length), lambda t: (t, 0))
    return pl.pallas_call(
        kernel,
        grid=(tiles,),
        out_shape=jax.ShapeDtypeStruct((groups, length), jnp.float32),
        in_specs=[pl.BlockSpec((8, 128), lambda t: (t, 0)), spec, spec],
        out_specs=spec,
    )(table, predictions, leaf_index)


def on_device(predictions, leaf_index, events, tie_start):
    first_rows, last_rows = tie_rows(tie_start)
    gradient, hessian, stacked = front(predictions, events, first_rows, last_rows)
    grad_hess, leaf_weights, new_pred = finish(
        stacked, leaf_index, gradient, hessian, predictions, LEAVES, 2
    )
    grad_hess = grad_hess.reshape(2, grad_hess.shape[1], 1, grad_hess.shape[2])
    return (new_pred, leaf_weights, grad_hess)


def solution(mesh):
    placed = (P("ep", "tm"), P("ep", "tm"), P("ep", "tm"), P("tm"))
    return jax.shard_map(
        on_device,
        mesh=mesh,
        in_specs=placed,
        out_specs=(P("ep", "tm"), P("ep", None), P(None, None, "tm", "ep")),
        check_vma=False,
    )
```
